128 devices in a mesh: fsdp: 16 (over x, y), dp: 8 (over z, core).
Axes of the slice: x: 4, y: 4, z: 4, core: 2. Of those that a mesh axis runs over, the one named last changes fastest.
Arguments:
- tokens: bfloat16 [32768, 960], P(('fsdp', 'dp')), may hold values from -6 to 6
- layer_weights: bfloat16 [1, 960, 10240], P(None, None, ('fsdp', 'dp'))
- norm_gains: bfloat16 [1, 1920], P(None, ('fsdp', 'dp')), may hold values from 0.5 to 1.5
- seq_ids: int32 [32768], P(('fsdp', 'dp')), may hold values from 0 to 255, as said below
- out_grad: bfloat16 [32768, 960], P(('fsdp', 'dp')), may hold values from -6 to 6
Outputs:
- activations: bfloat16 [32768, 960], P(('fsdp', 'dp'))
- input_grad: float32 [32768, 960], P(('fsdp', 'dp'))
- weight_grad: float32 [1, 960, 10240], P(None, None, ('fsdp', 'dp'))
- gain_grad: float32 [1, 1920], P(None, ('fsdp', 'dp'))
The draws below stay inside these ranges and needn't reach their ends.
Inputs may be any that keep to these rules, and one draw needn't show every extreme that they name: `seq_ids`: within each device's 256 rows: 0 in the first row, never falling, rising by at most one from a row to the next, so every sequence lies whole on one device; on some device all rows form one sequence, on another every row is a sequence of its own.
All inputs are finite; a program needn't handle non-finite values.
Results may differ from the reference program's by a relative error of at most 0.013.
Values may be sent and summed in bfloat16 or wider, within the bound.
A program may use at most 256 MiB of HBM per device.

```python
import math
import jax
import jax.numpy as jnp
from jax import lax

D = 960
QUERY_HEADS = 15
KEY_VALUE_HEADS = 5
HEAD_SIZE = 64
FF = 2560
LAYERS = 1
TOK_DEV = 256
WCOLS = 10240
TOKENS = 32768


def draw_layer_weights(key, part):
    columns = jnp.arange(WCOLS)
    query_width = QUERY_HEADS * HEAD_SIZE
    key_value_width = KEY_VALUE_HEADS * HEAD_SIZE
    perceptron_begin = 2 * query_width + 2 * key_value_width
    spread = jnp.where(columns < query_width + 2 * key_value_width, 1.0 / math.sqrt(D), jnp.where(columns < perceptron_begin, 2.5 / math.sqrt(query_width), jnp.where(columns < perceptron_begin + 2 * FF, 1.0 / math.sqrt(D), 1.5 / math.sqrt(FF))))
    values = jax.random.normal(key, (LAYERS, D, WCOLS), jnp.float32)
    return (values * spread[None, None, :]).astype(jnp.bfloat16)


def draw_seq_ids(key, part):
    block_count = TOKENS // TOK_DEV
    first_key, second_key, third_key, fourth_key = jax.random.split(key, 4)
    rates = jax.random.randint(third_key, (block_count, 1), 6, 96)
    draws_int = jax.random.randint(first_key, (block_count, TOK_DEV), 0, rates)
    breaks = (draws_int == 0).astype(jnp.int32)
    single = jax.random.randint(second_key, (), 0, block_count)
    offset = jax.random.randint(fourth_key, (), 1, block_count)
    dense = (single + offset) % block_count
    block_index = jnp.arange(block_count)[:, None]
    column_index = jnp.arange(TOK_DEV)[None, :]
    breaks = jnp.where(block_index == dense, 1, breaks)
    breaks = jnp.where((block_index == single) | (column_index == 0), 0, breaks)
    return jnp.cumsum(breaks, axis=1).reshape(-1).astype(jnp.int32)


def shard_levels(own_key, shape, pieces, least, top_value):
    def one(dim, parts):
        heights = jax.random.uniform(jax.random.fold_in(jax.random.fold_in(own_key, 6), dim), (parts,), jnp.float32, least / len(pieces), top_value / len(pieces))
        return jnp.repeat(jnp.exp(heights), shape[dim] // parts).reshape((-1,) + (1,) * (len(shape) - dim - 1))

    factor_of = one(*pieces[0])
    for cut in pieces[1:]:
        factor_of = factor_of * one(*cut)
    return factor_of


def gaussian(rng, dims, scale, bound, shards=(), kind=jnp.bfloat16):
    array = jax.random.normal(rng, dims, jnp.float32) * scale
    if len(shards) > 0:
        array = shard_levels(rng, dims, shards, -0.22, 0.18) * array
    return jnp.clip(array, min=-bound, max=bound).astype(kind)


def setup_inputs(seed: int = 0) -> dict:
    key_of = jax.random.split(jax.random.key(seed), 6)
    return {
        "tokens": gaussian(key_of[0], (TOKENS, D), 1.0, 6.0, ((0, 128),)),
        "layer_weights": draw_layer_weights(jax.random.fold_in(key_of[5], 71), 0),
        "norm_gains": jnp.clip(1.0 + 0.1 * jax.random.normal(key_of[2], (LAYERS, 2 * D), jnp.float32), 0.5, 1.5).astype(jnp.bfloat16),
        "seq_ids": draw_seq_ids(jax.random.fold_in(key_of[5], 71), 0),
        "out_grad": gaussian(key_of[4], (TOKENS, D), 1.0, 6.0, ((0, 128),)),
    }


epsilon = 1e-05
rope_base = 100000.0

def mix_heads(pattern, left, right):
    return jnp.einsum(pattern, left.astype(jnp.float32), right.astype(jnp.float32))

def across(left, right):
    return lax.dot_general(left, right, (((0,), (0,)), ((), ())), preferred_element_type=jnp.float32)

def against(left, right):
    return lax.dot_general(left, right, (((1,), (1,)), ((), ())), preferred_element_type=jnp.float32)

def tables(block_ids, head_width):
    sequence_length = block_ids.shape[0]
    row_index = jnp.arange(sequence_length, dtype=jnp.int32)
    same_seq = block_ids[:, None] == block_ids[None, :]
    seq_start = lax.optimization_barrier(jnp.min(jnp.where(same_seq, row_index[None, :], sequence_length), axis=1))
    position = (row_index - seq_start).astype(jnp.float32)
    inv_freq = rope_base ** (-jnp.arange(0, head_width, 2).astype(jnp.float32) / head_width)
    angles = position[:, None] * inv_freq[None, :]
    allowed = same_seq & (row_index[None, :] <= row_index[:, None])
    return (jnp.cos(angles)[:, None, :], jnp.sin(angles)[:, None, :], allowed)

def apply_rotary(values, cosine_table, sine_table, direction):
    half_dim = values.shape[-1] // 2
    a = values[..., :half_dim]
    b = values[..., half_dim:]
    return jnp.concatenate([a * cosine_table - direction * b * sine_table, b * cosine_table + direction * a * sine_table], axis=-1)

def norm_forward(values, gain):
    inv_rms = lax.rsqrt(lax.optimization_barrier(jnp.mean(values * values, axis=-1, keepdims=True)) + epsilon)
    return (inv_rms, (values * inv_rms * gain).astype(jnp.bfloat16))

def norm_backward(d_norm, values, inv_rms, gain):
    u = d_norm * gain
    d_gain = lax.optimization_barrier(jnp.sum(d_norm * values * inv_rms, axis=0))
    d_values = inv_rms * u - values * inv_rms ** 3 * lax.optimization_barrier(jnp.mean(u * values, axis=-1, keepdims=True))
    return (d_values, d_gain)

def widths(weight_tree, cosine_table):
    head_width = cosine_table.shape[-1] * 2
    query_width = QUERY_HEADS * head_width
    key_value_width = KEY_VALUE_HEADS * head_width
    perceptron_begin = 2 * query_width + 2 * key_value_width
    hidden_width = (weight_tree.shape[1] - perceptron_begin) // 3
    return (head_width, query_width, key_value_width, perceptron_begin, hidden_width)

def scores(query_rows, key_rows, allowed, head_width):
    score_vals = mix_heads('tkgd,skd->kgts', query_rows, key_rows) * head_width ** (-0.5)
    return jnp.where(allowed, score_vals, -1e+30)

def layer_forward(stream, weight_tree, gain_row, cosine_table, sine_table, allowed):
    head_width, query_width, key_value_width, perceptron_begin, hidden_width = widths(weight_tree, cosine_table)
    width = stream.shape[1]
    sequence_length = stream.shape[0]
    head_group = QUERY_HEADS // KEY_VALUE_HEADS
    gain_a = gain_row[:width].astype(jnp.float32)
    gain_b = gain_row[width:].astype(jnp.float32)
    rms_a, normed_a = norm_forward(stream, gain_a)
    query_key_value = jnp.dot(normed_a, weight_tree[:, :query_width + 2 * key_value_width], preferred_element_type=jnp.float32)
    query_rows = apply_rotary(query_key_value[:, :query_width].reshape(sequence_length, QUERY_HEADS, head_width), cosine_table, sine_table, 1.0).astype(jnp.bfloat16).reshape(sequence_length, KEY_VALUE_HEADS, head_group, head_width)
    key_rows = apply_rotary(query_key_value[:, query_width:query_width + key_value_width].reshape(sequence_length, KEY_VALUE_HEADS, head_width), cosine_table, sine_table, 1.0).astype(jnp.bfloat16)
    value_rows = query_key_value[:, query_width + key_value_width:query_width + 2 * key_value_width].reshape(sequence_length, KEY_VALUE_HEADS, head_width).astype(jnp.bfloat16)
    score_vals = scores(query_rows, key_rows, allowed, head_width)
    row_max = lax.optimization_barrier(jnp.max(score_vals, axis=-1, keepdims=True))
    expon = jnp.exp(score_vals - row_max)
    row_sum = lax.optimization_barrier(jnp.sum(expon, axis=-1, keepdims=True))
    log_total = row_max + jnp.log(row_sum)
    attended = mix_heads('kgts,skd->tkgd', (expon / row_sum).astype(jnp.bfloat16), value_rows).reshape(sequence_length, query_width).astype(jnp.bfloat16)
    middle = stream + against(attended, weight_tree[:, query_width + 2 * key_value_width:perceptron_begin])
    rms_b, normed_b = norm_forward(middle, gain_b)
    gate_up = jnp.dot(normed_b, weight_tree[:, perceptron_begin:perceptron_begin + 2 * hidden_width], preferred_element_type=jnp.float32)
    gate_val = gate_up[:, :hidden_width]
    upward = gate_up[:, hidden_width:]
    hidden = (jax.nn.silu(gate_val) * upward).astype(jnp.bfloat16)
    result = middle + against(hidden, weight_tree[:, perceptron_begin + 2 * hidden_width:])
    return (result, (stream, rms_a, normed_a, query_rows, key_rows, value_rows, log_total, attended, middle, rms_b, normed_b, gate_val, upward, hidden))

def layer_backward(upstream, saved_acts, weight_tree, gain_row, cosine_table, sine_table, allowed):
    stream, rms_a, normed_a, query_rows, key_rows, value_rows, log_total, attended, middle, rms_b, normed_b, gate_val, upward, hidden = saved_acts
    head_width, query_width, key_value_width, perceptron_begin, hidden_width = widths(weight_tree, cosine_table)
    width = stream.shape[1]
    sequence_length = stream.shape[0]
    head_group = QUERY_HEADS // KEY_VALUE_HEADS
    gain_a = gain_row[:width].astype(jnp.float32)
    gain_b = gain_row[width:].astype(jnp.float32)
    out_rounded = upstream.astype(jnp.bfloat16)
    d_hidden = jnp.dot(out_rounded, weight_tree[:, perceptron_begin + 2 * hidden_width:], preferred_element_type=jnp.float32)
    d_down = across(out_rounded, hidden)
    sig_gate = jax.nn.sigmoid(gate_val)
    d_gate = d_hidden * upward * sig_gate * (1.0 + gate_val * (1.0 - sig_gate))
    d_upward = d_hidden * gate_val * sig_gate
    d_gate_up = jnp.concatenate([d_gate, d_upward], axis=1).astype(jnp.bfloat16)
    d_normed_b = against(d_gate_up, weight_tree[:, perceptron_begin:perceptron_begin + 2 * hidden_width])
    d_gate_up_w = across(normed_b, d_gate_up)
    d_mid_norm, d_gain_b = norm_backward(d_normed_b, middle, rms_b, gain_b)
    d_middle = upstream + d_mid_norm
    middle_cast = d_middle.astype(jnp.bfloat16)
    attended_gradient = jnp.dot(middle_cast, weight_tree[:, query_width + 2 * key_value_width:perceptron_begin], preferred_element_type=jnp.float32).astype(jnp.bfloat16).reshape(sequence_length, KEY_VALUE_HEADS, head_group, head_width)
    d_out_w = across(middle_cast, attended)
    expon = jnp.exp(scores(query_rows, key_rows, allowed, head_width) - log_total)
    d_v = mix_heads('kgts,tkgd->skd', expon.astype(jnp.bfloat16), attended_gradient)
    d_p = mix_heads('tkgd,skd->kgts', attended_gradient, value_rows)
    d_s = expon * (d_p - lax.optimization_barrier(jnp.sum(expon * d_p, axis=-1, keepdims=True)))
    d_s_rounded = (d_s * head_width ** (-0.5)).astype(jnp.bfloat16)
    d_q = mix_heads('kgts,skd->tkgd', d_s_rounded, key_rows).reshape(sequence_length, QUERY_HEADS, head_width)
    d_k = mix_heads('kgts,tkgd->skd', d_s_rounded, query_rows)
    d_q = apply_rotary(d_q, cosine_table, sine_table, -1.0).reshape(sequence_length, query_width)
    d_k = apply_rotary(d_k, cosine_table, sine_table, -1.0).reshape(sequence_length, key_value_width)
    d_qkv = jnp.concatenate([d_q, d_k, d_v.reshape(sequence_length, key_value_width)], axis=1).astype(jnp.bfloat16)
    d_normed_a = against(d_qkv, weight_tree[:, :query_width + 2 * key_value_width])
    d_qkv_w = across(normed_a, d_qkv)
    d_in_norm, d_gain_a = norm_backward(d_normed_a, stream, rms_a, gain_a)
    d_stream = d_middle + d_in_norm
    weight_part = jnp.concatenate([d_qkv_w, d_out_w, d_gate_up_w, d_down], axis=1)
    return (d_stream, weight_part, jnp.concatenate([d_gain_a, d_gain_b]))

def reference(tokens, layer_weights, norm_gains, seq_ids, out_grad):
    block_count = tokens.shape[0] // TOK_DEV
    width = tokens.shape[1]
    layer_count = layer_weights.shape[0]
    block_tokens = tokens.reshape(block_count, TOK_DEV, width)
    block_ids = seq_ids.reshape(block_count, TOK_DEV)
    block_grad = out_grad.reshape(block_count, TOK_DEV, width)

    def one_block(totals, inputs):
        rows_in, ids_in, grad_in = inputs
        cosine_table, sine_table, allowed = tables(ids_in, HEAD_SIZE)
        stream = rows_in.astype(jnp.float32)
        saved_list = []
        for layer in range(layer_count):
            stream, saved_acts = layer_forward(stream, layer_weights[layer], norm_gains[layer], cosine_table, sine_table, allowed)
            saved_list.append(saved_acts)
        upstream = grad_in.astype(jnp.float32)
        weight_parts = [None] * layer_count
        gain_parts = [None] * layer_count
        for layer in reversed(range(layer_count)):
            upstream, weight_parts[layer], gain_parts[layer] = layer_backward(upstream, saved_list[layer], layer_weights[layer], norm_gains[layer], cosine_table, sine_table, allowed)
        new_totals = (totals[0] + jnp.stack(weight_parts), totals[1] + jnp.stack(gain_parts))
        return (new_totals, (stream.astype(jnp.bfloat16), upstream))
    start_totals = (jnp.zeros(layer_weights.shape, jnp.float32), jnp.zeros(norm_gains.shape, jnp.float32))
    totals, outputs = lax.scan(one_block, start_totals, (block_tokens, block_ids, block_grad))
    return (outputs[0].reshape(tokens.shape[0], width), outputs[1].reshape(tokens.shape[0], width), totals[0], totals[1])
```

```python
import functools
import jax
import jax.numpy as jnp
from jax import lax
from jax.experimental import pallas as pl
from jax.experimental.pallas import tpu as pltpu
from jax.sharding import PartitionSpec as P

QUERY_HEADS = 15
KEY_VALUE_HEADS = 5
HEAD_SIZE = 64


epsilon = 1e-05
rope_base = 100000.0


def mix_heads(pattern, left, right):
    return jnp.einsum(pattern, left, right, preferred_element_type=jnp.float32)


def across(left, right):
    return lax.dot_general(
        left, right, (((0,), (0,)), ((), ())), preferred_element_type=jnp.float32
    )


def against(left, right):
    return lax.dot_general(
        left, right, (((1,), (1,)), ((), ())), preferred_element_type=jnp.float32
    )


def tables(block_ids, head_width):
    sequence_length = block_ids.shape[0]
    row_index = jnp.arange(sequence_length, dtype=jnp.int32)
    same_seq = block_ids[:, None] == block_ids[None, :]
    seq_start = jnp.min(jnp.where(same_seq, row_index[None, :], sequence_length), axis=1)
    position = (row_index - seq_start).astype(jnp.float32)
    inv_freq = rope_base ** (-jnp.arange(0, head_width, 2).astype(jnp.float32) / head_width)
    angles = position[:, None] * inv_freq[None, :]
    allowed = same_seq & (row_index[None, :] <= row_index[:, None])
    return (jnp.cos(angles)[:, None, :], jnp.sin(angles)[:, None, :], allowed)


def apply_rotary(values, cosine_table, sine_table, direction):
    half_dim = values.shape[-1] // 2
    a = values[..., :half_dim]
    b = values[..., half_dim:]
    return jnp.concatenate(
        [
            a * cosine_table - direction * b * sine_table,
            b * cosine_table + direction * a * sine_table,
        ],
        axis=-1,
    )


def norm_forward(values, gain):
    inv_rms = lax.rsqrt(jnp.mean(values * values, axis=-1, keepdims=True) + epsilon)
    return (inv_rms, (values * inv_rms * gain).astype(jnp.bfloat16))


def norm_backward(d_norm, values, inv_rms, gain):
    u = d_norm * gain
    d_gain = jnp.sum(d_norm * values * inv_rms, axis=0)
    d_values = inv_rms * u - values * inv_rms**3 * jnp.mean(u * values, axis=-1, keepdims=True)
    return (d_values, d_gain)


def widths(weight_tree, cosine_table):
    head_width = cosine_table.shape[-1] * 2
    query_width = QUERY_HEADS * head_width
    key_value_width = KEY_VALUE_HEADS * head_width
    perceptron_begin = 2 * query_width + 2 * key_value_width
    hidden_width = (weight_tree.shape[1] - perceptron_begin) // 3
    return (head_width, query_width, key_value_width, perceptron_begin, hidden_width)


def scores(query_rows, key_rows, allowed, head_width):
    score_vals = mix_heads("tkgd,skd->kgts", query_rows, key_rows) * head_width ** (-0.5)
    return jnp.where(allowed, score_vals, -1e30)


def layer_forward(stream, weight_tree, gain_row, cosine_table, sine_table, allowed):
    head_width, query_width, key_value_width, perceptron_begin, hidden_width = widths(
        weight_tree, cosine_table
    )
    width = stream.shape[1]
    sequence_length = stream.shape[0]
    head_group = QUERY_HEADS // KEY_VALUE_HEADS
    gain_a = gain_row[:width].astype(jnp.float32)
    gain_b = gain_row[width:].astype(jnp.float32)
    rms_a, normed_a = norm_forward(stream, gain_a)
    query_key_value = jnp.dot(
        normed_a,
        weight_tree[:, : query_width + 2 * key_value_width],
        preferred_element_type=jnp.float32,
    )
    query_rows = (
        apply_rotary(
            query_key_value[:, :query_width].reshape(sequence_length, QUERY_HEADS, head_width),
            cosine_table,
            sine_table,
            1.0,
        )
        .astype(jnp.bfloat16)
        .reshape(sequence_length, KEY_VALUE_HEADS, head_group, head_width)
    )
    key_rows = apply_rotary(
        query_key_value[:, query_width : query_width + key_value_width].reshape(
            sequence_length, KEY_VALUE_HEADS, head_width
        ),
        cosine_table,
        sine_table,
        1.0,
    ).astype(jnp.bfloat16)
    value_rows = (
        query_key_value[:, query_width + key_value_width : query_width + 2 * key_value_width]
        .reshape(sequence_length, KEY_VALUE_HEADS, head_width)
        .astype(jnp.bfloat16)
    )
    score_vals = scores(query_rows, key_rows, allowed, head_width)
    row_max = jnp.max(score_vals, axis=-1, keepdims=True)
    expon = jnp.exp(score_vals - row_max)
    row_sum = jnp.sum(expon, axis=-1, keepdims=True)
    log_total = row_max + jnp.log(row_sum)
    attended = (
        mix_heads("kgts,skd->tkgd", (expon / row_sum).astype(jnp.bfloat16), value_rows)
        .reshape(sequence_length, query_width)
        .astype(jnp.bfloat16)
    )
    middle = stream + against(
        attended, weight_tree[:, query_width + 2 * key_value_width : perceptron_begin]
    )
    rms_b, normed_b = norm_forward(middle, gain_b)
    gate_up = jnp.dot(
        normed_b,
        weight_tree[:, perceptron_begin : perceptron_begin + 2 * hidden_width],
        preferred_element_type=jnp.float32,
    )
    gate_val = gate_up[:, :hidden_width]
    upward = gate_up[:, hidden_width:]
    hidden = (jax.nn.silu(gate_val) * upward).astype(jnp.bfloat16)
    result = middle + against(hidden, weight_tree[:, perceptron_begin + 2 * hidden_width :])
    return (
        result,
        (
            stream,
            rms_a,
            normed_a,
            query_rows,
            key_rows,
            value_rows,
            log_total,
            attended,
            middle,
            rms_b,
            normed_b,
            gate_val,
            upward,
            hidden,
        ),
    )


def layer_backward(upstream, saved_acts, weight_tree, gain_row, cosine_table, sine_table, allowed):
    (
        stream,
        rms_a,
        normed_a,
        query_rows,
        key_rows,
        value_rows,
        log_total,
        attended,
        middle,
        rms_b,
        normed_b,
        gate_val,
        upward,
        hidden,
    ) = saved_acts
    head_width, query_width, key_value_width, perceptron_begin, hidden_width = widths(
        weight_tree, cosine_table
    )
    width = stream.shape[1]
    sequence_length = stream.shape[0]
    head_group = QUERY_HEADS // KEY_VALUE_HEADS
    gain_a = gain_row[:width].astype(jnp.float32)
    gain_b = gain_row[width:].astype(jnp.float32)
    out_rounded = upstream.astype(jnp.bfloat16)
    d_hidden = jnp.dot(
        out_rounded,
        weight_tree[:, perceptron_begin + 2 * hidden_width :],
        preferred_element_type=jnp.float32,
    )
    d_down = across(out_rounded, hidden)
    sig_gate = jax.nn.sigmoid(gate_val)
    d_gate = d_hidden * upward * sig_gate * (1.0 + gate_val * (1.0 - sig_gate))
    d_upward = d_hidden * gate_val * sig_gate
    d_gate_up = jnp.concatenate([d_gate, d_upward], axis=1).astype(jnp.bfloat16)
    d_normed_b = against(
        d_gate_up, weight_tree[:, perceptron_begin : perceptron_begin + 2 * hidden_width]
    )
    d_gate_up_w = across(normed_b, d_gate_up)
    d_mid_norm, d_gain_b = norm_backward(d_normed_b, middle, rms_b, gain_b)
    d_middle = upstream + d_mid_norm
    middle_cast = d_middle.astype(jnp.bfloat16)
    attended_gradient = (
        jnp.dot(
            middle_cast,
            weight_tree[:, query_width + 2 * key_value_width : perceptron_begin],
            preferred_element_type=jnp.float32,
        )
        .astype(jnp.bfloat16)
        .reshape(sequence_length, KEY_VALUE_HEADS, head_group, head_width)
    )
    d_out_w = across(middle_cast, attended)
    expon = jnp.exp(scores(query_rows, key_rows, allowed, head_width) - log_total)
    d_v = mix_heads("kgts,tkgd->skd", expon.astype(jnp.bfloat16), attended_gradient)
    d_p = mix_heads("tkgd,skd->kgts", attended_gradient, value_rows)
    d_s = expon * (d_p - jnp.sum(expon * d_p, axis=-1, keepdims=True))
    d_s_rounded = (d_s * head_width ** (-0.5)).astype(jnp.bfloat16)
    d_q = mix_heads("kgts,skd->tkgd", d_s_rounded, key_rows).reshape(
        sequence_length, QUERY_HEADS, head_width
    )
    d_k = mix_heads("kgts,tkgd->skd", d_s_rounded, query_rows)
    d_q = apply_rotary(d_q, cosine_table, sine_table, -1.0).reshape(sequence_length, query_width)
    d_k = apply_rotary(d_k, cosine_table, sine_table, -1.0).reshape(
        sequence_length, key_value_width
    )
    d_qkv = jnp.concatenate(
        [d_q, d_k, d_v.reshape(sequence_length, key_value_width)], axis=1
    ).astype(jnp.bfloat16)
    d_normed_a = against(d_qkv, weight_tree[:, : query_width + 2 * key_value_width])
    d_qkv_w = across(normed_a, d_qkv)
    d_in_norm, d_gain_a = norm_backward(d_normed_a, stream, rms_a, gain_a)
    d_stream = d_middle + d_in_norm
    weight_part = (d_qkv_w, d_out_w, d_gate_up_w, d_down)
    return (d_stream, weight_part, jnp.concatenate([d_gain_a, d_gain_b]))


MESH = pl.DeviceIdType.MESH
BF = jnp.bfloat16
LANES = ((0, 384), (384, 384), (768, 256))
ORDERS = ((0, 1, 2), (1, 2, 0), (2, 0, 1))


def place():
    f = lax.axis_index("fsdp")
    d = lax.axis_index("dp")
    return (f // 4, f % 4, d // 2), d % 2


def device_of(xyz, core):
    return (xyz[0] * 4 + xyz[1], xyz[2] * 2 + core)


def moved(xyz, axis, step):
    out = list(xyz)
    out[axis] = (out[axis] + step + 4) % 4
    return tuple(out)


def enter(xyz, core):
    barrier = pltpu.get_barrier_semaphore()
    for axis in range(3):
        for step in (1, -1):
            pl.semaphore_signal(barrier, inc=1, device_id=device_of(moved(xyz, axis, step), core), device_id_type=MESH)
    pl.semaphore_signal(barrier, inc=1, device_id=device_of(xyz, 1 - core), device_id_type=MESH)
    pl.semaphore_wait(barrier, 7)


def gather_kernel(shard, out, own_sem, send_sem, recv_sem, sib_send, sib_recv):
    xyz, core = place()
    enter(xyz, core)
    counts = [0]
    waits = []

    def region(part, index):
        start, size = LANES[part]
        return out.at[index[0], index[1], index[2], core, :, pl.ds(start, size)]

    def remote(part, slot, src, index, to):
        copy = pltpu.make_async_remote_copy(
            src_ref=region(part, index) if src is None else src,
            dst_ref=region(part, index),
            send_sem=send_sem.at[part, slot],
            recv_sem=recv_sem.at[part, slot],
            device_id=to,
            device_id_type=MESH,
        )
        copy.start()
        waits.append(copy)
        return copy

    def sibling(part, slot, index):
        copy = pltpu.make_async_remote_copy(
            src_ref=region(part, index),
            dst_ref=region(part, index),
            send_sem=sib_send.at[part, slot],
            recv_sem=sib_recv.at[part, slot],
            device_id=device_of(xyz, 1 - core),
            device_id_type=MESH,
        )
        copy.start()
        sib.append(copy)

    sib = []
    own = []
    for part in range(3):
        start, size = LANES[part]
        c = pltpu.make_async_copy(shard.at[:, pl.ds(start, size)], region(part, xyz), own_sem.at[part])
        c.start()
        own.append(c)

    first = [None] * 3
    for part in range(3):
        a = ORDERS[part][0]
        start, size = LANES[part]
        src = shard.at[:, pl.ds(start, size)]
        plus = remote(part, 0, src, xyz, device_of(moved(xyz, a, 1), core))
        minus = remote(part, 1, src, xyz, device_of(moved(xyz, a, -1), core))
        first[part] = (plus, minus)
    second = [None] * 3
    for part in range(3):
        a = ORDERS[part][0]
        first[part][0].wait_recv()
        second[part] = remote(part, 2, None, moved(xyz, a, -1), device_of(moved(xyz, a, 1), core))
    for part in range(3):
        own[part].wait()

    def line(part, b_value, c_value, lo=None):
        a, b, c = ORDERS[part]
        index = [None] * 3
        index[a] = slice(None) if lo is None else pl.ds(lo, 2)
        index[b] = b_value
        index[c] = c_value
        return tuple(index)

    third = [[None] * 4 for _ in range(3)]
    hops = [None] * 3
    for part in range(3):
        a, b, c = ORDERS[part]
        first[part][1].wait_recv()
        second[part].wait_recv()
        mine = line(part, xyz[b], xyz[c])
        bp = remote(part, 3, None, mine, device_of(moved(xyz, b, 1), core))
        bm = remote(part, 4, None, mine, device_of(moved(xyz, b, -1), core))
        hops[part] = (bp, bm)
        cp = remote(part, 7, None, mine, device_of(moved(xyz, c, 1), core))
        cm = remote(part, 8, None, mine, device_of(moved(xyz, c, -1), core))
        third[part][0] = (cp, cm)
        sibling(part, 0, mine)
    halves = [None] * 3
    for part in range(3):
        a, b, c = ORDERS[part]
        hops[part][0].wait_recv()
        bv = moved(xyz, b, -1)[b]
        h0 = remote(part, 5, None, line(part, bv, xyz[c], 0), device_of(moved(xyz, b, 1), core))
        mine = line(part, bv, xyz[c])
        cp = remote(part, 9, None, mine, device_of(moved(xyz, c, 1), core))
        cm = remote(part, 10, None, mine, device_of(moved(xyz, c, -1), core))
        third[part][1] = (cp, cm)
        sibling(part, 1, mine)
        hops[part][1].wait_recv()
        bv = moved(xyz, b, 1)[b]
        h1 = remote(part, 6, None, line(part, bv, xyz[c], 2), device_of(moved(xyz, b, -1), core))
        mine = line(part, bv, xyz[c])
        cp = remote(part, 11, None, mine, device_of(moved(xyz, c, 1), core))
        cm = remote(part, 12, None, mine, device_of(moved(xyz, c, -1), core))
        third[part][2] = (cp, cm)
        sibling(part, 2, mine)
        halves[part] = (h0, h1)
    last = [[None] * 4 for _ in range(3)]

    def relative(part, rel):
        b = ORDERS[part][1]
        return moved(xyz, b, (0, -1, 1, 2)[rel])[b]

    def forward(part, rel):
        a, b, c = ORDERS[part]
        bv = relative(part, rel)
        third[part][rel][0].wait_recv()
        cv = moved(xyz, c, -1)[c]
        h0 = remote(part, 15 + 2 * rel, None, line(part, bv, cv, 0), device_of(moved(xyz, c, 1), core))
        sibling(part, 4 + rel, line(part, bv, cv))
        third[part][rel][1].wait_recv()
        cv = moved(xyz, c, 1)[c]
        h1 = remote(part, 16 + 2 * rel, None, line(part, bv, cv, 2), device_of(moved(xyz, c, -1), core))
        sibling(part, 8 + rel, line(part, bv, cv))
        last[part][rel] = (h0, h1)

    for part in range(3):
        forward(part, 0)
    for part in range(3):
        a, b, c = ORDERS[part]
        halves[part][0].wait_recv()
        halves[part][1].wait_recv()
        mine = line(part, relative(part, 3), xyz[c])
        cp = remote(part, 13, None, mine, device_of(moved(xyz, c, 1), core))
        cm = remote(part, 14, None, mine, device_of(moved(xyz, c, -1), core))
        third[part][3] = (cp, cm)
        sibling(part, 3, mine)
    for rel in (1, 2, 3):
        for part in range(3):
            forward(part, rel)
    for rel in range(4):
        for part in range(3):
            a, b, c = ORDERS[part]
            last[part][rel][0].wait_recv()
            last[part][rel][1].wait_recv()
            sibling(part, 12 + rel, line(part, relative(part, rel), moved(xyz, c, 2)[c]))
    for copy in sib:
        copy.wait()
    for copy in waits:
        copy.wait_send()


def gather(shard):
    return pl.pallas_call(
        gather_kernel,
        out_shape=jax.ShapeDtypeStruct((4, 4, 4, 2, 80, 1024), BF),
        in_specs=[pl.BlockSpec(memory_space=pl.ANY)],
        out_specs=pl.BlockSpec(memory_space=pl.ANY),
        scratch_shapes=[
            pltpu.SemaphoreType.DMA((3,)),
            pltpu.SemaphoreType.DMA((3, 23)),
            pltpu.SemaphoreType.DMA((3, 23)),
            pltpu.SemaphoreType.DMA((3, 16)),
            pltpu.SemaphoreType.DMA((3, 16)),
        ],
        compiler_params=pltpu.CompilerParams(collective_id=0, has_side_effects=True),
    )(shard)


RELS = (0, -1, 1, 2)


def scatter_kernel(g, out, tail, acc, r0, xb0, xb1, xb2, yb0, yb1, yb2, ub0, ub1, ub2, vb0, vb1, vb2, tb0, tb1, tb2,
                   load_sem, sib_send, sib_recv, send_sem, recv_sem):
    xyz, core = place()
    enter(xyz, core)
    xb, yb, ub, vb, tb = (xb0, xb1, xb2), (yb0, yb1, yb2), (ub0, ub1, ub2), (vb0, vb1, vb2), (tb0, tb1, tb2)
    sends = []

    def lanes(part):
        return pl.ds(*LANES[part])

    def bval(part, rel):
        b = ORDERS[part][1]
        return moved(xyz, b, RELS[rel])[b]

    def cval(part, step):
        c = ORDERS[part][2]
        return moved(xyz, c, step)[c]

    def spot(part, a_value, b_value, c_value):
        a, b, c = ORDERS[part]
        index = [None] * 3
        index[a], index[b], index[c] = a_value, b_value, c_value
        return tuple(index)

    def push(part, slot, src, dst, axis, step):
        copy = pltpu.make_async_remote_copy(
            src_ref=src, dst_ref=dst, send_sem=send_sem.at[part, slot], recv_sem=recv_sem.at[part, slot],
            device_id=device_of(moved(xyz, axis, step), core), device_id_type=MESH)
        copy.start()
        sends.append(copy)
        return copy

    GROUPS = (2, 1, -1, 0)
    local, sib = {}, {}
    n = 0
    for group in range(4):
        for rel in (3, 1, 2, 0):
            for part in range(3):
                i = spot(part, slice(None), bval(part, rel), cval(part, GROUPS[group]))
                here = acc.at[i + (slice(None), lanes(part))]
                there = r0.at[i + (slice(None), lanes(part))]
                lc = pltpu.make_async_copy(g.at[i + (core, slice(None), lanes(part))], here, load_sem.at[part, group * 4 + rel])
                lc.start()
                sc = pltpu.make_async_remote_copy(
                    src_ref=g.at[i + (1 - core, slice(None), lanes(part))], dst_ref=there,
                    send_sem=sib_send.at[part, group * 4 + rel], recv_sem=sib_recv.at[part, group * 4 + rel],
                    device_id=device_of(xyz, 1 - core), device_id_type=MESH)
                sc.start()
                local[part, group, rel] = lc
                sib[part, group, rel] = sc

    def add_line(part, b_value, c_value, bufs, lo=0, count=4):
        def step(s, carry):
            i = spot(part, s + lo, b_value, c_value) + (slice(None), lanes(part))
            total = acc[i].astype(jnp.float32)
            for buf in bufs:
                total = total + buf(s, i).astype(jnp.float32)
            acc[i] = total.astype(BF)
            return carry
        lax.fori_loop(0, count, step, 0)

    def ready(part, group, rel):
        local[part, group, rel].wait()
        sib[part, group, rel].wait_recv()

    def own(s, i):
        return r0[i]

    def line(part, b_value, c_value):
        return acc.at[spot(part, slice(None), b_value, c_value) + (slice(None), lanes(part))]

    first, second = {}, {}
    for rel in (3, 1, 2, 0):
        for part in range(3):
            c = ORDERS[part][2]
            bv, cv = bval(part, rel), cval(part, 2)
            ready(part, 0, rel)
            add_line(part, bv, cv, [own])
            k = {3: 0, 0: 1, 1: 2, 2: 3}[rel]
            first[part, rel] = push(part, k, line(part, bv, cv), xb[part].at[k], c, 1 if rel in (3, 0) else -1)
    for rel in (3, 1, 2, 0):
        for part in range(3):
            c = ORDERS[part][2]
            bv = bval(part, rel)
            k = {3: 0, 0: 1, 1: 2, 2: 3}[rel]
            via_plus = rel in (3, 0)
            for step, group, slot in ((1, 1, 4 + rel), (-1, 2, 8 + rel)):
                ready(part, group, rel)
                bufs = [own]
                if via_plus == (step == 1):
                    first[part, rel].wait_recv()
                    bufs.append(lambda s, i, part=part, k=k: xb[part][k, s])
                add_line(part, bv, cval(part, step), bufs)
                second[part, rel, step] = push(part, slot, line(part, bv, cval(part, step)), yb[part].at[(0 if step == 1 else 4) + rel], c, step)
    third, fourth = {}, {}
    for rel in (3, 1, 2, 0):
        for part in range(3):
            a, b, c = ORDERS[part]
            bv, cv = bval(part, rel), xyz[c]
            ready(part, 3, rel)
            second[part, rel, 1].wait_recv()
            second[part, rel, -1].wait_recv()
            bufs = [own, lambda s, i, part=part, rel=rel: yb[part][rel, s], lambda s, i, part=part, rel=rel: yb[part][4 + rel, s]]
            add_line(part, bv, cv, bufs)
            if rel == 3:
                for half, step in ((0, 1), (1, -1)):
                    src = acc.at[spot(part, pl.ds(2 * half, 2), bv, cv) + (slice(None), lanes(part))]
                    third[part, half] = push(part, 12 + half, src, ub[part].at[half], b, step)
            if rel == 1:
                third[part, 1].wait_recv()
                add_line(part, bv, cv, [lambda s, i, part=part: ub[part][1, s]], 2, 2)
                fourth[part, -1] = push(part, 14, line(part, bv, cv), vb[part].at[0], b, -1)
            if rel == 2:
                third[part, 0].wait_recv()
                add_line(part, bv, cv, [lambda s, i, part=part: ub[part][0, s]], 0, 2)
                fourth[part, 1] = push(part, 15, line(part, bv, cv), vb[part].at[1], b, 1)
    def one(part, step):
        a, b, c = ORDERS[part]
        return acc.at[moved(xyz, a, step) + (slice(None), lanes(part))]

    fifth = {}
    for part in range(3):
        a, b, c = ORDERS[part]
        fourth[part, 1].wait_recv()
        fourth[part, -1].wait_recv()
        add_line(part, xyz[b], xyz[c], [lambda s, i, part=part: vb[part][0, s], lambda s, i, part=part: vb[part][1, s]])
        fifth[part, 0] = push(part, 16, one(part, 2), tb[part].at[0], a, 1)
        fifth[part, 1] = push(part, 17, one(part, -1), tb[part].at[1], a, -1)
    for part in range(3):
        a, b, c = ORDERS[part]
        fifth[part, 0].wait_recv()
        i = moved(xyz, a, 1) + (slice(None), lanes(part))
        acc[i] = (acc[i].astype(jnp.float32) + tb[part][0].astype(jnp.float32)).astype(BF)
        fifth[part, 2] = push(part, 18, one(part, 1), tb[part].at[2], a, 1)
    for part in range(3):
        fifth[part, 1].wait_recv()
        fifth[part, 2].wait_recv()
        total = acc[xyz + (slice(None), lanes(part))].astype(jnp.float32) + tb[part][1].astype(jnp.float32) + tb[part][2].astype(jnp.float32)
        start, size = LANES[part]
        if part < 2:
            out[:, start:start + size] = total
        else:
            out[:, 768:960] = total[:, :192]
            tail[...] = total[0:8, 128:256]
    for copy in sib.values():
        copy.wait_send()
    for copy in sends:
        copy.wait_send()


def scatter(g):
    lines = lambda k, m: [pltpu.VMEM((k, m, 80, size), BF) for _, size in LANES]
    return pl.pallas_call(
        scatter_kernel,
        out_shape=(jax.ShapeDtypeStruct((80, 960), jnp.float32), jax.ShapeDtypeStruct((8, 128), jnp.float32)),
        in_specs=[pl.BlockSpec(memory_space=pl.ANY)],
        out_specs=(pl.BlockSpec(memory_space=pltpu.VMEM), pl.BlockSpec(memory_space=pltpu.VMEM)),
        scratch_shapes=[
            pltpu.VMEM((4, 4, 4, 80, 1024), BF),
            pltpu.VMEM((4, 4, 4, 80, 1024), BF),
            *lines(4, 4), *lines(8, 4), *lines(2, 2), *lines(2, 4),
            *[pltpu.VMEM((3, 80, size), BF) for _, size in LANES],
            pltpu.SemaphoreType.DMA((3, 16)),
            pltpu.SemaphoreType.DMA((3, 16)),
            pltpu.SemaphoreType.DMA((3, 16)),
            pltpu.SemaphoreType.DMA((3, 19)),
            pltpu.SemaphoreType.DMA((3, 19)),
        ],
        compiler_params=pltpu.CompilerParams(collective_id=1, has_side_effects=True, vmem_limit_bytes=56 << 20),
    )(g)


def body(tokens, layer_weights, norm_gains, seq_ids, out_grad):
    cosine_table, sine_table, allowed = tables(seq_ids, HEAD_SIZE)
    shard = jnp.pad(layer_weights[0].T, ((0, 0), (0, 64)))
    shard = lax.dynamic_update_slice(shard, norm_gains, (0, 960))
    packed = gather(shard).reshape(128, 80, 1024)
    gain_row = packed[:, 0, 960:975].reshape(1920)
    weights = packed.reshape(10240, 1024)[:, :960].T
    stream, saved = layer_forward(
        tokens.astype(jnp.float32), weights, gain_row, cosine_table, sine_table, allowed
    )
    upstream, parts, gain_term = layer_backward(
        out_grad.astype(jnp.float32), saved, weights, gain_row, cosine_table, sine_table, allowed
    )
    grads = jnp.concatenate([p.astype(BF).T for p in parts], axis=0).reshape(128, 80, 960)
    tail = jnp.pad(gain_term.reshape(128, 1, 15).astype(BF), ((0, 0), (0, 79), (0, 49)))
    grads = jnp.concatenate([grads, tail], axis=2).reshape(4, 4, 4, 2, 80, 1024)
    weight_grad, last = scatter(grads)
    return (
        stream.astype(jnp.bfloat16),
        upstream,
        weight_grad.T[None],
        last[0:1, 64:79],
    )


def solution(mesh):
    return jax.shard_map(
        body,
        mesh=mesh,
        in_specs=(
            P(("fsdp", "dp"), None),
            P(None, None, ("fsdp", "dp")),
            P(None, ("fsdp", "dp")),
            P(("fsdp", "dp")),
            P(("fsdp", "dp"), None),
        ),
        out_specs=(
            P(("fsdp", "dp"), None),
            P(("fsdp", "dp"), None),
            P(None, None, ("fsdp", "dp")),
            P(None, ("fsdp", "dp")),
        ),
        check_vma=False,
    )
```

```python
import functools
import numpy as np
import jax
import jax.numpy as jnp
from jax import lax
from jax.experimental import pallas as pl
from jax.experimental.pallas import tpu as pltpu
from jax.sharding import PartitionSpec as P

epsilon = 1e-05
rope_base = 100000.0
MESH = pl.DeviceIdType.MESH
BF = jnp.bfloat16
LANES = ((0, 384), (384, 384), (768, 256))
ORDERS = ((0, 1, 2), (1, 2, 0), (2, 0, 1))


def place():
    f = lax.axis_index("fsdp")
    d = lax.axis_index("dp")
    return (f // 4, f % 4, d // 2), d % 2


def device_of(xyz, core):
    return (xyz[0] * 4 + xyz[1], xyz[2] * 2 + core)


def moved(xyz, axis, step):
    out = list(xyz)
    out[axis] = (out[axis] + step + 4) % 4
    return tuple(out)


def enter(xyz, core):
    barrier = pltpu.get_barrier_semaphore()
    for axis in range(3):
        for step in (1, -1):
            pl.semaphore_signal(barrier, inc=1, device_id=device_of(moved(xyz, axis, step), core), device_id_type=MESH)
    pl.semaphore_signal(barrier, inc=1, device_id=device_of(xyz, 1 - core), device_id_type=MESH)
    pl.semaphore_wait(barrier, 7)


def gather_kernel(shard, out, own_sem, send_sem, recv_sem, sib_send, sib_recv):
    xyz, core = place()
    enter(xyz, core)
    counts = [0]
    waits = []

    def region(part, index):
        start, size = LANES[part]
        return out.at[index[0], index[1], index[2], core, :, pl.ds(start, size)]

    def remote(part, slot, src, index, to):
        copy = pltpu.make_async_remote_copy(
            src_ref=region(part, index) if src is None else src,
            dst_ref=region(part, index),
            send_sem=send_sem.at[part, slot],
            recv_sem=recv_sem.at[part, slot],
            device_id=to,
            device_id_type=MESH,
        )
        copy.start()
        waits.append(copy)
        return copy

    def sibling(part, slot, index):
        copy = pltpu.make_async_remote_copy(
            src_ref=region(part, index),
            dst_ref=region(part, index),
            send_sem=sib_send.at[part, slot],
            recv_sem=sib_recv.at[part, slot],
            device_id=device_of(xyz, 1 - core),
            device_id_type=MESH,
        )
        copy.start()
        sib.append(copy)

    sib = []
    own = []
    for part in range(3):
        start, size = LANES[part]
        c = pltpu.make_async_copy(shard.at[:, pl.ds(start, size)], region(part, xyz), own_sem.at[part])
        c.start()
        own.append(c)

    first = [None] * 3
    for part in range(3):
        a = ORDERS[part][0]
        start, size = LANES[part]
        src = shard.at[:, pl.ds(start, size)]
        plus = remote(part, 0, src, xyz, device_of(moved(xyz, a, 1), core))
        minus = remote(part, 1, src, xyz, device_of(moved(xyz, a, -1), core))
        first[part] = (plus, minus)
    second = [None] * 3
    for part in range(3):
        a = ORDERS[part][0]
        first[part][0].wait_recv()
        second[part] = remote(part, 2, None, moved(xyz, a, -1), device_of(moved(xyz, a, 1), core))
    for part in range(3):
        own[part].wait()

    def line(part, b_value, c_value, lo=None):
        a, b, c = ORDERS[part]
        index = [None] * 3
        index[a] = slice(None) if lo is None else pl.ds(lo, 2)
        index[b] = b_value
        index[c] = c_value
        return tuple(index)

    third = [[None] * 4 for _ in range(3)]
    hops = [None] * 3
    for part in range(3):
        a, b, c = ORDERS[part]
        first[part][1].wait_recv()
        second[part].wait_recv()
        mine = line(part, xyz[b], xyz[c])
        bp = remote(part, 3, None, mine, device_of(moved(xyz, b, 1), core))
        bm = remote(part, 4, None, mine, device_of(moved(xyz, b, -1), core))
        hops[part] = (bp, bm)
        cp = remote(part, 7, None, mine, device_of(moved(xyz, c, 1), core))
        cm = remote(part, 8, None, mine, device_of(moved(xyz, c, -1), core))
        third[part][0] = (cp, cm)
        sibling(part, 0, mine)
    halves = [None] * 3
    for part in range(3):
        a, b, c = ORDERS[part]
        hops[part][0].wait_recv()
        bv = moved(xyz, b, -1)[b]
        h0 = remote(part, 5, None, line(part, bv, xyz[c], 0), device_of(moved(xyz, b, 1), core))
        mine = line(part, bv, xyz[c])
        cp = remote(part, 9, None, mine, device_of(moved(xyz, c, 1), core))
        cm = remote(part, 10, None, mine, device_of(moved(xyz, c, -1), core))
        third[part][1] = (cp, cm)
        sibling(part, 1, mine)
        hops[part][1].wait_recv()
        bv = moved(xyz, b, 1)[b]
        h1 = remote(part, 6, None, line(part, bv, xyz[c], 2), device_of(moved(xyz, b, -1), core))
        mine = line(part, bv, xyz[c])
        cp = remote(part, 11, None, mine, device_of(moved(xyz, c, 1), core))
        cm = remote(part, 12, None, mine, device_of(moved(xyz, c, -1), core))
        third[part][2] = (cp, cm)
        sibling(part, 2, mine)
        halves[part] = (h0, h1)
    last = [[None] * 4 for _ in range(3)]

    def relative(part, rel):
        b = ORDERS[part][1]
        return moved(xyz, b, (0, -1, 1, 2)[rel])[b]

    def forward(part, rel):
        a, b, c = ORDERS[part]
        bv = relative(part, rel)
        third[part][rel][0].wait_recv()
        cv = moved(xyz, c, -1)[c]
        h0 = remote(part, 15 + 2 * rel, None, line(part, bv, cv, 0), device_of(moved(xyz, c, 1), core))
        sibling(part, 4 + rel, line(part, bv, cv))
        third[part][rel][1].wait_recv()
        cv = moved(xyz, c, 1)[c]
        h1 = remote(part, 16 + 2 * rel, None, line(part, bv, cv, 2), device_of(moved(xyz, c, -1), core))
        sibling(part, 8 + rel, line(part, bv, cv))
        last[part][rel] = (h0, h1)

    for part in range(3):
        forward(part, 0)
    for part in range(3):
        a, b, c = ORDERS[part]
        halves[part][0].wait_recv()
        halves[part][1].wait_recv()
        mine = line(part, relative(part, 3), xyz[c])
        cp = remote(part, 13, None, mine, device_of(moved(xyz, c, 1), core))
        cm = remote(part, 14, None, mine, device_of(moved(xyz, c, -1), core))
        third[part][3] = (cp, cm)
        sibling(part, 3, mine)
    for rel in (1, 2, 3):
        for part in range(3):
            forward(part, rel)
    for rel in range(4):
        for part in range(3):
            a, b, c = ORDERS[part]
            last[part][rel][0].wait_recv()
            last[part][rel][1].wait_recv()
            sibling(part, 12 + rel, line(part, relative(part, rel), moved(xyz, c, 2)[c]))
    for copy in sib:
        copy.wait()
    for copy in waits:
        copy.wait_send()


def gather(shard):
    return pl.pallas_call(
        gather_kernel,
        out_shape=jax.ShapeDtypeStruct((4, 4, 4, 2, 80, 1024), BF),
        in_specs=[pl.BlockSpec(memory_space=pl.ANY)],
        out_specs=pl.BlockSpec(memory_space=pl.ANY),
        scratch_shapes=[
            pltpu.SemaphoreType.DMA((3,)),
            pltpu.SemaphoreType.DMA((3, 23)),
            pltpu.SemaphoreType.DMA((3, 23)),
            pltpu.SemaphoreType.DMA((3, 16)),
            pltpu.SemaphoreType.DMA((3, 16)),
        ],
        compiler_params=pltpu.CompilerParams(collective_id=0, has_side_effects=True),
    )(shard)


RELS = (0, -1, 1, 2)


def scatter_kernel(g, out, tail, acc, r0, xb0, xb1, xb2, yb0, yb1, yb2, ub0, ub1, ub2, vb0, vb1, vb2, tb0, tb1, tb2,
                   load_sem, sib_send, sib_recv, send_sem, recv_sem):
    xyz, core = place()
    enter(xyz, core)
    xb, yb, ub, vb, tb = (xb0, xb1, xb2), (yb0, yb1, yb2), (ub0, ub1, ub2), (vb0, vb1, vb2), (tb0, tb1, tb2)
    sends = []

    def lanes(part):
        return pl.ds(*LANES[part])

    def bval(part, rel):
        b = ORDERS[part][1]
        return moved(xyz, b, RELS[rel])[b]

    def cval(part, step):
        c = ORDERS[part][2]
        return moved(xyz, c, step)[c]

    def spot(part, a_value, b_value, c_value):
        a, b, c = ORDERS[part]
        index = [None] * 3
        index[a], index[b], index[c] = a_value, b_value, c_value
        return tuple(index)

    def push(part, slot, src, dst, axis, step):
        copy = pltpu.make_async_remote_copy(
            src_ref=src, dst_ref=dst, send_sem=send_sem.at[part, slot], recv_sem=recv_sem.at[part, slot],
            device_id=device_of(moved(xyz, axis, step), core), device_id_type=MESH)
        copy.start()
        sends.append(copy)
        return copy

    GROUPS = (2, 1, -1, 0)
    local, sib = {}, {}
    n = 0
    for group in range(4):
        for rel in (3, 1, 2, 0):
            for part in range(3):
                i = spot(part, slice(None), bval(part, rel), cval(part, GROUPS[group]))
                here = acc.at[i + (slice(None), lanes(part))]
                there = r0.at[i + (slice(None), lanes(part))]
                lc = pltpu.make_async_copy(g.at[i + (core, slice(None), lanes(part))], here, load_sem.at[part, group * 4 + rel])
                lc.start()
                sc = pltpu.make_async_remote_copy(
                    src_ref=g.at[i + (1 - core, slice(None), lanes(part))], dst_ref=there,
                    send_sem=sib_send.at[part, group * 4 + rel], recv_sem=sib_recv.at[part, group * 4 + rel],
                    device_id=device_of(xyz, 1 - core), device_id_type=MESH)
                sc.start()
                local[part, group, rel] = lc
                sib[part, group, rel] = sc

    def add_line(part, b_value, c_value, bufs, lo=0, count=4):
        def step(s, carry):
            i = spot(part, s + lo, b_value, c_value) + (slice(None), lanes(part))
            total = acc[i].astype(jnp.float32)
            for buf in bufs:
                total = total + buf(s, i).astype(jnp.float32)
            acc[i] = total.astype(BF)
            return carry
        lax.fori_loop(0, count, step, 0)

    def ready(part, group, rel):
        local[part, group, rel].wait()
        sib[part, group, rel].wait_recv()

    def own(s, i):
        return r0[i]

    def line(part, b_value, c_value):
        return acc.at[spot(part, slice(None), b_value, c_value) + (slice(None), lanes(part))]

    first, second = {}, {}
    for rel in (3, 1, 2, 0):
        for part in range(3):
            c = ORDERS[part][2]
            bv, cv = bval(part, rel), cval(part, 2)
            ready(part, 0, rel)
            add_line(part, bv, cv, [own])
            k = {3: 0, 0: 1, 1: 2, 2: 3}[rel]
            first[part, rel] = push(part, k, line(part, bv, cv), xb[part].at[k], c, 1 if rel in (3, 0) else -1)
    for rel in (3, 1, 2, 0):
        for part in range(3):
            c = ORDERS[part][2]
            bv = bval(part, rel)
            k = {3: 0, 0: 1, 1: 2, 2: 3}[rel]
            via_plus = rel in (3, 0)
            for step, group, slot in ((1, 1, 4 + rel), (-1, 2, 8 + rel)):
                ready(part, group, rel)
                bufs = [own]
                if via_plus == (step == 1):
                    first[part, rel].wait_recv()
                    bufs.append(lambda s, i, part=part, k=k: xb[part][k, s])
                add_line(part, bv, cval(part, step), bufs)
                second[part, rel, step] = push(part, slot, line(part, bv, cval(part, step)), yb[part].at[(0 if step == 1 else 4) + rel], c, step)
    third, fourth = {}, {}
    for rel in (3, 1, 2, 0):
        for part in range(3):
            a, b, c = ORDERS[part]
            bv, cv = bval(part, rel), xyz[c]
            ready(part, 3, rel)
            second[part, rel, 1].wait_recv()
            second[part, rel, -1].wait_recv()
            bufs = [own, lambda s, i, part=part, rel=rel: yb[part][rel, s], lambda s, i, part=part, rel=rel: yb[part][4 + rel, s]]
            add_line(part, bv, cv, bufs)
            if rel == 3:
                for half, step in ((0, 1), (1, -1)):
                    src = acc.at[spot(part, pl.ds(2 * half, 2), bv, cv) + (slice(None), lanes(part))]
                    third[part, half] = push(part, 12 + half, src, ub[part].at[half], b, step)
            if rel == 1:
                third[part, 1].wait_recv()
                add_line(part, bv, cv, [lambda s, i, part=part: ub[part][1, s]], 2, 2)
                fourth[part, -1] = push(part, 14, line(part, bv, cv), vb[part].at[0], b, -1)
            if rel == 2:
                third[part, 0].wait_recv()
                add_line(part, bv, cv, [lambda s, i, part=part: ub[part][0, s]], 0, 2)
                fourth[part, 1] = push(part, 15, line(part, bv, cv), vb[part].at[1], b, 1)
    def one(part, step):
        a, b, c = ORDERS[part]
        return acc.at[moved(xyz, a, step) + (slice(None), lanes(part))]

    fifth = {}
    for part in range(3):
        a, b, c = ORDERS[part]
        fourth[part, 1].wait_recv()
        fourth[part, -1].wait_recv()
        add_line(part, xyz[b], xyz[c], [lambda s, i, part=part: vb[part][0, s], lambda s, i, part=part: vb[part][1, s]])
        fifth[part, 0] = push(part, 16, one(part, 2), tb[part].at[0], a, 1)
        fifth[part, 1] = push(part, 17, one(part, -1), tb[part].at[1], a, -1)
    for part in range(3):
        a, b, c = ORDERS[part]
        fifth[part, 0].wait_recv()
        i = moved(xyz, a, 1) + (slice(None), lanes(part))
        acc[i] = (acc[i].astype(jnp.float32) + tb[part][0].astype(jnp.float32)).astype(BF)
        fifth[part, 2] = push(part, 18, one(part, 1), tb[part].at[2], a, 1)
    for part in range(3):
        fifth[part, 1].wait_recv()
        fifth[part, 2].wait_recv()
        total = acc[xyz + (slice(None), lanes(part))].astype(jnp.float32) + tb[part][1].astype(jnp.float32) + tb[part][2].astype(jnp.float32)
        start, size = LANES[part]
        if part < 2:
            out[:, start:start + size] = total
        else:
            out[:, 768:960] = total[:, :192]
            tail[...] = total[0:8, 128:256]
    for copy in sib.values():
        copy.wait_send()
    for copy in sends:
        copy.wait_send()


def scatter(g):
    lines = lambda k, m: [pltpu.VMEM((k, m, 80, size), BF) for _, size in LANES]
    return pl.pallas_call(
        scatter_kernel,
        out_shape=(jax.ShapeDtypeStruct((80, 960), jnp.float32), jax.ShapeDtypeStruct((8, 128), jnp.float32)),
        in_specs=[pl.BlockSpec(memory_space=pl.ANY)],
        out_specs=(pl.BlockSpec(memory_space=pltpu.VMEM), pl.BlockSpec(memory_space=pltpu.VMEM)),
        scratch_shapes=[
            pltpu.VMEM((4, 4, 4, 80, 1024), BF),
            pltpu.VMEM((4, 4, 4, 80, 1024), BF),
            *lines(4, 4), *lines(8, 4), *lines(2, 2), *lines(2, 4),
            *[pltpu.VMEM((3, 80, size), BF) for _, size in LANES],
            pltpu.SemaphoreType.DMA((3, 16)),
            pltpu.SemaphoreType.DMA((3, 16)),
            pltpu.SemaphoreType.DMA((3, 16)),
            pltpu.SemaphoreType.DMA((3, 19)),
            pltpu.SemaphoreType.DMA((3, 19)),
        ],
        compiler_params=pltpu.CompilerParams(collective_id=1, has_side_effects=True, vmem_limit_bytes=56 << 20),
    )(g)


F32 = jnp.float32
SCALE = 64 ** (-0.5)


def nt(left, right):
    return lax.dot_general(left, right, (((1,), (1,)), ((), ())), preferred_element_type=F32)


def tn(left, right):
    return lax.dot_general(left, right, (((0,), (0,)), ((), ())), preferred_element_type=F32)


def nn(left, right):
    return jnp.dot(left, right, preferred_element_type=F32)


def turn(pair, cos, sin, direction):
    a, b = pair[0:32], pair[32:64]
    return jnp.concatenate([a * cos - direction * b * sin, b * cos + direction * a * sin], axis=0)


def real(values):
    lane = lax.broadcasted_iota(jnp.int32, values.shape, 1)
    return jnp.where(lane < 960, values, 0.0)


def prepare(xt, et, ids, freq, e, x32, cos3, sin3, mask3):
    zero = jnp.zeros((256, 64), F32)
    x32[:, 0:960] = xt[...].astype(F32).T
    x32[:, 960:1024] = zero
    e[:, 0:960] = et[...].astype(F32).T.astype(BF)
    e[:, 960:1024] = zero.astype(BF)
    across = jnp.broadcast_to(ids[...], (256, 256))
    same = across == across.T
    down = lax.broadcasted_iota(jnp.int32, (256, 256), 0)
    along = lax.broadcasted_iota(jnp.int32, (256, 256), 1)
    start = jnp.min(jnp.where(same, down, 256).astype(F32), axis=0, keepdims=True)
    row = lax.broadcasted_iota(jnp.int32, (1, 256), 1).astype(F32)
    angle = freq[...][:, 0:1] * (row - start)
    cos, sin = jnp.cos(angle), jnp.sin(angle)
    allowed = jnp.where(same & (down <= along), 0.0, -1e30)
    for i in range(3):
        cos3[:, 256 * i : 256 * i + 256] = cos
        sin3[:, 256 * i : 256 * i + 256] = sin
        mask3[:, 256 * i : 256 * i + 256] = allowed


def three(ref, k):
    return jnp.concatenate([ref[3 * k], ref[3 * k + 1], ref[3 * k + 2]], axis=1)


def attention(w, gains, x32, n1, r1, qt, kt, vt, p, ot, mid, n2, r2, cos3, sin3, mask3):
    x = x32[...]
    inv = lax.rsqrt(jnp.sum(x * x, axis=1, keepdims=True) * (1.0 / 960) + epsilon)
    r1[...] = inv
    n1[...] = (x * inv * gains[0:1, :]).astype(BF)

    def project(y, lo, hi):
        rows = w[0, y].reshape(640, 1024)[lo:hi]
        return nt(rows, n1[...])

    cos, sin = cos3[:, 0:256], sin3[:, 0:256]
    part = project(0, 0, 640)
    for h in range(10):
        qt[h] = turn(part[64 * h : 64 * h + 64], cos, sin, 1.0).astype(BF)
    part = project(1, 0, 640)
    for h in range(5):
        qt[10 + h] = turn(part[64 * h : 64 * h + 64], cos, sin, 1.0).astype(BF)
        kt[h] = turn(part[320 + 64 * h : 384 + 64 * h], cos, sin, 1.0).astype(BF)
    part = project(2, 0, 320)
    for h in range(5):
        vt[h] = part[64 * h : 64 * h + 64].astype(BF)

    def group(k, carry):
        q3 = three(qt, k)
        s = nn(kt[k].T, q3) * SCALE
        s = jnp.where(mask3[...] == 0.0, s, -1e30)
        s = jnp.exp(s - jnp.max(s, axis=0, keepdims=True))
        s = (s * (1.0 / jnp.sum(s, axis=0, keepdims=True))).astype(BF)
        p[k] = s
        o3 = nn(vt[k], s).astype(BF)
        for i in range(3):
            ot[3 * k + i] = o3[:, 256 * i : 256 * i + 256]
        return carry

    lax.fori_loop(0, 5, group, 0)
    o = ot[...].reshape(960, 256)
    m = x32[...] + tn(o[0:320], w[0, 2].reshape(640, 1024)[320:640])
    m = real(m + tn(o[320:960], w[0, 3].reshape(640, 1024)))
    mid[...] = m
    inv = lax.rsqrt(jnp.sum(m * m, axis=1, keepdims=True) * (1.0 / 960) + epsilon)
    r2[...] = inv
    n2[...] = (m * inv * gains[1:2, :]).astype(BF)


def feed(w, y, n2, e, down, dn, store):
    w1, w2, w3 = w[1, y].reshape(640, 1024), w[2, y].reshape(640, 1024), w[3, y].reshape(640, 1024)
    gate = nt(w1, n2[...])
    up = nt(w2, n2[...])
    sig = jax.nn.sigmoid(gate)
    hidden = (gate * sig * up).astype(BF)
    store(3, y, nn(hidden, e[...]))
    down[...] += tn(hidden, w3)
    dh = nt(w3, e[...])
    d_gate = (dh * up * sig * (1.0 + gate * (1.0 - sig))).astype(BF)
    d_up = (dh * gate * sig).astype(BF)
    store(1, y, nn(d_gate, n2[...]))
    store(2, y, nn(d_up, n2[...]))
    dn[...] += tn(d_gate, w1) + tn(d_up, w2)


def norm_back(d_norm, values, inv, gain):
    d_norm = real(d_norm)
    u = d_norm * gain
    d_gain = jnp.sum(d_norm * values * inv, axis=0, keepdims=True)
    mean = jnp.sum(u * values, axis=1, keepdims=True) * (1.0 / 960)
    return inv * u - values * (inv * inv * inv * mean), d_gain


def attention_back(w, gains, x32, n1, r1, qt, kt, vt, p, ot, mid, r2, e, dn, dm, dmb, dot_, dqkv, cos3, sin3, dg, store_rows, dxt):
    d, dg2 = norm_back(dn[...], mid[...], r2[...], gains[1:2, :])
    d = d + e[...].astype(F32)
    dm[...] = d
    db = d.astype(BF)
    dmb[...] = db
    dg[1:2, :] = dg2
    d_o = nt(w[0, 2].reshape(640, 1024)[320:640], db).astype(BF)
    for h in range(5):
        dot_[h] = d_o[64 * h : 64 * h + 64]
    d_o = nt(w[0, 3].reshape(640, 1024), db).astype(BF)
    for h in range(10):
        dot_[5 + h] = d_o[64 * h : 64 * h + 64]
    o = ot[...].reshape(960, 256)
    store_rows(3, 0, nn(o[320:960], db))

    def group(k, carry):
        d3 = three(dot_, k)
        q3 = three(qt, k)
        pb = p[k]
        dp = nn(vt[k].T, d3)
        pf = pb.astype(F32)
        ds = pf * (dp - jnp.sum(pf * dp, axis=0, keepdims=True))
        ds = (ds * SCALE).astype(BF)
        dqkv[20 + k] = nt(d3, pb).astype(BF)
        dq = turn(nn(kt[k], ds), cos3[...], sin3[...], -1.0).astype(BF)
        for i in range(3):
            dqkv[3 * k + i] = dq[:, 256 * i : 256 * i + 256]
        dqkv[15 + k] = turn(nt(q3, ds), cos3[:, 0:256], sin3[:, 0:256], -1.0).astype(BF)
        return carry

    lax.fori_loop(0, 5, group, 0)
    a = dqkv[0:10].reshape(640, 256)
    store_rows(0, 0, nn(a, n1[...]))
    total = tn(a, w[0, 0].reshape(640, 1024))
    a = dqkv[10:20].reshape(640, 256)
    store_rows(1, 0, nn(a, n1[...]))
    total = total + tn(a, w[0, 1].reshape(640, 1024))
    a = dqkv[20:25].reshape(320, 256)
    store_rows(2, 0, nn(a, n1[...]))
    store_rows(2, 320, nn(o[0:320], dmb[...]))
    total = total + tn(a, w[0, 2].reshape(640, 1024)[0:320])
    d, dg1 = norm_back(total, x32[...], r1[...], gains[0:1, :])
    dg[0:1, :] = dg1
    dxt[...] = (dm[...] + d)[:, 0:960].T


def spread_gains(dg, tails):
    p = lax.broadcasted_iota(jnp.int32, (64, 1024), 1)
    owner = lax.broadcasted_iota(jnp.int32, (64, 1024), 0)
    mine = (p >= 15 * owner) & (p < 15 * owner + 15)
    pos = lax.broadcasted_iota(jnp.int32, (128, 1024), 1)
    lane = lax.broadcasted_iota(jnp.int32, (128, 1024), 0)
    base = ((pos.astype(F32) + 0.5) * (1.0 / 15)).astype(jnp.int32) * 15
    pick = jnp.where(pos - base + 64 == lane, 1.0, 0.0).astype(BF)
    for half in range(2):
        rows = jnp.where(mine, dg[half : half + 1, :], 0.0).astype(BF)
        tails[64 * half : 64 * half + 64, :] = nt(rows, pick)


def layer_kernel(wh, gains, xt, et, ids, freq, gh, yt, dxt, w, g, n1, n2, e, x32, mid, down, dn, dm, dmb, qt, kt, vt, p, ot, dot_, dqkv,
                 r1, r2, cos3, sin3, mask3, dg, tails, in_sem, out_sem):
    def load(x, y):
        return pltpu.make_async_copy(wh.at[x, y], w.at[x, y], in_sem.at[x, y])

    def save(x, y):
        return pltpu.make_async_copy(g.at[x, y], gh.at[x, y], out_sem.at[x, y])

    for x, y in [(0, i) for i in range(4)] + [(x, y) for y in range(4) for x in (1, 2, 3)]:
        load(x, y).start()
    prepare(xt, et, ids, freq, e, x32, cos3, sin3, mask3)
    for y in range(4):
        load(0, y).wait()
    attention(w, gains, x32, n1, r1, qt, kt, vt, p, ot, mid, n2, r2, cos3, sin3, mask3)
    down[...] = jnp.zeros_like(down)
    dn[...] = jnp.zeros_like(dn)

    def store(x, y, value):
        g[x, y] = value.astype(BF).reshape(4, 2, 80, 1024)

    def chunk(y, carry):
        for x in (1, 2, 3):
            load(x, y).wait()
        feed(w, y, n2, e, down, dn, store)
        return carry

    lax.fori_loop(0, 4, chunk, 0)
    yt[...] = (mid[...] + down[...])[:, 0:960].T.astype(BF)

    def store_rows(y, at, value):
        rows = value.shape[0]
        value = value.astype(BF)
        if rows == 640:
            g[0, y] = value.reshape(4, 2, 80, 1024)
        else:
            g[0, y, at // 160 : at // 160 + 2] = value.reshape(2, 2, 80, 1024)

    attention_back(w, gains, x32, n1, r1, qt, kt, vt, p, ot, mid, r2, e, dn, dm, dmb, dot_, dqkv, cos3, sin3, dg, store_rows, dxt)
    spread_gains(dg, tails)
    for x in range(4):
        for y in range(4):
            def place_tail(z, carry, x=x, y=y):
                for c in range(2):
                    old = g[x, y, z, c, 0:16, 896:1024].astype(F32)
                    row = tails[pl.ds(((x * 4 + y) * 4 + z) * 2 + c, 1), :]
                    r = lax.broadcasted_iota(jnp.int32, (16, 128), 0)
                    l = lax.broadcasted_iota(jnp.int32, (16, 128), 1)
                    g[x, y, z, c, 0:16, 896:1024] = jnp.where((r == 0) & (l >= 64), row, old).astype(BF)
                return carry
            lax.fori_loop(0, 4, place_tail, 0)
            save(x, y).start()
    for x in range(4):
        for y in range(4):
            save(x, y).wait()


def layer(packed, gains, tokens_t, grad_t, ids, freq):
    vm = pl.BlockSpec(memory_space=pltpu.VMEM)
    hbm = pl.BlockSpec(memory_space=pl.ANY)
    return pl.pallas_call(
        layer_kernel,
        out_shape=(
            jax.ShapeDtypeStruct((4, 4, 4, 2, 80, 1024), BF),
            jax.ShapeDtypeStruct((960, 256), BF),
            jax.ShapeDtypeStruct((960, 256), F32),
        ),
        in_specs=[hbm, vm, vm, vm, vm, vm],
        out_specs=(hbm, vm, vm),
        scratch_shapes=[
            pltpu.VMEM((4, 4, 4, 2, 80, 1024), BF),
            pltpu.VMEM((4, 4, 4, 2, 80, 1024), BF),
            pltpu.VMEM((256, 1024), BF),
            pltpu.VMEM((256, 1024), BF),
            pltpu.VMEM((256, 1024), BF),
            pltpu.VMEM((256, 1024), F32),
            pltpu.VMEM((256, 1024), F32),
            pltpu.VMEM((256, 1024), F32),
            pltpu.VMEM((256, 1024), F32),
            pltpu.VMEM((256, 1024), F32),
            pltpu.VMEM((256, 1024), BF),
            pltpu.VMEM((15, 64, 256), BF),
            pltpu.VMEM((5, 64, 256), BF),
            pltpu.VMEM((5, 64, 256), BF),
            pltpu.VMEM((5, 256, 768), BF),
            pltpu.VMEM((15, 64, 256), BF),
            pltpu.VMEM((15, 64, 256), BF),
            pltpu.VMEM((25, 64, 256), BF),
            pltpu.VMEM((256, 1), F32),
            pltpu.VMEM((256, 1), F32),
            pltpu.VMEM((32, 768), F32),
            pltpu.VMEM((32, 768), F32),
            pltpu.VMEM((256, 768), F32),
            pltpu.VMEM((2, 1024), F32),
            pltpu.VMEM((128, 128), F32),
            pltpu.SemaphoreType.DMA((4, 4)),
            pltpu.SemaphoreType.DMA((4, 4)),
        ],
        compiler_params=pltpu.CompilerParams(vmem_limit_bytes=63 << 20),
    )(packed, gains, tokens_t, grad_t, ids, freq)


def body(tokens, layer_weights, norm_gains, seq_ids, out_grad):
    shard = jnp.pad(layer_weights[0].T, ((0, 0), (0, 64)))
    shard = lax.dynamic_update_slice(shard, norm_gains, (0, 960))
    packed = gather(shard)
    gains = packed.reshape(128, 80, 1024)[:, 0, 960:975].reshape(2, 960).astype(F32)
    gains = jnp.pad(gains, ((0, 0), (0, 64)))
    freq = np.power(rope_base, -np.arange(0, 64, 2) / 64).astype(np.float32)
    grads, out_t, grad_t = layer(
        packed, gains, tokens.T, out_grad.T, seq_ids.reshape(1, 256), jnp.asarray(np.repeat(freq[:, None], 128, 1))
    )
    weight_grad, last = scatter(grads)
    return (out_t.T, grad_t.T, weight_grad.T[None], last[0:1, 64:79])


def solution(mesh):
    return jax.shard_map(
        body,
        mesh=mesh,
        in_specs=(
            P(("fsdp", "dp"), None),
            P(None, None, ("fsdp", "dp")),
            P(None, ("fsdp", "dp")),
            P(("fsdp", "dp")),
            P(("fsdp", "dp"), None),
        ),
        out_specs=(
            P(("fsdp", "dp"), None),
            P(("fsdp", "dp"), None),
            P(None, None, ("fsdp", "dp")),
            P(None, ("fsdp", "dp")),
        ),
        check_vma=False,
    )
```

```python
import functools
import numpy as np
import jax
import jax.numpy as jnp
from jax import lax
from jax.experimental import pallas as pl
from jax.experimental.pallas import tpu as pltpu
from jax.sharding import PartitionSpec as P

epsilon = 1e-05
rope_base = 100000.0
MESH = pl.DeviceIdType.MESH
BF = jnp.bfloat16
LANES = ((0, 384), (384, 384), (768, 256))
ORDERS = ((0, 1, 2), (1, 2, 0), (2, 0, 1))


def place():
    f = lax.axis_index("fsdp")
    d = lax.axis_index("dp")
    return (f // 4, f % 4, d // 2), d % 2


def device_of(xyz, core):
    return (xyz[0] * 4 + xyz[1], xyz[2] * 2 + core)


def moved(xyz, axis, step):
    out = list(xyz)
    out[axis] = (out[axis] + step + 4) % 4
    return tuple(out)


def gather_into(xyz, core, shard, out, own_sem, send_sem, recv_sem, sib_send, sib_recv, between):
    waits = []

    def region(part, index):
        start, size = LANES[part]
        return out.at[index[0], index[1], index[2], core, :, pl.ds(start, size)]

    def remote(part, slot, src, index, to):
        copy = pltpu.make_async_remote_copy(
            src_ref=region(part, index) if src is None else src,
            dst_ref=region(part, index),
            send_sem=send_sem.at[part, slot],
            recv_sem=recv_sem.at[part, slot],
            device_id=to,
            device_id_type=MESH,
        )
        copy.start()
        waits.append(copy)
        return copy

    def sibling(part, slot, index):
        copy = pltpu.make_async_remote_copy(
            src_ref=region(part, index),
            dst_ref=region(part, index),
            send_sem=sib_send.at[part, slot],
            recv_sem=sib_recv.at[part, slot],
            device_id=device_of(xyz, 1 - core),
            device_id_type=MESH,
        )
        copy.start()
        sib.append(copy)

    sib = []
    own = []
    for part in range(3):
        start, size = LANES[part]
        c = pltpu.make_async_copy(shard.at[:, pl.ds(start, size)], region(part, xyz), own_sem.at[part])
        c.start()
        own.append(c)

    first = [None] * 3
    for part in range(3):
        a = ORDERS[part][0]
        start, size = LANES[part]
        src = shard.at[:, pl.ds(start, size)]
        plus = remote(part, 0, src, xyz, device_of(moved(xyz, a, 1), core))
        minus = remote(part, 1, src, xyz, device_of(moved(xyz, a, -1), core))
        first[part] = (plus, minus)
    second = [None] * 3
    for part in range(3):
        a = ORDERS[part][0]
        first[part][0].wait_recv()
        second[part] = remote(part, 2, None, moved(xyz, a, -1), device_of(moved(xyz, a, 1), core))
    for part in range(3):
        own[part].wait()

    def line(part, b_value, c_value, lo=None):
        a, b, c = ORDERS[part]
        index = [None] * 3
        index[a] = slice(None) if lo is None else pl.ds(lo, 2)
        index[b] = b_value
        index[c] = c_value
        return tuple(index)

    third = [[None] * 4 for _ in range(3)]
    hops = [None] * 3
    for part in range(3):
        a, b, c = ORDERS[part]
        first[part][1].wait_recv()
        second[part].wait_recv()
        mine = line(part, xyz[b], xyz[c])
        bp = remote(part, 3, None, mine, device_of(moved(xyz, b, 1), core))
        bm = remote(part, 4, None, mine, device_of(moved(xyz, b, -1), core))
        hops[part] = (bp, bm)
        cp = remote(part, 7, None, mine, device_of(moved(xyz, c, 1), core))
        cm = remote(part, 8, None, mine, device_of(moved(xyz, c, -1), core))
        third[part][0] = (cp, cm)
        sibling(part, 0, mine)
    halves = [None] * 3
    for part in range(3):
        a, b, c = ORDERS[part]
        hops[part][0].wait_recv()
        bv = moved(xyz, b, -1)[b]
        h0 = remote(part, 5, None, line(part, bv, xyz[c], 0), device_of(moved(xyz, b, 1), core))
        mine = line(part, bv, xyz[c])
        cp = remote(part, 9, None, mine, device_of(moved(xyz, c, 1), core))
        cm = remote(part, 10, None, mine, device_of(moved(xyz, c, -1), core))
        third[part][1] = (cp, cm)
        sibling(part, 1, mine)
        hops[part][1].wait_recv()
        bv = moved(xyz, b, 1)[b]
        h1 = remote(part, 6, None, line(part, bv, xyz[c], 2), device_of(moved(xyz, b, -1), core))
        mine = line(part, bv, xyz[c])
        cp = remote(part, 11, None, mine, device_of(moved(xyz, c, 1), core))
        cm = remote(part, 12, None, mine, device_of(moved(xyz, c, -1), core))
        third[part][2] = (cp, cm)
        sibling(part, 2, mine)
        halves[part] = (h0, h1)
    last = [[None] * 4 for _ in range(3)]

    def relative(part, rel):
        b = ORDERS[part][1]
        return moved(xyz, b, (0, -1, 1, 2)[rel])[b]

    def forward(part, rel):
        a, b, c = ORDERS[part]
        bv = relative(part, rel)
        third[part][rel][0].wait_recv()
        cv = moved(xyz, c, -1)[c]
        h0 = remote(part, 15 + 2 * rel, None, line(part, bv, cv, 0), device_of(moved(xyz, c, 1), core))
        sibling(part, 4 + rel, line(part, bv, cv))
        third[part][rel][1].wait_recv()
        cv = moved(xyz, c, 1)[c]
        h1 = remote(part, 16 + 2 * rel, None, line(part, bv, cv, 2), device_of(moved(xyz, c, -1), core))
        sibling(part, 8 + rel, line(part, bv, cv))
        last[part][rel] = (h0, h1)

    between()
    for part in range(3):
        forward(part, 0)
    for part in range(3):
        a, b, c = ORDERS[part]
        halves[part][0].wait_recv()
        halves[part][1].wait_recv()
        mine = line(part, relative(part, 3), xyz[c])
        cp = remote(part, 13, None, mine, device_of(moved(xyz, c, 1), core))
        cm = remote(part, 14, None, mine, device_of(moved(xyz, c, -1), core))
        third[part][3] = (cp, cm)
        sibling(part, 3, mine)
    for rel in (1, 2, 3):
        for part in range(3):
            forward(part, rel)
    for rel in range(4):
        for part in range(3):
            a, b, c = ORDERS[part]
            last[part][rel][0].wait_recv()
            last[part][rel][1].wait_recv()
            sibling(part, 12 + rel, line(part, relative(part, rel), moved(xyz, c, 2)[c]))
    for copy in sib:
        copy.wait()
    for copy in waits:
        copy.wait_send()


F32 = jnp.float32
SCALE = 64 ** (-0.5)


def nt(left, right):
    return lax.dot_general(left, right, (((1,), (1,)), ((), ())), preferred_element_type=F32)


def tn(left, right):
    return lax.dot_general(left, right, (((0,), (0,)), ((), ())), preferred_element_type=F32)


def nn(left, right):
    return jnp.dot(left, right, preferred_element_type=F32)


def turn(pair, cos, sin, direction):
    a, b = pair[0:32], pair[32:64]
    return jnp.concatenate([a * cos - direction * b * sin, b * cos + direction * a * sin], axis=0)


def real(values):
    lane = lax.broadcasted_iota(jnp.int32, values.shape, 1)
    return jnp.where(lane < 960, values, 0.0)


def prepare(xt, et, ids, freq, e, x32, cos3, sin3, mask3):
    zero = jnp.zeros((256, 64), F32)
    x32[:, 0:960] = xt[0:15].reshape(960, 256).astype(F32).T.astype(BF)
    x32[:, 960:1024] = zero.astype(BF)
    e[:, 0:960] = et[...].reshape(960, 256).astype(F32).T.astype(BF)
    e[:, 960:1024] = zero.astype(BF)
    across = jnp.broadcast_to(ids[...], (256, 256))
    same = across == across.T
    down = lax.broadcasted_iota(jnp.int32, (256, 256), 0)
    along = lax.broadcasted_iota(jnp.int32, (256, 256), 1)
    start = jnp.min(jnp.where(same, down, 256).astype(F32), axis=0, keepdims=True)
    row = lax.broadcasted_iota(jnp.int32, (1, 256), 1).astype(F32)
    angle = freq[...][:, 0:1] * (row - start)
    cos, sin = jnp.cos(angle), jnp.sin(angle)
    mask3[...] = jnp.where(same & (down <= along), 1.0, 0.0).astype(BF)
    cos3[...] = cos
    sin3[...] = sin


def wide(ref):
    return jnp.concatenate([ref[...]] * 3, axis=1)


def three(ref, k):
    return jnp.concatenate([ref[3 * k], ref[3 * k + 1], ref[3 * k + 2]], axis=1)


def attention(w, gains, x32, n1, r1, qt, kt, vt, p, ot, mid, n2, cos3, sin3, mask3):
    x = x32[...].astype(F32)
    inv = lax.rsqrt(jnp.sum(x * x, axis=1, keepdims=True) * (1.0 / 960) + epsilon)
    r1[:, 0:1] = inv
    n1[...] = (x * inv * gains[0:1, :]).astype(BF)

    def project(y, lo, hi):
        rows = w[0, y].reshape(640, 1024)[lo:hi]
        return nt(rows, n1[...])

    cos, sin = cos3[...], sin3[...]
    part = project(0, 0, 640)
    for h in range(10):
        qt[h] = turn(part[64 * h : 64 * h + 64], cos, sin, 1.0).astype(BF)
    part = project(1, 0, 640)
    for h in range(5):
        qt[10 + h] = turn(part[64 * h : 64 * h + 64], cos, sin, 1.0).astype(BF)
        kt[h] = turn(part[320 + 64 * h : 384 + 64 * h], cos, sin, 1.0).astype(BF)
    part = project(2, 0, 320)
    for h in range(5):
        vt[h] = part[64 * h : 64 * h + 64].astype(BF)

    def group(k, carry):
        q3 = three(qt, k)
        s = nn(kt[k].T, q3) * SCALE
        allowed = mask3[...].astype(F32) > 0.0
        s = jnp.concatenate([jnp.where(allowed, s[:, 256 * i : 256 * i + 256], -1e30) for i in range(3)], axis=1)
        s = jnp.exp(s - jnp.max(s, axis=0, keepdims=True))
        s = (s * (1.0 / jnp.sum(s, axis=0, keepdims=True))).astype(BF)
        p[k] = s
        o3 = nn(vt[k], s).astype(BF)
        for i in range(3):
            ot[3 * k + i] = o3[:, 256 * i : 256 * i + 256]
        return carry

    lax.fori_loop(0, 5, group, 0)
    o = ot[...].reshape(960, 256)
    m = x32[...].astype(F32) + tn(o[0:320], w[0, 2].reshape(640, 1024)[320:640])
    m = real(m + tn(o[320:960], w[0, 3].reshape(640, 1024)))
    mid[...] = m
    inv = lax.rsqrt(jnp.sum(m * m, axis=1, keepdims=True) * (1.0 / 960) + epsilon)
    r1[:, 1:2] = inv
    n2[...] = (m * inv * gains[1:2, :]).astype(BF)


def feed(w, y, n2, e, down, dn, store, hook):
    w1, w2, w3 = w[1, y].reshape(640, 1024), w[2, y].reshape(640, 1024), w[3, y].reshape(640, 1024)
    gate = nt(w1, n2[...])
    up = nt(w2, n2[...])
    sig = jax.nn.sigmoid(gate)
    hidden = (gate * sig * up).astype(BF)
    hook(1)
    store(3, y, nn(hidden, e[...]))
    down[...] += tn(hidden, w3)
    dh = nt(w3, e[...])
    d_gate = (dh * up * sig * (1.0 + gate * (1.0 - sig))).astype(BF)
    d_up = (dh * gate * sig).astype(BF)
    store(1, y, nn(d_gate, n2[...]))
    store(2, y, nn(d_up, n2[...]))
    hook(2)
    dn[...] += tn(d_gate, w1) + tn(d_up, w2)


def norm_back(d_norm, values, inv, gain):
    d_norm = real(d_norm)
    u = d_norm * gain
    d_gain = jnp.sum(d_norm * values * inv, axis=0, keepdims=True)
    mean = jnp.sum(u * values, axis=1, keepdims=True) * (1.0 / 960)
    return inv * u - values * (inv * inv * inv * mean), d_gain


def attention_back(w, gains, x32, n1, r1, qt, kt, vt, p, ot, mid, e, dn, dm, dmb, dot_, dqkv, cos3, sin3, dg, store_rows, dxt,
                   after_first, after_groups, after_rows, before):
    d, dg2 = norm_back(dn[...], mid[...], r1[:, 1:2], gains[1:2, :])
    d = d + e[...].astype(F32)
    dm[...] = d
    db = d.astype(BF)
    dmb[...] = db
    dg[1:2, :] = dg2
    d_o = nt(w[0, 2].reshape(640, 1024)[320:640], db).astype(BF)
    before()
    for h in range(5):
        dot_[h] = d_o[64 * h : 64 * h + 64]
    d_o = nt(w[0, 3].reshape(640, 1024), db).astype(BF)
    for h in range(10):
        dot_[5 + h] = d_o[64 * h : 64 * h + 64]
    o = ot[...].reshape(960, 256)
    store_rows(3, 0, nn(o[320:960], db))
    after_first()

    def group(k, carry):
        d3 = three(dot_, k)
        q3 = three(qt, k)
        pb = p[k]
        dp = nn(vt[k].T, d3)
        pf = pb.astype(F32)
        ds = pf * (dp - jnp.sum(pf * dp, axis=0, keepdims=True))
        ds = (ds * SCALE).astype(BF)
        dqkv[20 + k] = nt(d3, pb).astype(BF)
        dq = turn(nn(kt[k], ds), wide(cos3), wide(sin3), -1.0).astype(BF)
        for i in range(3):
            dqkv[3 * k + i] = dq[:, 256 * i : 256 * i + 256]
        dqkv[15 + k] = turn(nt(q3, ds), cos3[...], sin3[...], -1.0).astype(BF)
        return carry

    lax.fori_loop(0, 5, group, 0)
    after_groups()
    a = dqkv[0:10].reshape(640, 256)
    store_rows(0, 0, nn(a, n1[...]))
    total = tn(a, w[0, 0].reshape(640, 1024))
    a = dqkv[10:20].reshape(640, 256)
    store_rows(1, 0, nn(a, n1[...]))
    total = total + tn(a, w[0, 1].reshape(640, 1024))
    a = dqkv[20:25].reshape(320, 256)
    store_rows(2, 0, nn(a, n1[...]))
    store_rows(2, 320, nn(o[0:320], dmb[...]))
    total = total + tn(a, w[0, 2].reshape(640, 1024)[0:320])
    d, dg1 = norm_back(total, x32[...].astype(F32), r1[:, 0:1], gains[0:1, :])
    dg[0:1, :] = dg1
    after_rows()
    dxt[...] = (dm[...] + d)[:, 0:960].T


def gain_places():
    p = lax.broadcasted_iota(jnp.int32, (64, 1024), 1)
    owner = lax.broadcasted_iota(jnp.int32, (64, 1024), 0)
    mine = (p >= 15 * owner) & (p < 15 * owner + 15)
    pos = lax.broadcasted_iota(jnp.int32, (128, 1024), 1)
    lane = lax.broadcasted_iota(jnp.int32, (128, 1024), 0)
    base = ((pos.astype(F32) + 0.5) * (1.0 / 15)).astype(jnp.int32) * 15
    pick = jnp.where(pos - base + 64 == lane, 1.0, 0.0).astype(BF)
    return mine, pick


def collect_gains(w, table, gains):
    def step(i, carry):
        x, rest = i // 16, i % 16
        r = lax.broadcasted_iota(jnp.int32, (16, 128), 0)
        for c in range(2):
            block = w[x, rest // 4, rest % 4, c, 0:16, 896:1024].astype(F32)
            table[pl.ds(i * 2 + c, 1), :] = jnp.sum(jnp.where(r == 0, block, 0.0), axis=0, keepdims=True)
        return carry

    lax.fori_loop(0, 64, step, 0)
    mine, pick = gain_places()
    for half in range(2):
        rows = nn(table[64 * half : 64 * half + 64, :].astype(BF), pick)
        gains[half : half + 1, :] = jnp.sum(jnp.where(mine, rows, 0.0), axis=0, keepdims=True)


def spread_gains(dg, tails):
    mine, pick = gain_places()
    for half in range(2):
        rows = jnp.where(mine, dg[half : half + 1, :], 0.0).astype(BF)
        tails[64 * half : 64 * half + 64, :] = nt(rows, pick)


def mega_kernel(shard, xt, et, ids, freq, yt, dxt, out, gain_out,
                w, acc, stage, xp1, xm1, yp1, ym1, xpb, xmb, ypb, ymb, n1, n2, e, x32, mid, down, dn, qt, kt, vt, p, ot, dqkv,
                r1, cos3, sin3, mask3, dg, tails, gains,
                own_sem, send_sem, recv_sem, sib_send, sib_recv, ring_send, ring_recv, core_send, core_recv, load_sem, free_sem):
    xyz, core = place()
    barrier = pltpu.get_barrier_semaphore()
    near = [device_of(moved(xyz, axis, step), core) for axis in range(3) for step in (1, -1)]
    near.append(device_of(moved(xyz, 0, 2), core))
    for other in near + [device_of(xyz, 1 - core)]:
        pl.semaphore_signal(barrier, inc=1, device_id=other, device_id_type=MESH)
    loads = [pltpu.make_async_copy(xt, dqkv.at[pl.ds(0, 15)], load_sem.at[0]), pltpu.make_async_copy(et, ot, load_sem.at[1])]
    for copy in loads:
        copy.start()
    pl.semaphore_wait(barrier, 8)

    def begin():
        for copy in loads:
            copy.wait()
        prepare(dqkv, ot, ids, freq, e, x32, cos3, sin3, mask3)

    gather_into(xyz, core, shard, w, own_sem, send_sem, recv_sem, sib_send, sib_recv, begin)
    collect_gains(w, tails, gains)
    attention(w, gains, x32, n1, r1, qt, kt, vt, p, ot, mid, n2, cos3, sin3, mask3)
    down[...] = jnp.zeros_like(down)
    dn[...] = jnp.zeros_like(dn)

    x, y, z = xyz
    late = w.at[3]
    pads = w.at[2]

    def to_sibling(j):
        if j < 4:
            src, dst = stage.at[1 + j % 2], acc.at[pl.ds(1, 3), (y + (2, 1, 3, 0)[j]) % 4]
        else:
            src, dst = w.at[1, :, :, 1], acc.at[0]
        return pltpu.make_async_remote_copy(src_ref=src, dst_ref=dst, send_sem=core_send.at[j], recv_sem=core_recv.at[j],
                                            device_id=device_of(xyz, 1 - core), device_id_type=MESH)

    def merge(j):
        to_sibling(j).wait_recv()
        if j < 4:
            yj = (y + (2, 1, 3, 0)[j]) % 4

            def step(i, carry):
                at = (1 + i // 4, yj, i % 4)
                acc[at] = (acc[at].astype(F32) + stage[0, i // 4, i % 4].astype(F32)).astype(BF)
                return carry

            lax.fori_loop(0, 12, step, 0)
        else:

            def step(i, carry):
                at = (0, i // 4, i % 4)
                acc[at] = (acc[at].astype(F32) + w[1, i // 4, i % 4, 0].astype(F32)).astype(BF)
                return carry

            lax.fori_loop(0, 16, step, 0)

    class Ring:
        def __init__(self, number, axis, lane, count, where, ref, bufs, item, half=256):
            self.half = half
            self.number, self.axis, self.lane, self.count = number, axis, lane, count
            self.where, self.ref, self.bufs, self.item = where, ref, bufs, item

        def copy(self, kind):
            h = self.half
            group, step, lo, size = ((2, 1, 0, h), (2, -1, h, h), (1, 1, 0, 2 * h), (-1, -1, 0, 2 * h))[kind]
            at = moved(xyz, self.axis, group)[self.axis]
            return pltpu.make_async_remote_copy(
                src_ref=self.ref(at, pl.ds(self.lane + lo, size)), dst_ref=self.bufs[kind],
                send_sem=ring_send.at[self.number, kind], recv_sem=ring_recv.at[self.number, kind],
                device_id=device_of(moved(xyz, self.axis, step), core), device_id_type=MESH)

        def fold(self, group, lo, size, kinds):
            for kind in kinds:
                self.copy(kind).wait_recv()
            at = moved(xyz, self.axis, group)[self.axis]

            def step(i, carry):
                spot = self.where(at, i) + (slice(None), pl.ds(self.lane + lo, size))
                total = acc[spot].astype(F32)
                for kind in kinds:
                    total = total + self.item(self.bufs[kind], i).astype(F32)
                acc[spot] = total.astype(BF)
                return carry

            if self.count == 1:
                step(0, 0)
            else:
                lax.fori_loop(0, self.count, step, 0)

        def begin(self):
            self.copy(0).start()
            self.copy(1).start()

        def plus(self):
            self.fold(1, 0, self.half, (0,))
            self.copy(2).start()

        def minus(self):
            self.fold(-1, self.half, self.half, (1,))
            self.copy(3).start()

        def middle(self):
            self.plus()
            self.minus()

        def end(self):
            self.fold(0, 0, 2 * self.half, (2, 3))

    mlp = pl.ds(1, 3)
    flat = lambda buf, i: buf[i]
    whole = lambda buf, i: buf[...]
    a1 = Ring(0, 1, 0, 12, lambda at, i: (1 + i // 4, at, i % 4), lambda at, l: acc.at[mlp, at, :, :, l],
              (xp1, xm1, yp1, ym1), lambda buf, i: buf[i // 4, i % 4])
    def slots(base, lead):
        return (base.at[lead + (0, slice(None), pl.ds(0, 256))], base.at[lead + (0, slice(None), pl.ds(256, 256))],
                base.at[lead + (1, slice(None), pl.ds(0, 512))], base.at[lead + (1, slice(None), pl.ds(512, 512))])

    b1 = []
    for j in range(4):
        yj = (y + (2, 1, 3, 0)[j]) % 4
        bufs = slots(pads, ((pl.ds(0, 3), 3), (1, pl.ds(0, 3)))[j - 2]) if j > 1 else (xpb.at[j], xmb.at[j], ypb.at[j], ymb.at[j])
        b1.append(Ring(1 + j, 2, 512, 3, lambda at, i, yj=yj: (1 + i, yj, at), lambda at, l, yj=yj: acc.at[mlp, yj, at, :, l], bufs, flat))

    a2 = Ring(5, 2, 0, 3, lambda at, i: (1 + i, y, at), lambda at, l: acc.at[mlp, y, at, :, l], slots(late, (3, pl.ds(0, 3))), flat)
    b2 = Ring(6, 1, 512, 3, lambda at, i: (1 + i, at, z), lambda at, l: acc.at[mlp, at, z, :, l], slots(pads, (0, pl.ds(0, 3))), flat)
    c1 = Ring(7, 1, 0, 4, lambda at, i: (0, at, i), lambda at, l: acc.at[0, at, :, :, l], slots(late, (0, slice(None))), flat)
    d1 = Ring(8, 2, 512, 4, lambda at, i: (0, i, at), lambda at, l: acc.at[0, :, at, :, l], slots(late, (1, slice(None))), flat)
    c2 = Ring(9, 2, 0, 1, lambda at, i: (0, y, at), lambda at, l: acc.at[0, y, at, :, l], slots(late, (2, 0)), whole)
    d2 = Ring(10, 1, 512, 1, lambda at, i: (0, at, z), lambda at, l: acc.at[0, at, z, :, l], slots(late, (2, 1)), whole)

    def chunk(j, carry):
        yj = (y + jnp.where(j == 0, 2, jnp.where(j == 1, 1, jnp.where(j == 2, 3, 0)))) % 4

        @pl.when(j == 2)
        def _():
            to_sibling(0).wait_send()

        @pl.when(j == 3)
        def _():
            to_sibling(1).wait_send()

        def store(cls, _, value):
            value = value.astype(BF).reshape(4, 2, 80, 1024)
            stage[core * (1 + j % 2), cls - 1] = value[:, 0]
            stage[(1 - core) * (1 + j % 2), cls - 1] = value[:, 1]

        def hook(n):
            if n == 1:

                @pl.when(j == 1)
                def _():
                    merge(0)
                    a1.begin()
                    b1[0].begin()

                @pl.when(j == 2)
                def _():
                    merge(1)
                    b1[1].begin()

                @pl.when(j == 3)
                def _():
                    merge(2)

            else:

                @pl.when(j == 2)
                def _():
                    b1[0].middle()

                @pl.when(j == 3)
                def _():
                    a1.plus()
                    a1.minus()
                    b1[1].middle()

        feed(w, yj, n2, e, down, dn, store, hook)
        for k in range(4):
            pl.when(j == k)(to_sibling(k).start)
        return carry

    lax.fori_loop(0, 4, chunk, 0)
    for other in near:
        pl.semaphore_signal(free_sem, inc=1, device_id=other, device_id_type=MESH)

    def after_first():
        merge(3)
        pl.semaphore_wait(free_sem, 7)
        b1[2].begin()
        b1[3].begin()
        b1[0].end()

    def after_groups():
        b1[2].middle()
        b1[3].middle()
        b1[1].end()

    def after_rows():
        spread_late()
        to_sibling(4).start()

    dqkv[0:15] = (mid[...] + down[...])[:, 0:960].T.astype(BF).reshape(15, 64, 256)
    away = pltpu.make_async_copy(dqkv.at[pl.ds(0, 15)], yt, load_sem.at[2])
    away.start()

    def store_rows(yy, at, value):
        rows = value.shape[0]
        value = value.astype(BF).reshape(rows // 160, 2, 80, 1024)
        lo = at // 160
        w[1, yy, lo : lo + rows // 160, core] = value[:, 0]
        w[1, yy, lo : lo + rows // 160, 1 - core] = value[:, 1]

    def place_tail(i, carry):
        yy, zz = i // 4, i % 4
        r = lax.broadcasted_iota(jnp.int32, (16, 128), 0)
        l = lax.broadcasted_iota(jnp.int32, (16, 128), 1)
        for c in range(2):
            side = c * (1 - core) + (1 - c) * core
            new = w[1, yy, zz, side, 0:16, 896:1024].astype(F32)
            for xx in range(4):
                row = tails[pl.ds(xx * 32 + i * 2 + c, 1), :]
                new = jnp.where((r == xx) & (l >= 64), row, new)
            w[1, yy, zz, side, 0:16, 896:1024] = new.astype(BF)
        return carry

    def spread_late():
        spread_gains(dg, tails)
        lax.fori_loop(0, 16, place_tail, 0)

    attention_back(w, gains, x32, n1, r1, qt, kt, vt, p, ot, mid, e, dn, down, n2, dqkv, dqkv, cos3, sin3, dg, store_rows, dxt,
                   after_first, after_groups, after_rows, away.wait)
    b1[2].end()
    merge(4)
    c1.begin()
    d1.begin()
    b1[3].end()
    b2.begin()
    a1.end()
    a2.begin()
    d1.middle()
    c1.middle()
    b2.middle()
    a2.middle()
    d1.end()
    d2.begin()
    c1.end()
    c2.begin()
    a2.end()
    b2.end()
    d2.middle()
    c2.middle()
    d2.end()
    c2.end()
    room = pads.at[2, :, 1]
    e1 = Ring(11, 0, 0, 1, lambda at, i: (at, y, z), lambda at, l: acc.at[at, y, z, :, l],
              (room.at[0, :, pl.ds(0, 512)], room.at[0, :, pl.ds(512, 512)], room.at[1], room.at[2]), whole, 512)

    def tile(k):
        return pltpu.make_async_remote_copy(
            src_ref=acc.at[0, y, z, pl.ds(0, 16), pl.ds(896, 128)], dst_ref=pads.at[3, k, 1, pl.ds(0, 16), pl.ds(896, 128)],
            send_sem=ring_send.at[12, k], recv_sem=ring_recv.at[12, k],
            device_id=device_of(moved(xyz, 0, (1, -1, 2)[k]), core), device_id_type=MESH)

    e1.begin()
    for k in range(3):
        tile(k).start()
    total = acc[0, y, z, 0:16, 896:1024].astype(F32)
    for k in range(3):
        tile(k).wait_recv()
        total = total + pads[3, k, 1, 0:16, 896:1024].astype(F32)
    r = lax.broadcasted_iota(jnp.int32, (16, 128), 0)
    gain_out[...] = jnp.sum(jnp.where(r == x, total, 0.0), axis=0, keepdims=True)
    for k in range(3):
        tile(k).wait_send()
    e1.middle()
    e1.copy(2).wait_recv()
    e1.copy(3).wait_recv()
    out[...] = (acc[xyz].astype(F32) + pads[2, 1, 1].astype(F32) + pads[2, 2, 1].astype(F32))[:, 0:960]
    for j in (2, 3, 4):
        to_sibling(j).wait_send()
    for ring in [a1, a2, b2, c1, d1, c2, d2, e1] + b1:
        for kind in range(4):
            ring.copy(kind).wait_send()


def mega(shard, tokens_t, grad_t, ids, freq):
    vm = pl.BlockSpec(memory_space=pltpu.VMEM)
    far = pl.BlockSpec(memory_space=pl.ANY)
    slot = lambda *lead: pltpu.VMEM(lead + (80, 256), BF)
    slot2 = lambda *lead: pltpu.VMEM(lead + (80, 512), BF)
    return pl.pallas_call(
        mega_kernel,
        out_shape=(
            jax.ShapeDtypeStruct((15, 64, 256), BF),
            jax.ShapeDtypeStruct((960, 256), F32),
            jax.ShapeDtypeStruct((80, 960), F32),
            jax.ShapeDtypeStruct((1, 128), F32),
        ),
        in_specs=[vm, far, far, vm, vm],
        out_specs=(far, vm, vm, vm),
        scratch_shapes=[
            pltpu.VMEM((4, 4, 4, 2, 80, 1024), BF),
            pltpu.VMEM((4, 4, 4, 80, 1024), BF),
            pltpu.VMEM((3, 3, 4, 80, 1024), BF),
            slot(3, 4), slot(3, 4), slot2(3, 4), slot2(3, 4),
            slot(2, 3), slot(2, 3), slot2(2, 3), slot2(2, 3),
            pltpu.VMEM((256, 1024), BF),
            pltpu.VMEM((256, 1024), BF),
            pltpu.VMEM((256, 1024), BF),
            pltpu.VMEM((256, 1024), BF),
            pltpu.VMEM((256, 1024), F32),
            pltpu.VMEM((256, 1024), F32),
            pltpu.VMEM((256, 1024), F32),
            pltpu.VMEM((15, 64, 256), BF),
            pltpu.VMEM((5, 64, 256), BF),
            pltpu.VMEM((5, 64, 256), BF),
            pltpu.VMEM((5, 256, 768), BF),
            pltpu.VMEM((15, 64, 256), BF),
            pltpu.VMEM((25, 64, 256), BF),
            pltpu.VMEM((256, 2), F32),
            pltpu.VMEM((32, 256), F32),
            pltpu.VMEM((32, 256), F32),
            pltpu.VMEM((256, 256), BF),
            pltpu.VMEM((2, 1024), F32),
            pltpu.VMEM((128, 128), F32),
            pltpu.VMEM((2, 1024), F32),
            pltpu.SemaphoreType.DMA((3,)),
            pltpu.SemaphoreType.DMA((3, 23)),
            pltpu.SemaphoreType.DMA((3, 23)),
            pltpu.SemaphoreType.DMA((3, 16)),
            pltpu.SemaphoreType.DMA((3, 16)),
            pltpu.SemaphoreType.DMA((13, 4)),
            pltpu.SemaphoreType.DMA((13, 4)),
            pltpu.SemaphoreType.DMA((5,)),
            pltpu.SemaphoreType.DMA((5,)),
            pltpu.SemaphoreType.DMA((3,)),
            pltpu.SemaphoreType.REGULAR,
        ],
        compiler_params=pltpu.CompilerParams(collective_id=0, has_side_effects=True, vmem_limit_bytes=66900000),
    )(shard, tokens_t.reshape(15, 64, 256), grad_t.reshape(15, 64, 256), ids, freq)


def body(tokens, layer_weights, norm_gains, seq_ids, out_grad):
    shard = jnp.pad(layer_weights[0].T, ((0, 0), (0, 64)))
    shard = lax.dynamic_update_slice(shard, norm_gains, (0, 960))
    freq = np.power(rope_base, -np.arange(0, 64, 2) / 64).astype(np.float32)
    out_t, grad_t, weight_grad, last = mega(
        shard, tokens.T, out_grad.T, seq_ids.reshape(1, 256), jnp.asarray(np.repeat(freq[:, None], 128, 1))
    )
    return (out_t.reshape(960, 256).T, grad_t.T, weight_grad.T[None], last[:, 64:79])


def solution(mesh):
    return jax.shard_map(
        body,
        mesh=mesh,
        in_specs=(
            P(("fsdp", "dp"), None),
            P(None, None, ("fsdp", "dp")),
            P(None, ("fsdp", "dp")),
            P(("fsdp", "dp")),
            P(("fsdp", "dp"), None),
        ),
        out_specs=(
            P(("fsdp", "dp"), None),
            P(("fsdp", "dp"), None),
            P(None, None, ("fsdp", "dp")),
            P(None, ("fsdp", "dp")),
        ),
        check_vma=False,
    )
```

```python
import functools
import numpy as np
import jax
import jax.numpy as jnp
from jax import lax
from jax.experimental import pallas as pl
from jax.experimental.pallas import tpu as pltpu
from jax.sharding import PartitionSpec as P

epsilon = 1e-05
rope_base = 100000.0
MESH = pl.DeviceIdType.MESH
BF = jnp.bfloat16
PIECES = ((0, 72, 0, 384), (0, 72, 384, 384), (0, 80, 768, 256), (72, 8, 0, 768))
ORDERS = ((0, 1, 2), (1, 2, 0), (2, 0, 1), (2, 0, 1))


def place():
    f = lax.axis_index("fsdp")
    d = lax.axis_index("dp")
    return (f // 4, f % 4, d // 2), d % 2


def device_of(xyz, core):
    return (xyz[0] * 4 + xyz[1], xyz[2] * 2 + core)


def moved(xyz, axis, step):
    out = list(xyz)
    out[axis] = (out[axis] + step + 4) % 4
    return tuple(out)


def gather_into(xyz, core, out, send_sem, recv_sem, sib_send, sib_recv, between):
    waits = []

    def region(part, index):
        top, rows, start, size = PIECES[part]
        return out.at[index[0], index[1], index[2], core, pl.ds(top, rows), pl.ds(start, size)]

    def remote(part, slot, src, index, to):
        copy = pltpu.make_async_remote_copy(
            src_ref=region(part, index) if src is None else src,
            dst_ref=region(part, index),
            send_sem=send_sem.at[part, slot],
            recv_sem=recv_sem.at[part, slot],
            device_id=to,
            device_id_type=MESH,
        )
        copy.start()
        waits.append(copy)
        return copy

    def sibling(part, slot, index):
        copy = pltpu.make_async_remote_copy(
            src_ref=region(part, index),
            dst_ref=region(part, index),
            send_sem=sib_send.at[part, slot],
            recv_sem=sib_recv.at[part, slot],
            device_id=device_of(xyz, 1 - core),
            device_id_type=MESH,
        )
        copy.start()
        sib.append(copy)

    sib = []
    first = [None] * 4
    for part in range(4):
        a = ORDERS[part][0]
        plus = remote(part, 0, None, xyz, device_of(moved(xyz, a, 1), core))
        minus = remote(part, 1, None, xyz, device_of(moved(xyz, a, -1), core))
        first[part] = (plus, minus)
    second = [None] * 4
    for part in range(4):
        a = ORDERS[part][0]
        first[part][0].wait_recv()
        second[part] = remote(part, 2, None, moved(xyz, a, -1), device_of(moved(xyz, a, 1), core))

    def line(part, b_value, c_value, lo=None):
        a, b, c = ORDERS[part]
        index = [None] * 3
        index[a] = slice(None) if lo is None else pl.ds(lo, 2)
        index[b] = b_value
        index[c] = c_value
        return tuple(index)

    third = [[None] * 4 for _ in range(4)]
    hops = [None] * 4
    for part in range(4):
        a, b, c = ORDERS[part]
        first[part][1].wait_recv()
        second[part].wait_recv()
        mine = line(part, xyz[b], xyz[c])
        bp = remote(part, 3, None, mine, device_of(moved(xyz, b, 1), core))
        bm = remote(part, 4, None, mine, device_of(moved(xyz, b, -1), core))
        hops[part] = (bp, bm)
        cp = remote(part, 7, None, mine, device_of(moved(xyz, c, 1), core))
        cm = remote(part, 8, None, mine, device_of(moved(xyz, c, -1), core))
        third[part][0] = (cp, cm)
        sibling(part, 0, mine)
    halves = [None] * 4
    for part in range(4):
        a, b, c = ORDERS[part]
        hops[part][0].wait_recv()
        bv = moved(xyz, b, -1)[b]
        h0 = remote(part, 5, None, line(part, bv, xyz[c], 0), device_of(moved(xyz, b, 1), core))
        mine = line(part, bv, xyz[c])
        cp = remote(part, 9, None, mine, device_of(moved(xyz, c, 1), core))
        cm = remote(part, 10, None, mine, device_of(moved(xyz, c, -1), core))
        third[part][1] = (cp, cm)
        sibling(part, 1, mine)
        hops[part][1].wait_recv()
        bv = moved(xyz, b, 1)[b]
        h1 = remote(part, 6, None, line(part, bv, xyz[c], 2), device_of(moved(xyz, b, -1), core))
        mine = line(part, bv, xyz[c])
        cp = remote(part, 11, None, mine, device_of(moved(xyz, c, 1), core))
        cm = remote(part, 12, None, mine, device_of(moved(xyz, c, -1), core))
        third[part][2] = (cp, cm)
        sibling(part, 2, mine)
        halves[part] = (h0, h1)
    last = [[None] * 4 for _ in range(4)]

    def relative(part, rel):
        b = ORDERS[part][1]
        return moved(xyz, b, (0, -1, 1, 2)[rel])[b]

    def forward(part, rel):
        a, b, c = ORDERS[part]
        bv = relative(part, rel)
        third[part][rel][0].wait_recv()
        cv = moved(xyz, c, -1)[c]
        h0 = remote(part, 15 + 2 * rel, None, line(part, bv, cv, 0), device_of(moved(xyz, c, 1), core))
        sibling(part, 4 + rel, line(part, bv, cv))
        third[part][rel][1].wait_recv()
        cv = moved(xyz, c, 1)[c]
        h1 = remote(part, 16 + 2 * rel, None, line(part, bv, cv, 2), device_of(moved(xyz, c, -1), core))
        sibling(part, 8 + rel, line(part, bv, cv))
        last[part][rel] = (h0, h1)

    between()
    for part in range(4):
        forward(part, 0)
    for part in range(4):
        a, b, c = ORDERS[part]
        halves[part][0].wait_recv()
        halves[part][1].wait_recv()
        mine = line(part, relative(part, 3), xyz[c])
        cp = remote(part, 13, None, mine, device_of(moved(xyz, c, 1), core))
        cm = remote(part, 14, None, mine, device_of(moved(xyz, c, -1), core))
        third[part][3] = (cp, cm)
        sibling(part, 3, mine)
    for rel in (1, 2, 3):
        for part in range(4):
            forward(part, rel)
    for rel in range(4):
        for part in range(4):
            a, b, c = ORDERS[part]
            last[part][rel][0].wait_recv()
            last[part][rel][1].wait_recv()
            sibling(part, 12 + rel, line(part, relative(part, rel), moved(xyz, c, 2)[c]))
    for copy in sib:
        copy.wait()
    for copy in waits:
        copy.wait_send()


F32 = jnp.float32
SCALE = 64 ** (-0.5)


def nt(left, right):
    return lax.dot_general(left, right, (((1,), (1,)), ((), ())), preferred_element_type=F32)


def tn(left, right):
    return lax.dot_general(left, right, (((0,), (0,)), ((), ())), preferred_element_type=F32)


def nn(left, right):
    return jnp.dot(left, right, preferred_element_type=F32)


def turn(pair, cos, sin, direction):
    a, b = pair[0:32], pair[32:64]
    return jnp.concatenate([a * cos - direction * b * sin, b * cos + direction * a * sin], axis=0)


def real(values):
    lane = lax.broadcasted_iota(jnp.int32, values.shape, 1)
    return jnp.where(lane < 960, values, 0.0)


def prepare(xt, et, ids, freq, e, x32, cos3, sin3, mask3):
    zero = jnp.zeros((256, 64), F32)
    x32[:, 0:960] = xt[0:15].reshape(960, 256).astype(F32).T.astype(BF)
    x32[:, 960:1024] = zero.astype(BF)
    e[:, 0:960] = et[...].reshape(960, 256).astype(F32).T.astype(BF)
    e[:, 960:1024] = zero.astype(BF)
    across = jnp.broadcast_to(ids[...], (256, 256))
    same = across == across.T
    down = lax.broadcasted_iota(jnp.int32, (256, 256), 0)
    along = lax.broadcasted_iota(jnp.int32, (256, 256), 1)
    start = jnp.min(jnp.where(same, down, 256).astype(F32), axis=0, keepdims=True)
    row = lax.broadcasted_iota(jnp.int32, (1, 256), 1).astype(F32)
    angle = freq[...][:, 0:1] * (row - start)
    cos, sin = jnp.cos(angle), jnp.sin(angle)
    mask3[...] = jnp.where(same & (down <= along), 1.0, 0.0).astype(BF)
    cos3[...] = cos
    sin3[...] = sin


def wide(ref):
    return jnp.concatenate([ref[...]] * 3, axis=1)


def three(ref, k):
    return jnp.concatenate([ref[3 * k], ref[3 * k + 1], ref[3 * k + 2]], axis=1)


def attention(w, gains, x32, n1, r1, qt, kt, vt, p, ot, mid, n2, cos3, sin3, mask3):
    x = x32[...].astype(F32)
    inv = lax.rsqrt(jnp.sum(x * x, axis=1, keepdims=True) * (1.0 / 960) + epsilon)
    r1[:, 0:1] = inv
    n1[...] = (x * inv * gains[0:1, :]).astype(BF)

    def project(y, lo, hi):
        rows = w[0, y].reshape(640, 1024)[lo:hi]
        return nt(rows, n1[...])

    cos, sin = cos3[...], sin3[...]
    part = project(0, 0, 640)
    for h in range(10):
        qt[h] = turn(part[64 * h : 64 * h + 64], cos, sin, 1.0).astype(BF)
    part = project(1, 0, 640)
    for h in range(5):
        qt[10 + h] = turn(part[64 * h : 64 * h + 64], cos, sin, 1.0).astype(BF)
        kt[h] = turn(part[320 + 64 * h : 384 + 64 * h], cos, sin, 1.0).astype(BF)
    part = project(2, 0, 320)
    for h in range(5):
        vt[h] = part[64 * h : 64 * h + 64].astype(BF)

    def group(k, carry):
        q3 = three(qt, k)
        s = nn(kt[k].T, q3) * SCALE
        allowed = mask3[...].astype(F32) > 0.0
        s = jnp.concatenate([jnp.where(allowed, s[:, 256 * i : 256 * i + 256], -1e30) for i in range(3)], axis=1)
        s = jnp.exp(s - jnp.max(s, axis=0, keepdims=True))
        s = (s * (1.0 / jnp.sum(s, axis=0, keepdims=True))).astype(BF)
        p[k] = s
        o3 = nn(vt[k], s).astype(BF)
        for i in range(3):
            ot[3 * k + i] = o3[:, 256 * i : 256 * i + 256]
        return carry

    lax.fori_loop(0, 5, group, 0)
    o = ot[...].reshape(960, 256)
    m = x32[...].astype(F32) + tn(o[0:320], w[0, 2].reshape(640, 1024)[320:640])
    m = real(m + tn(o[320:960], w[0, 3].reshape(640, 1024)))
    mid[...] = m
    inv = lax.rsqrt(jnp.sum(m * m, axis=1, keepdims=True) * (1.0 / 960) + epsilon)
    r1[:, 1:2] = inv
    n2[...] = (m * inv * gains[1:2, :]).astype(BF)


def feed(w, y, n2, e, down, dn, store, hook):
    w1, w2, w3 = w[1, y].reshape(640, 1024), w[2, y].reshape(640, 1024), w[3, y].reshape(640, 1024)
    gate = nt(w1, n2[...])
    up = nt(w2, n2[...])
    sig = jax.nn.sigmoid(gate)
    hidden = (gate * sig * up).astype(BF)
    down[...] += tn(hidden, w3)
    dh = nt(w3, e[...])
    d_gate = (dh * up * sig * (1.0 + gate * (1.0 - sig))).astype(BF)
    d_up = (dh * gate * sig).astype(BF)
    dn[...] += tn(d_gate, w1) + tn(d_up, w2)
    hook(2)
    store(3, y, nn(hidden, e[...]))
    store(1, y, nn(d_gate, n2[...]))
    store(2, y, nn(d_up, n2[...]))


def norm_back(d_norm, values, inv, gain):
    d_norm = real(d_norm)
    u = d_norm * gain
    d_gain = jnp.sum(d_norm * values * inv, axis=0, keepdims=True)
    mean = jnp.sum(u * values, axis=1, keepdims=True) * (1.0 / 960)
    return inv * u - values * (inv * inv * inv * mean), d_gain


def attention_back(w, gains, x32, n1, r1, qt, kt, vt, p, ot, mid, e, dn, dm, dmb, dot_, dqkv, cos3, sin3, dg, store_rows, dxt,
                   after_first, after_groups, after_rows, before):
    d, dg2 = norm_back(dn[...], mid[...], r1[:, 1:2], gains[1:2, :])
    d = d + e[...].astype(F32)
    dm[...] = d
    db = d.astype(BF)
    dmb[...] = db
    dg[1:2, :] = dg2
    d_o = nt(w[0, 2].reshape(640, 1024)[320:640], db).astype(BF)
    before()
    for h in range(5):
        dot_[h] = d_o[64 * h : 64 * h + 64]
    d_o = nt(w[0, 3].reshape(640, 1024), db).astype(BF)
    for h in range(10):
        dot_[5 + h] = d_o[64 * h : 64 * h + 64]
    o = ot[...].reshape(960, 256)
    store_rows(3, 0, nn(o[320:960], db))
    after_first()

    def group(k, carry):
        d3 = three(dot_, k)
        q3 = three(qt, k)
        pb = p[k]
        dp = nn(vt[k].T, d3)
        pf = pb.astype(F32)
        ds = pf * (dp - jnp.sum(pf * dp, axis=0, keepdims=True))
        ds = (ds * SCALE).astype(BF)
        dqkv[20 + k] = nt(d3, pb).astype(BF)
        dq = turn(nn(kt[k], ds), wide(cos3), wide(sin3), -1.0).astype(BF)
        for i in range(3):
            dqkv[3 * k + i] = dq[:, 256 * i : 256 * i + 256]
        dqkv[15 + k] = turn(nt(q3, ds), cos3[...], sin3[...], -1.0).astype(BF)
        return carry

    lax.fori_loop(0, 5, group, 0)
    after_groups()
    a = dqkv[0:10].reshape(640, 256)
    total = tn(a, w[0, 0].reshape(640, 1024))
    store_rows(0, 0, nn(a, n1[...]))
    a = dqkv[10:20].reshape(640, 256)
    total = total + tn(a, w[0, 1].reshape(640, 1024))
    store_rows(1, 0, nn(a, n1[...]))
    a = dqkv[20:25].reshape(320, 256)
    total = total + tn(a, w[0, 2].reshape(640, 1024)[0:320])
    store_rows(2, 0, nn(a, n1[...]))
    store_rows(2, 320, nn(o[0:320], dmb[...]))
    d, dg1 = norm_back(total, x32[...].astype(F32), r1[:, 0:1], gains[0:1, :])
    dg[0:1, :] = dg1
    after_rows()
    dxt[...] = (dm[...] + d)[:, 0:960].T


def gain_places():
    p = lax.broadcasted_iota(jnp.int32, (64, 1024), 1)
    owner = lax.broadcasted_iota(jnp.int32, (64, 1024), 0)
    mine = (p >= 15 * owner) & (p < 15 * owner + 15)
    pos = lax.broadcasted_iota(jnp.int32, (128, 1024), 1)
    lane = lax.broadcasted_iota(jnp.int32, (128, 1024), 0)
    base = ((pos.astype(F32) + 0.5) * (1.0 / 15)).astype(jnp.int32) * 15
    pick = jnp.where(pos - base + 64 == lane, 1.0, 0.0).astype(BF)
    return mine, pick


def collect_gains(w, table, gains):
    def step(i, carry):
        x, rest = i // 16, i % 16
        r = lax.broadcasted_iota(jnp.int32, (16, 128), 0)
        for c in range(2):
            block = w[x, rest // 4, rest % 4, c, 0:16, 896:1024].astype(F32)
            table[pl.ds(i * 2 + c, 1), :] = jnp.sum(jnp.where(r == 0, block, 0.0), axis=0, keepdims=True)
        return carry

    lax.fori_loop(0, 64, step, 0)
    mine, pick = gain_places()
    for half in range(2):
        rows = nn(table[64 * half : 64 * half + 64, :].astype(BF), pick)
        gains[half : half + 1, :] = jnp.sum(jnp.where(mine, rows, 0.0), axis=0, keepdims=True)


def spread_gains(dg, tails):
    mine, pick = gain_places()
    for half in range(2):
        rows = jnp.where(mine, dg[half : half + 1, :], 0.0).astype(BF)
        tails[64 * half : 64 * half + 64, :] = nt(rows, pick)


def mega_kernel(wt, own_gains, xt, et, ids, freq, yt, dxt, out, gain_out,
                w, acc, xp1, xm1, yp1, ym1, xpb, xmb, ypb, ymb, xps, xms, yps, yms, xpc, xmc, ypc, ymc, xpd, xmd, ypd, ymd, room, tiles, n1, n2, e, x32, mid, down, dn, qt, kt, vt, p, ot, dqkv,
                r1, cos3, sin3, mask3, dg, tails, gains,
                send_sem, recv_sem, sib_send, sib_recv, ring_send, ring_recv, core_send, core_recv, load_sem):
    xyz, core = place()
    barrier = pltpu.get_barrier_semaphore()
    near = [device_of(moved(xyz, axis, step), core) for axis in range(3) for step in (1, -1)]
    near.append(device_of(moved(xyz, 0, 2), core))
    for other in near + [device_of(xyz, 1 - core)]:
        pl.semaphore_signal(barrier, inc=1, device_id=other, device_id_type=MESH)
    loads = [pltpu.make_async_copy(xt, dqkv.at[pl.ds(0, 15)], load_sem.at[0]), pltpu.make_async_copy(et, ot, load_sem.at[1])]
    for copy in loads:
        copy.start()
    mine = xyz + (core,)
    w[mine + (slice(None), slice(0, 960))] = wt[...]
    w[mine + (slice(None), slice(960, 1024))] = jnp.zeros((80, 64), BF)
    block = w[mine + (slice(0, 16), slice(896, 1024))].astype(F32)
    row = jnp.concatenate([jnp.zeros((1, 64), F32), own_gains[...].astype(F32), jnp.zeros((1, 49), F32)], axis=1)
    r = lax.broadcasted_iota(jnp.int32, (16, 128), 0)
    w[mine + (slice(0, 16), slice(896, 1024))] = jnp.where(r == 0, block + row, block).astype(BF)
    pl.semaphore_wait(barrier, 8)

    def begin():
        for copy in loads:
            copy.wait()
        prepare(dqkv, ot, ids, freq, e, x32, cos3, sin3, mask3)

    gather_into(xyz, core, w, send_sem, recv_sem, sib_send, sib_recv, begin)
    collect_gains(w, tails, gains)
    attention(w, gains, x32, n1, r1, qt, kt, vt, p, ot, mid, n2, cos3, sin3, mask3)
    down[...] = jnp.zeros_like(down)
    dn[...] = jnp.zeros_like(dn)

    x, y, z = xyz

    order = [(y + step) % 4 for step in (2, 1, 3, 0)]

    def to_sibling(j):
        if j < 4:
            src, dst = w.at[pl.ds(1, 3), order[j], :, 1 - core], acc.at[pl.ds(1, 3), order[j]]
        else:
            src, dst = w.at[0, :, :, 1 - core], acc.at[0]
        return pltpu.make_async_remote_copy(src_ref=src, dst_ref=dst, send_sem=core_send.at[j], recv_sem=core_recv.at[j],
                                            device_id=device_of(xyz, 1 - core), device_id_type=MESH)

    def merge(j):
        to_sibling(j).wait_recv()

        def step(i, carry):
            at = (1 + i // 4, order[j], i % 4) if j < 4 else (0, i // 4, i % 4)
            acc[at] = (acc[at].astype(F32) + w[at + (core,)].astype(F32)).astype(BF)
            return carry

        lax.fori_loop(0, 12 if j < 4 else 16, step, 0)

    class Ring:
        def __init__(self, number, axis, lane, count, where, ref, bufs, item, half=256):
            self.half = half
            self.number, self.axis, self.lane, self.count = number, axis, lane, count
            self.where, self.ref, self.bufs, self.item = where, ref, bufs, item

        def copy(self, kind):
            h = self.half
            group, step, lo, size = ((2, 1, 0, h), (2, -1, h, h), (1, 1, 0, 2 * h), (-1, -1, 0, 2 * h))[kind]
            at = moved(xyz, self.axis, group)[self.axis]
            return pltpu.make_async_remote_copy(
                src_ref=self.ref(at, pl.ds(self.lane + lo, size)), dst_ref=self.bufs[kind],
                send_sem=ring_send.at[self.number, kind], recv_sem=ring_recv.at[self.number, kind],
                device_id=device_of(moved(xyz, self.axis, step), core), device_id_type=MESH)

        def fold(self, group, lo, size, kinds):
            for kind in kinds:
                self.copy(kind).wait_recv()
            at = moved(xyz, self.axis, group)[self.axis]

            def step(i, carry):
                spot = self.where(at, i) + (slice(None), pl.ds(self.lane + lo, size))
                total = acc[spot].astype(F32)
                for kind in kinds:
                    total = total + self.item(self.bufs[kind], i).astype(F32)
                acc[spot] = total.astype(BF)
                return carry

            if self.count == 1:
                step(0, 0)
            else:
                lax.fori_loop(0, self.count, step, 0)

        def begin(self):
            self.copy(0).start()
            self.copy(1).start()

        def plus(self):
            self.fold(1, 0, self.half, (0,))
            self.copy(2).start()

        def minus(self):
            self.fold(-1, self.half, self.half, (1,))
            self.copy(3).start()

        def middle(self):
            self.plus()
            self.minus()

        def end(self):
            self.fold(0, 0, 2 * self.half, (2, 3))

    mlp = pl.ds(1, 3)
    flat = lambda buf, i: buf[i]
    whole = lambda buf, i: buf[...]
    a1 = Ring(0, 1, 0, 12, lambda at, i: (1 + i // 4, at, i % 4), lambda at, l: acc.at[mlp, at, :, :, l],
              (xp1, xm1, yp1, ym1), lambda buf, i: buf[i // 4, i % 4])
    b1 = []
    for j in range(4):
        b1.append(Ring(1 + j, 2, 512, 3, lambda at, i, yj=order[j]: (1 + i, yj, at), lambda at, l, yj=order[j]: acc.at[mlp, yj, at, :, l],
                       (xpb.at[j], xmb.at[j], ypb.at[j], ymb.at[j]), flat))
    second = lambda n: (xps.at[n], xms.at[n], yps.at[n], yms.at[n])
    a2 = Ring(5, 2, 0, 3, lambda at, i: (1 + i, y, at), lambda at, l: acc.at[mlp, y, at, :, l], second(0), flat)
    b2 = Ring(6, 1, 512, 3, lambda at, i: (1 + i, at, z), lambda at, l: acc.at[mlp, at, z, :, l], second(1), flat)
    third = lambda n: (xpc.at[n], xmc.at[n], ypc.at[n], ymc.at[n])
    c1 = Ring(7, 1, 0, 4, lambda at, i: (0, at, i), lambda at, l: acc.at[0, at, :, :, l], third(0), flat)
    d1 = Ring(8, 2, 512, 4, lambda at, i: (0, i, at), lambda at, l: acc.at[0, :, at, :, l], third(1), flat)
    fourth = lambda n: (xpd.at[n], xmd.at[n], ypd.at[n], ymd.at[n])
    c2 = Ring(9, 2, 0, 1, lambda at, i: (0, y, at), lambda at, l: acc.at[0, y, at, :, l], fourth(0), whole)
    d2 = Ring(10, 1, 512, 1, lambda at, i: (0, at, z), lambda at, l: acc.at[0, at, z, :, l], fourth(1), whole)

    def chunk(j, carry):
        yj = (y + jnp.where(j == 0, 2, jnp.where(j == 1, 1, jnp.where(j == 2, 3, 0)))) % 4

        def store(cls, _, value):
            w[cls, yj] = value.astype(BF).reshape(4, 2, 80, 1024)

        def hook(n):
            @pl.when(j == 1)
            def _():
                merge(0)
                a1.begin()
                b1[0].begin()

            @pl.when(j == 2)
            def _():
                merge(1)
                b1[1].begin()
                b1[0].middle()

            @pl.when(j == 3)
            def _():
                merge(2)
                b1[2].begin()
                b1[1].middle()

        feed(w, yj, n2, e, down, dn, store, hook)
        for k in range(4):
            pl.when(j == k)(to_sibling(k).start)
        return carry

    lax.fori_loop(0, 4, chunk, 0)
    a1.plus()
    a1.minus()

    def after_first():
        merge(3)
        b1[3].begin()
        b1[2].middle()
        b1[0].end()

    def after_groups():
        b1[3].middle()
        b1[1].end()

    def after_rows():
        spread_late()
        to_sibling(4).start()

    dqkv[0:15] = (mid[...] + down[...])[:, 0:960].T.astype(BF).reshape(15, 64, 256)
    away = pltpu.make_async_copy(dqkv.at[pl.ds(0, 15)], yt, load_sem.at[2])
    away.start()

    def store_rows(yy, at, value):
        rows = value.shape[0]
        value = value.astype(BF).reshape(rows // 160, 2, 80, 1024)
        lo = at // 160
        w[0, yy, lo : lo + rows // 160] = value

    def place_tail(i, carry):
        yy, zz = i // 4, i % 4
        r = lax.broadcasted_iota(jnp.int32, (16, 128), 0)
        l = lax.broadcasted_iota(jnp.int32, (16, 128), 1)
        for c in range(2):
            new = w[0, yy, zz, c, 0:16, 896:1024].astype(F32)
            for xx in range(4):
                row = tails[pl.ds(xx * 32 + i * 2 + c, 1), :]
                new = jnp.where((r == xx) & (l >= 64), row, new)
            w[0, yy, zz, c, 0:16, 896:1024] = new.astype(BF)
        return carry

    def spread_late():
        spread_gains(dg, tails)
        lax.fori_loop(0, 16, place_tail, 0)

    attention_back(w, gains, x32, n1, r1, qt, kt, vt, p, ot, mid, e, dn, down, n2, dqkv, dqkv, cos3, sin3, dg, store_rows, dxt,
                   after_first, after_groups, after_rows, away.wait)
    merge(4)
    c1.begin()
    d1.begin()
    b1[2].end()
    b1[3].end()
    b2.begin()
    a1.end()
    a2.begin()
    d1.middle()
    c1.middle()
    b2.middle()
    a2.middle()
    d1.end()
    d2.begin()
    c1.end()
    c2.begin()
    a2.end()
    b2.end()
    d2.middle()
    c2.middle()
    d2.end()
    c2.end()
    e1 = Ring(11, 0, 0, 1, lambda at, i: (at, y, z), lambda at, l: acc.at[at, y, z, :, l],
              (room.at[0, :, pl.ds(0, 512)], room.at[0, :, pl.ds(512, 512)], room.at[1], room.at[2]), whole, 512)

    def tile(k):
        return pltpu.make_async_remote_copy(
            src_ref=acc.at[0, y, z, pl.ds(0, 16), pl.ds(896, 128)], dst_ref=tiles.at[k],
            send_sem=ring_send.at[12, k], recv_sem=ring_recv.at[12, k],
            device_id=device_of(moved(xyz, 0, (1, -1, 2)[k]), core), device_id_type=MESH)

    e1.begin()
    for k in range(3):
        tile(k).start()
    total = acc[0, y, z, 0:16, 896:1024].astype(F32)
    for k in range(3):
        tile(k).wait_recv()
        total = total + tiles[k].astype(F32)
    r = lax.broadcasted_iota(jnp.int32, (16, 128), 0)
    gain_out[...] = jnp.sum(jnp.where(r == x, total, 0.0), axis=0, keepdims=True)[:, 64:79]
    for k in range(3):
        tile(k).wait_send()
    e1.middle()
    e1.copy(2).wait_recv()
    e1.copy(3).wait_recv()
    out[...] = (acc[xyz].astype(F32) + room[1].astype(F32) + room[2].astype(F32))[:, 0:960]
    for j in range(5):
        to_sibling(j).wait_send()
    for ring in [a1, a2, b2, c1, d1, c2, d2, e1] + b1:
        for kind in range(4):
            ring.copy(kind).wait_send()


def mega(shard, own_gains, tokens_t, grad_t, ids, freq):
    vm = pl.BlockSpec(memory_space=pltpu.VMEM)
    far = pl.BlockSpec(memory_space=pl.ANY)
    slot = lambda *lead: pltpu.VMEM(lead + (80, 256), BF)
    slot2 = lambda *lead: pltpu.VMEM(lead + (80, 512), BF)
    return pl.pallas_call(
        mega_kernel,
        out_shape=(
            jax.ShapeDtypeStruct((15, 64, 256), BF),
            jax.ShapeDtypeStruct((960, 256), F32),
            jax.ShapeDtypeStruct((80, 960), F32),
            jax.ShapeDtypeStruct((1, 15), F32),
        ),
        in_specs=[vm, vm, far, far, vm, vm],
        out_specs=(far, vm, vm, vm),
        scratch_shapes=[
            pltpu.VMEM((4, 4, 4, 2, 80, 1024), BF),
            pltpu.VMEM((4, 4, 4, 80, 1024), BF),
            slot(3, 4), slot(3, 4), slot2(3, 4), slot2(3, 4),
            slot(4, 3), slot(4, 3), slot2(4, 3), slot2(4, 3),
            slot(2, 3), slot(2, 3), slot2(2, 3), slot2(2, 3),
            slot(2, 4), slot(2, 4), slot2(2, 4), slot2(2, 4),
            slot(2), slot(2), slot2(2), slot2(2),
            pltpu.VMEM((3, 80, 1024), BF),
            pltpu.VMEM((3, 16, 128), BF),
            pltpu.VMEM((256, 1024), BF),
            pltpu.VMEM((256, 1024), BF),
            pltpu.VMEM((256, 1024), BF),
            pltpu.VMEM((256, 1024), BF),
            pltpu.VMEM((256, 1024), F32),
            pltpu.VMEM((256, 1024), F32),
            pltpu.VMEM((256, 1024), F32),
            pltpu.VMEM((15, 64, 256), BF),
            pltpu.VMEM((5, 64, 256), BF),
            pltpu.VMEM((5, 64, 256), BF),
            pltpu.VMEM((5, 256, 768), BF),
            pltpu.VMEM((15, 64, 256), BF),
            pltpu.VMEM((25, 64, 256), BF),
            pltpu.VMEM((256, 2), F32),
            pltpu.VMEM((32, 256), F32),
            pltpu.VMEM((32, 256), F32),
            pltpu.VMEM((256, 256), BF),
            pltpu.VMEM((2, 1024), F32),
            pltpu.VMEM((128, 128), F32),
            pltpu.VMEM((2, 1024), F32),
            pltpu.SemaphoreType.DMA((4, 23)),
            pltpu.SemaphoreType.DMA((4, 23)),
            pltpu.SemaphoreType.DMA((4, 16)),
            pltpu.SemaphoreType.DMA((4, 16)),
            pltpu.SemaphoreType.DMA((13, 4)),
            pltpu.SemaphoreType.DMA((13, 4)),
            pltpu.SemaphoreType.DMA((5,)),
            pltpu.SemaphoreType.DMA((5,)),
            pltpu.SemaphoreType.DMA((3,)),
        ],
        compiler_params=pltpu.CompilerParams(collective_id=0, has_side_effects=True, vmem_limit_bytes=66900000),
    )(shard, own_gains, tokens_t.reshape(15, 64, 256), grad_t.reshape(15, 64, 256), ids, freq)


def body(tokens, layer_weights, norm_gains, seq_ids, out_grad):
    freq = np.power(rope_base, -np.arange(0, 64, 2) / 64).astype(np.float32)
    out_t, grad_t, weight_grad, last = mega(
        layer_weights[0].T, norm_gains, tokens.T, out_grad.T, seq_ids.reshape(1, 256), jnp.asarray(np.repeat(freq[:, None], 128, 1))
    )
    return (out_t.reshape(960, 256).T, grad_t.T, weight_grad.T[None], last)


def solution(mesh):
    return jax.shard_map(
        body,
        mesh=mesh,
        in_specs=(
            P(("fsdp", "dp"), None),
            P(None, None, ("fsdp", "dp")),
            P(None, ("fsdp", "dp")),
            P(("fsdp", "dp")),
            P(("fsdp", "dp"), None),
        ),
        out_specs=(
            P(("fsdp", "dp"), None),
            P(("fsdp", "dp"), None),
            P(None, None, ("fsdp", "dp")),
            P(None, ("fsdp", "dp")),
        ),
        check_vma=False,
    )
```

```python
import functools
import numpy as np
import jax
import jax.numpy as jnp
from jax import lax
from jax.experimental import pallas as pl
from jax.experimental.pallas import tpu as pltpu
from jax.sharding import PartitionSpec as P

epsilon = 1e-05
rope_base = 100000.0
MESH = pl.DeviceIdType.MESH
BF = jnp.bfloat16
PIECES = ((0, 72, 0, 384), (0, 72, 384, 384), (0, 80, 768, 256), (72, 8, 0, 768))
ORDERS = ((0, 1, 2), (1, 2, 0), (2, 0, 1), (2, 0, 1))


def place():
    f = lax.axis_index("fsdp")
    d = lax.axis_index("dp")
    return (f // 4, f % 4, d // 2), d % 2


def device_of(xyz, core):
    return (xyz[0] * 4 + xyz[1], xyz[2] * 2 + core)


def moved(xyz, axis, step):
    out = list(xyz)
    out[axis] = (out[axis] + step + 4) % 4
    return tuple(out)


def gather_into(xyz, core, out, send_sem, recv_sem, sib_send, sib_recv, between):
    waits = []

    def region(part, index):
        top, rows, start, size = PIECES[part]
        return out.at[index[0], index[1], index[2], core, pl.ds(top, rows), pl.ds(start, size)]

    def remote(part, slot, src, index, to):
        copy = pltpu.make_async_remote_copy(
            src_ref=region(part, index) if src is None else src,
            dst_ref=region(part, index),
            send_sem=send_sem.at[part, slot],
            recv_sem=recv_sem.at[part, slot],
            device_id=to,
            device_id_type=MESH,
        )
        copy.start()
        waits.append(copy)
        return copy

    def sibling(part, slot, index):
        copy = pltpu.make_async_remote_copy(
            src_ref=region(part, index),
            dst_ref=region(part, index),
            send_sem=sib_send.at[part, slot],
            recv_sem=sib_recv.at[part, slot],
            device_id=device_of(xyz, 1 - core),
            device_id_type=MESH,
        )
        copy.start()
        sib.append(copy)

    sib = []
    first = [None] * 4
    for part in range(4):
        a = ORDERS[part][0]
        plus = remote(part, 0, None, xyz, device_of(moved(xyz, a, 1), core))
        minus = remote(part, 1, None, xyz, device_of(moved(xyz, a, -1), core))
        first[part] = (plus, minus)
    second = [None] * 4
    for part in range(4):
        a = ORDERS[part][0]
        first[part][0].wait_recv()
        second[part] = remote(part, 2, None, moved(xyz, a, -1), device_of(moved(xyz, a, 1), core))

    def line(part, b_value, c_value, lo=None):
        a, b, c = ORDERS[part]
        index = [None] * 3
        index[a] = slice(None) if lo is None else pl.ds(lo, 2)
        index[b] = b_value
        index[c] = c_value
        return tuple(index)

    third = [[None] * 4 for _ in range(4)]
    hops = [None] * 4
    for part in range(4):
        a, b, c = ORDERS[part]
        first[part][1].wait_recv()
        second[part].wait_recv()
        mine = line(part, xyz[b], xyz[c])
        bp = remote(part, 3, None, mine, device_of(moved(xyz, b, 1), core))
        bm = remote(part, 4, None, mine, device_of(moved(xyz, b, -1), core))
        hops[part] = (bp, bm)
        cp = remote(part, 7, None, mine, device_of(moved(xyz, c, 1), core))
        cm = remote(part, 8, None, mine, device_of(moved(xyz, c, -1), core))
        third[part][0] = (cp, cm)
        sibling(part, 0, mine)
    halves = [None] * 4
    for part in range(4):
        a, b, c = ORDERS[part]
        hops[part][0].wait_recv()
        bv = moved(xyz, b, -1)[b]
        h0 = remote(part, 5, None, line(part, bv, xyz[c], 0), device_of(moved(xyz, b, 1), core))
        mine = line(part, bv, xyz[c])
        cp = remote(part, 9, None, mine, device_of(moved(xyz, c, 1), core))
        cm = remote(part, 10, None, mine, device_of(moved(xyz, c, -1), core))
        third[part][1] = (cp, cm)
        sibling(part, 1, mine)
        hops[part][1].wait_recv()
        bv = moved(xyz, b, 1)[b]
        h1 = remote(part, 6, None, line(part, bv, xyz[c], 2), device_of(moved(xyz, b, -1), core))
        mine = line(part, bv, xyz[c])
        cp = remote(part, 11, None, mine, device_of(moved(xyz, c, 1), core))
        cm = remote(part, 12, None, mine, device_of(moved(xyz, c, -1), core))
        third[part][2] = (cp, cm)
        sibling(part, 2, mine)
        halves[part] = (h0, h1)
    last = [[None] * 4 for _ in range(4)]

    def relative(part, rel):
        b = ORDERS[part][1]
        return moved(xyz, b, (0, -1, 1, 2)[rel])[b]

    def forward(part, rel):
        a, b, c = ORDERS[part]
        bv = relative(part, rel)
        third[part][rel][0].wait_recv()
        cv = moved(xyz, c, -1)[c]
        h0 = remote(part, 15 + 2 * rel, None, line(part, bv, cv, 0), device_of(moved(xyz, c, 1), core))
        sibling(part, 4 + rel, line(part, bv, cv))
        third[part][rel][1].wait_recv()
        cv = moved(xyz, c, 1)[c]
        h1 = remote(part, 16 + 2 * rel, None, line(part, bv, cv, 2), device_of(moved(xyz, c, -1), core))
        sibling(part, 8 + rel, line(part, bv, cv))
        last[part][rel] = (h0, h1)

    between()
    for part in range(4):
        forward(part, 0)
    for part in range(4):
        a, b, c = ORDERS[part]
        halves[part][0].wait_recv()
        halves[part][1].wait_recv()
        mine = line(part, relative(part, 3), xyz[c])
        cp = remote(part, 13, None, mine, device_of(moved(xyz, c, 1), core))
        cm = remote(part, 14, None, mine, device_of(moved(xyz, c, -1), core))
        third[part][3] = (cp, cm)
        sibling(part, 3, mine)
    for rel in (1, 2, 3):
        for part in range(4):
            forward(part, rel)
    for rel in range(4):
        for part in range(4):
            a, b, c = ORDERS[part]
            last[part][rel][0].wait_recv()
            last[part][rel][1].wait_recv()
            sibling(part, 12 + rel, line(part, relative(part, rel), moved(xyz, c, 2)[c]))
    for copy in sib:
        copy.wait()
    for copy in waits:
        copy.wait_send()


F32 = jnp.float32
SCALE = 64 ** (-0.5)


def nt(left, right):
    return lax.dot_general(left, right, (((1,), (1,)), ((), ())), preferred_element_type=F32)


def tn(left, right):
    return lax.dot_general(left, right, (((0,), (0,)), ((), ())), preferred_element_type=F32)


def nn(left, right):
    return jnp.dot(left, right, preferred_element_type=F32)


def turn(pair, cos, sin, direction):
    a, b = pair[0:32], pair[32:64]
    return jnp.concatenate([a * cos - direction * b * sin, b * cos + direction * a * sin], axis=0)


def real(values):
    lane = lax.broadcasted_iota(jnp.int32, values.shape, 1)
    return jnp.where(lane < 960, values, 0.0)


def prepare(xt, et, ids, freq, e, x32, cos3, sin3, mask3):
    zero = jnp.zeros((256, 64), F32)
    x32[:, 0:960] = xt[0:15].reshape(960, 256).astype(F32).T.astype(BF)
    x32[:, 960:1024] = zero.astype(BF)
    e[:, 0:960] = et[...].reshape(960, 256).astype(F32).T.astype(BF)
    e[:, 960:1024] = zero.astype(BF)
    across = jnp.broadcast_to(ids[...], (256, 256))
    same = across == across.T
    down = lax.broadcasted_iota(jnp.int32, (256, 256), 0)
    along = lax.broadcasted_iota(jnp.int32, (256, 256), 1)
    start = jnp.min(jnp.where(same, down, 256).astype(F32), axis=0, keepdims=True)
    row = lax.broadcasted_iota(jnp.int32, (1, 256), 1).astype(F32)
    angle = freq[...][:, 0:1] * (row - start)
    cos, sin = jnp.cos(angle), jnp.sin(angle)
    mask3[...] = jnp.where(same & (down <= along), 1.0, 0.0).astype(BF)
    cos3[...] = cos
    sin3[...] = sin


def wide(ref):
    return jnp.concatenate([ref[...]] * 3, axis=1)


def three(ref, k):
    return jnp.concatenate([ref[3 * k], ref[3 * k + 1], ref[3 * k + 2]], axis=1)


def attention(w, gains, x32, n1, r1, qt, kt, vt, p, ot, mid, n2, cos3, sin3, mask3):
    x = x32[...].astype(F32)
    inv = lax.rsqrt(jnp.sum(x * x, axis=1, keepdims=True) * (1.0 / 960) + epsilon)
    r1[:, 0:1] = inv
    n1[...] = (x * inv * gains[0:1, :]).astype(BF)

    def project(y, lo, hi):
        rows = w[0, y].reshape(640, 1024)[lo:hi]
        return nt(rows, n1[...])

    cos, sin = cos3[...], sin3[...]
    part = project(0, 0, 640)
    for h in range(10):
        qt[h] = turn(part[64 * h : 64 * h + 64], cos, sin, 1.0).astype(BF)
    part = project(1, 0, 640)
    for h in range(5):
        qt[10 + h] = turn(part[64 * h : 64 * h + 64], cos, sin, 1.0).astype(BF)
        kt[h] = turn(part[320 + 64 * h : 384 + 64 * h], cos, sin, 1.0).astype(BF)
    part = project(2, 0, 320)
    for h in range(5):
        vt[h] = part[64 * h : 64 * h + 64].astype(BF)

    def group(k, carry):
        q3 = three(qt, k)
        s = nn(kt[k].T, q3) * SCALE
        allowed = mask3[...].astype(F32) > 0.0
        s = jnp.concatenate([jnp.where(allowed, s[:, 256 * i : 256 * i + 256], -1e30) for i in range(3)], axis=1)
        s = jnp.exp(s - jnp.max(s, axis=0, keepdims=True))
        s = (s * (1.0 / jnp.sum(s, axis=0, keepdims=True))).astype(BF)
        p[k] = s
        o3 = nn(vt[k], s).astype(BF)
        for i in range(3):
            ot[3 * k + i] = o3[:, 256 * i : 256 * i + 256]
        return carry

    lax.fori_loop(0, 5, group, 0)
    o = ot[...].reshape(960, 256)
    m = x32[...].astype(F32) + tn(o[0:320], w[0, 2].reshape(640, 1024)[320:640])
    m = real(m + tn(o[320:960], w[0, 3].reshape(640, 1024)))
    mid[...] = m
    inv = lax.rsqrt(jnp.sum(m * m, axis=1, keepdims=True) * (1.0 / 960) + epsilon)
    r1[:, 1:2] = inv
    n2[...] = (m * inv * gains[1:2, :]).astype(BF)


def feed(w, y, n2, e, down, dn, store, hook):
    w1, w2, w3 = w[1, y].reshape(640, 1024), w[2, y].reshape(640, 1024), w[3, y].reshape(640, 1024)
    gate = nt(w1, n2[...])
    up = nt(w2, n2[...])
    sig = jax.nn.sigmoid(gate)
    hidden = (gate * sig * up).astype(BF)
    down[...] += tn(hidden, w3)
    dh = nt(w3, e[...])
    d_gate = (dh * up * sig * (1.0 + gate * (1.0 - sig))).astype(BF)
    d_up = (dh * gate * sig).astype(BF)
    dn[...] += tn(d_gate, w1) + tn(d_up, w2)
    hook(2)
    store(3, y, nn(hidden, e[...]))
    store(1, y, nn(d_gate, n2[...]))
    store(2, y, nn(d_up, n2[...]))


def norm_back(d_norm, values, inv, gain):
    d_norm = real(d_norm)
    u = d_norm * gain
    d_gain = jnp.sum(d_norm * values * inv, axis=0, keepdims=True)
    mean = jnp.sum(u * values, axis=1, keepdims=True) * (1.0 / 960)
    return inv * u - values * (inv * inv * inv * mean), d_gain


def attention_back(w, gains, x32, n1, r1, qt, kt, vt, p, ot, mid, e, dn, dm, dmb, dot_, dqkv, cos3, sin3, dg, store_rows, dxt,
                   after_first, after_groups, after_rows, before):
    d, dg2 = norm_back(dn[...], mid[...], r1[:, 1:2], gains[1:2, :])
    d = d + e[...].astype(F32)
    dm[...] = d
    db = d.astype(BF)
    dmb[...] = db
    dg[1:2, :] = dg2
    d_o = nt(w[0, 2].reshape(640, 1024)[320:640], db).astype(BF)
    before()
    for h in range(5):
        dot_[h] = d_o[64 * h : 64 * h + 64]
    d_o = nt(w[0, 3].reshape(640, 1024), db).astype(BF)
    for h in range(10):
        dot_[5 + h] = d_o[64 * h : 64 * h + 64]
    o = ot[...].reshape(960, 256)
    store_rows(3, 0, nn(o[320:960], db))
    after_first()

    def group(k, carry):
        d3 = three(dot_, k)
        q3 = three(qt, k)
        pb = p[k]
        dp = nn(vt[k].T, d3)
        pf = pb.astype(F32)
        ds = pf * (dp - jnp.sum(pf * dp, axis=0, keepdims=True))
        ds = (ds * SCALE).astype(BF)
        dqkv[20 + k] = nt(d3, pb).astype(BF)
        dq = turn(nn(kt[k], ds), wide(cos3), wide(sin3), -1.0).astype(BF)
        for i in range(3):
            dqkv[3 * k + i] = dq[:, 256 * i : 256 * i + 256]
        dqkv[15 + k] = turn(nt(q3, ds), cos3[...], sin3[...], -1.0).astype(BF)
        return carry

    lax.fori_loop(0, 5, group, 0)
    after_groups()
    a = dqkv[0:10].reshape(640, 256)
    total = tn(a, w[0, 0].reshape(640, 1024))
    store_rows(0, 0, nn(a, n1[...]))
    a = dqkv[10:20].reshape(640, 256)
    total = total + tn(a, w[0, 1].reshape(640, 1024))
    store_rows(1, 0, nn(a, n1[...]))
    a = dqkv[20:25].reshape(320, 256)
    total = total + tn(a, w[0, 2].reshape(640, 1024)[0:320])
    store_rows(2, 0, nn(a, n1[...]))
    store_rows(2, 320, nn(o[0:320], dmb[...]))
    d, dg1 = norm_back(total, x32[...].astype(F32), r1[:, 0:1], gains[0:1, :])
    dg[0:1, :] = dg1
    after_rows()
    dxt[...] = (dm[...] + d)[:, 0:960].T


def gain_places():
    p = lax.broadcasted_iota(jnp.int32, (64, 1024), 1)
    owner = lax.broadcasted_iota(jnp.int32, (64, 1024), 0)
    mine = (p >= 15 * owner) & (p < 15 * owner + 15)
    pos = lax.broadcasted_iota(jnp.int32, (128, 1024), 1)
    lane = lax.broadcasted_iota(jnp.int32, (128, 1024), 0)
    base = ((pos.astype(F32) + 0.5) * (1.0 / 15)).astype(jnp.int32) * 15
    pick = jnp.where(pos - base + 64 == lane, 1.0, 0.0).astype(BF)
    return mine, pick


def collect_gains(w, table, gains):
    def step(i, carry):
        x, rest = i // 16, i % 16
        r = lax.broadcasted_iota(jnp.int32, (16, 128), 0)
        for c in range(2):
            block = w[x, rest // 4, rest % 4, c, 0:16, 896:1024].astype(F32)
            table[pl.ds(i * 2 + c, 1), :] = jnp.sum(jnp.where(r == 0, block, 0.0), axis=0, keepdims=True)
        return carry

    lax.fori_loop(0, 64, step, 0)
    mine, pick = gain_places()
    for half in range(2):
        rows = nn(table[64 * half : 64 * half + 64, :].astype(BF), pick)
        gains[half : half + 1, :] = jnp.sum(jnp.where(mine, rows, 0.0), axis=0, keepdims=True)


def spread_gains(dg, tails):
    mine, pick = gain_places()
    for half in range(2):
        rows = jnp.where(mine, dg[half : half + 1, :], 0.0).astype(BF)
        tails[64 * half : 64 * half + 64, :] = nt(rows, pick)


def mega_kernel(wt, own_gains, xt, et, ids, freq, yt, dxt, out, gain_out,
                w, acc, xp1, xm1, yp1, ym1, xpb, xmb, ypb, ymb, xps, xms, yps, yms, xpc, xmc, ypc, ymc, xpd, xmd, ypd, ymd, room, tiles, tails_in, n1, n2, e, x32, mid, down, dn, qt, kt, vt, p, ot, dqkv,
                r1, cos3, sin3, mask3, dg, tails, gains,
                send_sem, recv_sem, sib_send, sib_recv, ring_send, ring_recv, core_send, core_recv, load_sem):
    xyz, core = place()
    barrier = pltpu.get_barrier_semaphore()
    near = [device_of(moved(xyz, axis, step), core) for axis in range(3) for step in (1, -1)]
    near.append(device_of(moved(xyz, 0, 2), core))
    for other in near + [device_of(xyz, 1 - core)]:
        pl.semaphore_signal(barrier, inc=1, device_id=other, device_id_type=MESH)
    loads = [pltpu.make_async_copy(xt, dqkv.at[pl.ds(0, 15)], load_sem.at[0]), pltpu.make_async_copy(et, ot, load_sem.at[1])]
    for copy in loads:
        copy.start()
    mine = xyz + (core,)
    w[mine + (slice(None), slice(0, 960))] = wt[...]
    w[mine + (slice(None), slice(960, 1024))] = jnp.zeros((80, 64), BF)
    block = w[mine + (slice(0, 16), slice(896, 1024))].astype(F32)
    row = jnp.concatenate([jnp.zeros((1, 64), F32), own_gains[...].astype(F32), jnp.zeros((1, 49), F32)], axis=1)
    r = lax.broadcasted_iota(jnp.int32, (16, 128), 0)
    w[mine + (slice(0, 16), slice(896, 1024))] = jnp.where(r == 0, block + row, block).astype(BF)
    pl.semaphore_wait(barrier, 8)

    def begin():
        for copy in loads:
            copy.wait()
        prepare(dqkv, ot, ids, freq, e, x32, cos3, sin3, mask3)

    gather_into(xyz, core, w, send_sem, recv_sem, sib_send, sib_recv, begin)
    collect_gains(w, tails, gains)
    attention(w, gains, x32, n1, r1, qt, kt, vt, p, ot, mid, n2, cos3, sin3, mask3)
    down[...] = jnp.zeros_like(down)
    dn[...] = jnp.zeros_like(dn)

    x, y, z = xyz

    order = [(y + step) % 4 for step in (2, 1, 3, 0)]

    def to_sibling(j):
        if j < 4:
            src, dst = w.at[pl.ds(1, 3), order[j], :, 1 - core], acc.at[pl.ds(1, 3), order[j]]
        else:
            src, dst = w.at[0, (3, 0, 1, 2)[j - 4], :, 1 - core], acc.at[0, (3, 0, 1, 2)[j - 4]]
        return pltpu.make_async_remote_copy(src_ref=src, dst_ref=dst, send_sem=core_send.at[j], recv_sem=core_recv.at[j],
                                            device_id=device_of(xyz, 1 - core), device_id_type=MESH)

    def merge(j):
        to_sibling(j).wait_recv()

        def step(i, carry):
            at = (1 + i // 4, order[j], i % 4) if j < 4 else (0, (3, 0, 1, 2)[j - 4], i)
            acc[at] = (acc[at].astype(F32) + w[at + (core,)].astype(F32)).astype(BF)
            return carry

        lax.fori_loop(0, 12 if j < 4 else 4, step, 0)

    class Ring:
        def __init__(self, number, axis, lane, count, where, ref, bufs, item, half=256):
            self.half = half
            self.number, self.axis, self.lane, self.count = number, axis, lane, count
            self.where, self.ref, self.bufs, self.item = where, ref, bufs, item

        def copy(self, kind):
            h = self.half
            group, step, lo, size = ((2, 1, 0, h), (2, -1, h, h), (1, 1, 0, 2 * h), (-1, -1, 0, 2 * h))[kind]
            at = moved(xyz, self.axis, group)[self.axis]
            return pltpu.make_async_remote_copy(
                src_ref=self.ref(at, pl.ds(self.lane + lo, size)), dst_ref=self.bufs[kind],
                send_sem=ring_send.at[self.number, kind], recv_sem=ring_recv.at[self.number, kind],
                device_id=device_of(moved(xyz, self.axis, step), core), device_id_type=MESH)

        def fold(self, group, lo, size, kinds):
            for kind in kinds:
                self.copy(kind).wait_recv()
            at = moved(xyz, self.axis, group)[self.axis]

            def step(i, carry):
                spot = self.where(at, i) + (slice(None), pl.ds(self.lane + lo, size))
                total = acc[spot].astype(F32)
                for kind in kinds:
                    total = total + self.item(self.bufs[kind], i).astype(F32)
                acc[spot] = total.astype(BF)
                return carry

            if self.count == 1:
                step(0, 0)
            else:
                lax.fori_loop(0, self.count, step, 0)

        def begin(self):
            self.copy(0).start()
            self.copy(1).start()

        def plus(self):
            self.fold(1, 0, self.half, (0,))
            self.copy(2).start()

        def minus(self):
            self.fold(-1, self.half, self.half, (1,))
            self.copy(3).start()

        def middle(self):
            self.plus()
            self.minus()

        def end(self):
            self.fold(0, 0, 2 * self.half, (2, 3))

    mlp = pl.ds(1, 3)
    flat = lambda buf, i: buf[i]
    whole = lambda buf, i: buf[...]
    a1, a2 = [], []
    for part in range(2):
        thin, thick = pl.ds(128 * part, 128), pl.ds(256 * part, 256)
        bufs = (xp1.at[:, :, :, thin], xm1.at[:, :, :, thin], yp1.at[:, :, :, thick], ym1.at[:, :, :, thick])
        a1.append(Ring(12 + part, 1, 256 * part, 12, lambda at, i: (1 + i // 4, at, i % 4), lambda at, l: acc.at[mlp, at, :, :, l], bufs,
                       lambda buf, i: buf[i // 4, i % 4], 128))
        bufs = (xps.at[0, :, :, thin], xms.at[0, :, :, thin], yps.at[0, :, :, thick], yms.at[0, :, :, thick])
        a2.append(Ring(14 + part, 2, 256 * part, 3, lambda at, i: (1 + i, y, at), lambda at, l: acc.at[mlp, y, at, :, l], bufs, flat, 128))
    b1 = []
    for j in range(4):
        b1.append(Ring(1 + j, 2, 512, 3, lambda at, i, yj=order[j]: (1 + i, yj, at), lambda at, l, yj=order[j]: acc.at[mlp, yj, at, :, l],
                       (xpb.at[j], xmb.at[j], ypb.at[j], ymb.at[j]), flat))
    second = lambda n: (xps.at[n], xms.at[n], yps.at[n], yms.at[n])
    b2 = Ring(6, 1, 512, 3, lambda at, i: (1 + i, at, z), lambda at, l: acc.at[mlp, at, z, :, l], second(1), flat)
    third = lambda n: (xpc.at[n], xmc.at[n], ypc.at[n], ymc.at[n])
    c1 = Ring(7, 1, 0, 4, lambda at, i: (0, at, i), lambda at, l: acc.at[0, at, :, :, l], third(0), flat)
    d1 = Ring(8, 2, 512, 4, lambda at, i: (0, i, at), lambda at, l: acc.at[0, :, at, :, l], third(1), flat)
    fourth = lambda n: (xpd.at[n], xmd.at[n], ypd.at[n], ymd.at[n])
    c2 = Ring(9, 2, 0, 1, lambda at, i: (0, y, at), lambda at, l: acc.at[0, y, at, :, l], fourth(0), whole)
    d2 = Ring(10, 1, 512, 1, lambda at, i: (0, at, z), lambda at, l: acc.at[0, at, z, :, l], fourth(1), whole)

    def chunk(j, carry):
        yj = (y + jnp.where(j == 0, 2, jnp.where(j == 1, 1, jnp.where(j == 2, 3, 0)))) % 4

        def store(cls, _, value):
            w[cls, yj] = value.astype(BF).reshape(4, 2, 80, 1024)

        def hook(n):
            @pl.when(j == 1)
            def _():
                merge(0)
                a1[0].begin()
                a1[1].begin()
                b1[0].begin()

            @pl.when(j == 2)
            def _():
                merge(1)
                b1[1].begin()
                b1[0].middle()

            @pl.when(j == 3)
            def _():
                merge(2)
                a1[0].middle()
                b1[2].begin()
                b1[1].middle()

        feed(w, yj, n2, e, down, dn, store, hook)
        for k in range(4):
            pl.when(j == k)(to_sibling(k).start)
        return carry

    lax.fori_loop(0, 4, chunk, 0)
    a1[1].middle()

    def after_first():
        to_sibling(4).start()
        merge(3)
        b1[3].begin()
        b1[2].middle()
        b1[0].end()

    def after_groups():
        b1[3].middle()
        b1[1].end()
        merge(4)

    def swap_tails():
        return pltpu.make_async_remote_copy(src_ref=tails, dst_ref=tails_in, send_sem=core_send.at[8], recv_sem=core_recv.at[8],
                                            device_id=device_of(xyz, 1 - core), device_id_type=MESH)

    def after_rows():
        spread_gains(dg, tails)
        swap_tails().start()
        merge(5)
        merge(6)

    dqkv[0:15] = (mid[...] + down[...])[:, 0:960].T.astype(BF).reshape(15, 64, 256)
    away = pltpu.make_async_copy(dqkv.at[pl.ds(0, 15)], yt, load_sem.at[2])
    away.start()

    def store_rows(yy, at, value):
        rows = value.shape[0]
        value = value.astype(BF).reshape(rows // 160, 2, 80, 1024)
        lo = at // 160
        w[0, yy, lo : lo + rows // 160] = value
        if yy < 2 or at == 320:
            to_sibling(5 + yy).start()

    def place_tail(i, carry):
        at = (0, i // 4, i % 4, slice(0, 16), slice(896, 1024))
        r = lax.broadcasted_iota(jnp.int32, (16, 128), 0)
        l = lax.broadcasted_iota(jnp.int32, (16, 128), 1)
        new = acc[at].astype(F32)
        for xx in range(4):
            spot = pl.ds(xx * 32 + i * 2 + core, 1)
            new = jnp.where((r == xx) & (l >= 64), tails[spot, :] + tails_in[spot, :], new)
        acc[at] = new.astype(BF)
        return carry

    attention_back(w, gains, x32, n1, r1, qt, kt, vt, p, ot, mid, e, dn, down, n2, dqkv, dqkv, cos3, sin3, dg, store_rows, dxt,
                   after_first, after_groups, after_rows, away.wait)
    merge(7)
    swap_tails().wait_recv()
    lax.fori_loop(0, 16, place_tail, 0)
    c1.begin()
    d1.begin()
    b1[2].end()
    b1[3].end()
    b2.begin()
    a1[0].end()
    a2[0].begin()
    d1.middle()
    a1[1].end()
    a2[1].begin()
    c1.middle()
    a2[0].middle()
    b2.middle()
    a2[1].middle()
    d1.end()
    d2.begin()
    c1.end()
    c2.begin()
    a2[0].end()
    d2.middle()
    b2.end()
    c2.middle()
    a2[1].end()
    d2.end()
    c2.end()
    e1 = Ring(11, 0, 0, 1, lambda at, i: (at, y, z), lambda at, l: acc.at[at, y, z, :, l],
              (room.at[0, :, pl.ds(0, 512)], room.at[0, :, pl.ds(512, 512)], room.at[1], room.at[2]), whole, 512)

    def tile(k):
        return pltpu.make_async_remote_copy(
            src_ref=acc.at[0, y, z, pl.ds(0, 16), pl.ds(896, 128)], dst_ref=tiles.at[k],
            send_sem=ring_send.at[0, k], recv_sem=ring_recv.at[0, k],
            device_id=device_of(moved(xyz, 0, (1, -1, 2)[k]), core), device_id_type=MESH)

    e1.begin()
    for k in range(3):
        tile(k).start()
    total = acc[0, y, z, 0:16, 896:1024].astype(F32)
    for k in range(3):
        tile(k).wait_recv()
        total = total + tiles[k].astype(F32)
    r = lax.broadcasted_iota(jnp.int32, (16, 128), 0)
    gain_out[...] = jnp.sum(jnp.where(r == x, total, 0.0), axis=0, keepdims=True)[:, 64:79]
    for k in range(3):
        tile(k).wait_send()
    e1.middle()
    e1.copy(2).wait_recv()
    e1.copy(3).wait_recv()
    out[...] = (acc[xyz].astype(F32) + room[1].astype(F32) + room[2].astype(F32))[:, 0:960]
    for j in range(8):
        to_sibling(j).wait_send()
    swap_tails().wait_send()
    for ring in [b2, c1, d1, c2, d2, e1] + a1 + a2 + b1:
        for kind in range(4):
            ring.copy(kind).wait_send()


def mega(shard, own_gains, tokens_t, grad_t, ids, freq):
    vm = pl.BlockSpec(memory_space=pltpu.VMEM)
    far = pl.BlockSpec(memory_space=pl.ANY)
    slot = lambda *lead: pltpu.VMEM(lead + (80, 256), BF)
    slot2 = lambda *lead: pltpu.VMEM(lead + (80, 512), BF)
    return pl.pallas_call(
        mega_kernel,
        out_shape=(
            jax.ShapeDtypeStruct((15, 64, 256), BF),
            jax.ShapeDtypeStruct((960, 256), F32),
            jax.ShapeDtypeStruct((80, 960), F32),
            jax.ShapeDtypeStruct((1, 15), F32),
        ),
        in_specs=[vm, vm, far, far, vm, vm],
        out_specs=(far, vm, vm, vm),
        scratch_shapes=[
            pltpu.VMEM((4, 4, 4, 2, 80, 1024), BF),
            pltpu.VMEM((4, 4, 4, 80, 1024), BF),
            slot(3, 4), slot(3, 4), slot2(3, 4), slot2(3, 4),
            slot(4, 3), slot(4, 3), slot2(4, 3), slot2(4, 3),
            slot(2, 3), slot(2, 3), slot2(2, 3), slot2(2, 3),
            slot(2, 4), slot(2, 4), slot2(2, 4), slot2(2, 4),
            slot(2), slot(2), slot2(2), slot2(2),
            pltpu.VMEM((3, 80, 1024), BF),
            pltpu.VMEM((3, 16, 128), BF),
            pltpu.VMEM((128, 128), F32),
            pltpu.VMEM((256, 1024), BF),
            pltpu.VMEM((256, 1024), BF),
            pltpu.VMEM((256, 1024), BF),
            pltpu.VMEM((256, 1024), BF),
            pltpu.VMEM((256, 1024), F32),
            pltpu.VMEM((256, 1024), F32),
            pltpu.VMEM((256, 1024), F32),
            pltpu.VMEM((15, 64, 256), BF),
            pltpu.VMEM((5, 64, 256), BF),
            pltpu.VMEM((5, 64, 256), BF),
            pltpu.VMEM((5, 256, 768), BF),
            pltpu.VMEM((15, 64, 256), BF),
            pltpu.VMEM((25, 64, 256), BF),
            pltpu.VMEM((256, 2), F32),
            pltpu.VMEM((32, 256), F32),
            pltpu.VMEM((32, 256), F32),
            pltpu.VMEM((256, 256), BF),
            pltpu.VMEM((2, 1024), F32),
            pltpu.VMEM((128, 128), F32),
            pltpu.VMEM((2, 1024), F32),
            pltpu.SemaphoreType.DMA((4, 23)),
            pltpu.SemaphoreType.DMA((4, 23)),
            pltpu.SemaphoreType.DMA((4, 16)),
            pltpu.SemaphoreType.DMA((4, 16)),
            pltpu.SemaphoreType.DMA((16, 4)),
            pltpu.SemaphoreType.DMA((16, 4)),
            pltpu.SemaphoreType.DMA((9,)),
            pltpu.SemaphoreType.DMA((9,)),
            pltpu.SemaphoreType.DMA((3,)),
        ],
        compiler_params=pltpu.CompilerParams(collective_id=0, has_side_effects=True, vmem_limit_bytes=66900000),
    )(shard, own_gains, tokens_t.reshape(15, 64, 256), grad_t.reshape(15, 64, 256), ids, freq)


def body(tokens, layer_weights, norm_gains, seq_ids, out_grad):
    freq = np.power(rope_base, -np.arange(0, 64, 2) / 64).astype(np.float32)
    out_t, grad_t, weight_grad, last = mega(
        layer_weights[0].T, norm_gains, tokens.T, out_grad.T, seq_ids.reshape(1, 256), jnp.asarray(np.repeat(freq[:, None], 128, 1))
    )
    return (out_t.reshape(960, 256).T, grad_t.T, weight_grad.T[None], last)


def solution(mesh):
    return jax.shard_map(
        body,
        mesh=mesh,
        in_specs=(
            P(("fsdp", "dp"), None),
            P(None, None, ("fsdp", "dp")),
            P(None, ("fsdp", "dp")),
            P(("fsdp", "dp")),
            P(("fsdp", "dp"), None),
        ),
        out_specs=(
            P(("fsdp", "dp"), None),
            P(("fsdp", "dp"), None),
            P(None, None, ("fsdp", "dp")),
            P(None, ("fsdp", "dp")),
        ),
        check_vma=False,
    )
```

```python
import functools
import numpy as np
import jax
import jax.numpy as jnp
from jax import lax
from jax.experimental import pallas as pl
from jax.experimental.pallas import tpu as pltpu
from jax.sharding import PartitionSpec as P

epsilon = 1e-05
rope_base = 100000.0
MESH = pl.DeviceIdType.MESH
BF = jnp.bfloat16
PIECES = ((0, 72, 0, 384), (0, 72, 384, 384), (0, 80, 768, 256), (72, 8, 0, 768))
ORDERS = ((0, 1, 2), (1, 2, 0), (2, 0, 1), (2, 0, 1))


def place():
    f = lax.axis_index("fsdp")
    d = lax.axis_index("dp")
    return (f // 4, f % 4, d // 2), d % 2


def device_of(xyz, core):
    return (xyz[0] * 4 + xyz[1], xyz[2] * 2 + core)


def moved(xyz, axis, step):
    out = list(xyz)
    out[axis] = (out[axis] + step + 4) % 4
    return tuple(out)


def gather_into(xyz, core, out, send_sem, recv_sem, sib_send, sib_recv, between):
    waits = []

    def region(part, index):
        top, rows, start, size = PIECES[part]
        return out.at[index[0], index[1], index[2], core, pl.ds(top, rows), pl.ds(start, size)]

    def remote(part, slot, src, index, to):
        copy = pltpu.make_async_remote_copy(
            src_ref=region(part, index) if src is None else src,
            dst_ref=region(part, index),
            send_sem=send_sem.at[part, slot],
            recv_sem=recv_sem.at[part, slot],
            device_id=to,
            device_id_type=MESH,
        )
        copy.start()
        waits.append(copy)
        return copy

    def sibling(part, slot, index):
        copy = pltpu.make_async_remote_copy(
            src_ref=region(part, index),
            dst_ref=region(part, index),
            send_sem=sib_send.at[part, slot],
            recv_sem=sib_recv.at[part, slot],
            device_id=device_of(xyz, 1 - core),
            device_id_type=MESH,
        )
        copy.start()
        sib.append(copy)

    sib = []
    first = [None] * 4
    for part in range(4):
        a = ORDERS[part][0]
        plus = remote(part, 0, None, xyz, device_of(moved(xyz, a, 1), core))
        minus = remote(part, 1, None, xyz, device_of(moved(xyz, a, -1), core))
        first[part] = (plus, minus)
    second = [None] * 4
    for part in range(4):
        a = ORDERS[part][0]
        first[part][0].wait_recv()
        second[part] = remote(part, 2, None, moved(xyz, a, -1), device_of(moved(xyz, a, 1), core))

    def line(part, b_value, c_value, lo=None):
        a, b, c = ORDERS[part]
        index = [None] * 3
        index[a] = slice(None) if lo is None else pl.ds(lo, 2)
        index[b] = b_value
        index[c] = c_value
        return tuple(index)

    third = [[None] * 4 for _ in range(4)]
    hops = [None] * 4
    for part in range(4):
        a, b, c = ORDERS[part]
        first[part][1].wait_recv()
        second[part].wait_recv()
        mine = line(part, xyz[b], xyz[c])
        bp = remote(part, 3, None, mine, device_of(moved(xyz, b, 1), core))
        bm = remote(part, 4, None, mine, device_of(moved(xyz, b, -1), core))
        hops[part] = (bp, bm)
        cp = remote(part, 7, None, mine, device_of(moved(xyz, c, 1), core))
        cm = remote(part, 8, None, mine, device_of(moved(xyz, c, -1), core))
        third[part][0] = (cp, cm)
        sibling(part, 0, mine)
    halves = [None] * 4
    for part in range(4):
        a, b, c = ORDERS[part]
        hops[part][0].wait_recv()
        bv = moved(xyz, b, -1)[b]
        h0 = remote(part, 5, None, line(part, bv, xyz[c], 0), device_of(moved(xyz, b, 1), core))
        mine = line(part, bv, xyz[c])
        cp = remote(part, 9, None, mine, device_of(moved(xyz, c, 1), core))
        cm = remote(part, 10, None, mine, device_of(moved(xyz, c, -1), core))
        third[part][1] = (cp, cm)
        sibling(part, 1, mine)
        hops[part][1].wait_recv()
        bv = moved(xyz, b, 1)[b]
        h1 = remote(part, 6, None, line(part, bv, xyz[c], 2), device_of(moved(xyz, b, -1), core))
        mine = line(part, bv, xyz[c])
        cp = remote(part, 11, None, mine, device_of(moved(xyz, c, 1), core))
        cm = remote(part, 12, None, mine, device_of(moved(xyz, c, -1), core))
        third[part][2] = (cp, cm)
        sibling(part, 2, mine)
        halves[part] = (h0, h1)
    last = [[None] * 4 for _ in range(4)]

    def relative(part, rel):
        b = ORDERS[part][1]
        return moved(xyz, b, (0, -1, 1, 2)[rel])[b]

    def forward(part, rel):
        a, b, c = ORDERS[part]
        bv = relative(part, rel)
        third[part][rel][0].wait_recv()
        cv = moved(xyz, c, -1)[c]
        h0 = remote(part, 15 + 2 * rel, None, line(part, bv, cv, 0), device_of(moved(xyz, c, 1), core))
        sibling(part, 4 + rel, line(part, bv, cv))
        third[part][rel][1].wait_recv()
        cv = moved(xyz, c, 1)[c]
        h1 = remote(part, 16 + 2 * rel, None, line(part, bv, cv, 2), device_of(moved(xyz, c, -1), core))
        sibling(part, 8 + rel, line(part, bv, cv))
        last[part][rel] = (h0, h1)

    between()
    for part in range(4):
        forward(part, 0)
    for part in range(4):
        a, b, c = ORDERS[part]
        halves[part][0].wait_recv()
        halves[part][1].wait_recv()
        mine = line(part, relative(part, 3), xyz[c])
        cp = remote(part, 13, None, mine, device_of(moved(xyz, c, 1), core))
        cm = remote(part, 14, None, mine, device_of(moved(xyz, c, -1), core))
        third[part][3] = (cp, cm)
        sibling(part, 3, mine)
    for rel in (1, 2, 3):
        for part in range(4):
            forward(part, rel)
    for rel in range(4):
        for part in range(4):
            a, b, c = ORDERS[part]
            last[part][rel][0].wait_recv()
            last[part][rel][1].wait_recv()
            sibling(part, 12 + rel, line(part, relative(part, rel), moved(xyz, c, 2)[c]))
    for copy in sib:
        copy.wait()
    for copy in waits:
        copy.wait_send()


F32 = jnp.float32
SCALE = 64 ** (-0.5)


def nt(left, right):
    return lax.dot_general(left, right, (((1,), (1,)), ((), ())), preferred_element_type=F32)


def tn(left, right):
    return lax.dot_general(left, right, (((0,), (0,)), ((), ())), preferred_element_type=F32)


def nn(left, right):
    return jnp.dot(left, right, preferred_element_type=F32)


def turn(pair, cos, sin, direction):
    a, b = pair[0:32], pair[32:64]
    return jnp.concatenate([a * cos - direction * b * sin, b * cos + direction * a * sin], axis=0)


def real(values):
    lane = lax.broadcasted_iota(jnp.int32, values.shape, 1)
    return jnp.where(lane < 960, values, 0.0)


def prepare(xt, et, ids, freq, e, x32, cos3, sin3, mask3):
    zero = jnp.zeros((256, 64), F32)
    x32[:, 0:960] = xt[0:15].reshape(960, 256).astype(F32).T.astype(BF)
    x32[:, 960:1024] = zero.astype(BF)
    e[:, 0:960] = et[...].reshape(960, 256).astype(F32).T.astype(BF)
    e[:, 960:1024] = zero.astype(BF)
    across = jnp.broadcast_to(ids[...], (256, 256))
    same = across == across.T
    down = lax.broadcasted_iota(jnp.int32, (256, 256), 0)
    along = lax.broadcasted_iota(jnp.int32, (256, 256), 1)
    start = jnp.min(jnp.where(same, down, 256).astype(F32), axis=0, keepdims=True)
    row = lax.broadcasted_iota(jnp.int32, (1, 256), 1).astype(F32)
    angle = freq[...][:, 0:1] * (row - start)
    cos, sin = jnp.cos(angle), jnp.sin(angle)
    mask3[...] = jnp.where(same & (down <= along), 1.0, 0.0).astype(BF)
    cos3[...] = cos
    sin3[...] = sin


def wide(ref):
    return jnp.concatenate([ref[...]] * 3, axis=1)


def three(ref, k):
    return jnp.concatenate([ref[3 * k], ref[3 * k + 1], ref[3 * k + 2]], axis=1)


def attention(w, gains, x32, n1, r1, qt, kt, vt, p, ot, mid, n2, cos3, sin3, mask3):
    x = x32[...].astype(F32)
    inv = lax.rsqrt(jnp.sum(x * x, axis=1, keepdims=True) * (1.0 / 960) + epsilon)
    r1[:, 0:1] = inv
    n1[...] = (x * inv * gains[0:1, :]).astype(BF)

    def project(y, lo, hi):
        rows = w[0, y].reshape(640, 1024)[lo:hi]
        return nt(rows, n1[...])

    cos, sin = cos3[...], sin3[...]
    part = project(0, 0, 640)
    for h in range(10):
        qt[h] = turn(part[64 * h : 64 * h + 64], cos, sin, 1.0).astype(BF)
    part = project(1, 0, 640)
    for h in range(5):
        qt[10 + h] = turn(part[64 * h : 64 * h + 64], cos, sin, 1.0).astype(BF)
        kt[h] = turn(part[320 + 64 * h : 384 + 64 * h], cos, sin, 1.0).astype(BF)
    part = project(2, 0, 320)
    for h in range(5):
        vt[h] = part[64 * h : 64 * h + 64].astype(BF)

    def group(k, carry):
        q3 = three(qt, k)
        s = nn(kt[k].T, q3) * SCALE
        allowed = mask3[...].astype(F32) > 0.0
        s = jnp.concatenate([jnp.where(allowed, s[:, 256 * i : 256 * i + 256], -1e30) for i in range(3)], axis=1)
        s = jnp.exp(s - jnp.max(s, axis=0, keepdims=True))
        s = (s * (1.0 / jnp.sum(s, axis=0, keepdims=True))).astype(BF)
        p[k] = s
        o3 = nn(vt[k], s).astype(BF)
        for i in range(3):
            ot[3 * k + i] = o3[:, 256 * i : 256 * i + 256]
        return carry

    lax.fori_loop(0, 5, group, 0)
    o = ot[...].reshape(960, 256)
    m = x32[...].astype(F32) + tn(o[0:320], w[0, 2].reshape(640, 1024)[320:640])
    m = real(m + tn(o[320:960], w[0, 3].reshape(640, 1024)))
    mid[...] = m
    inv = lax.rsqrt(jnp.sum(m * m, axis=1, keepdims=True) * (1.0 / 960) + epsilon)
    r1[:, 1:2] = inv
    n2[...] = (m * inv * gains[1:2, :]).astype(BF)


def feed(w, y, n2, e, down, dn, store, hook):
    w1, w2, w3 = w[1, y].reshape(640, 1024), w[2, y].reshape(640, 1024), w[3, y].reshape(640, 1024)
    gate = nt(w1, n2[...])
    up = nt(w2, n2[...])
    sig = jax.nn.sigmoid(gate)
    hidden = (gate * sig * up).astype(BF)
    down[...] += tn(hidden, w3)
    dh = nt(w3, e[...])
    d_gate = (dh * up * sig * (1.0 + gate * (1.0 - sig))).astype(BF)
    d_up = (dh * gate * sig).astype(BF)
    dn[...] += tn(d_gate, w1) + tn(d_up, w2)
    hook(2)
    store(3, y, nn(hidden, e[...]))
    store(1, y, nn(d_gate, n2[...]))
    store(2, y, nn(d_up, n2[...]))


def norm_back(d_norm, values, inv, gain):
    d_norm = real(d_norm)
    u = d_norm * gain
    d_gain = jnp.sum(d_norm * values * inv, axis=0, keepdims=True)
    mean = jnp.sum(u * values, axis=1, keepdims=True) * (1.0 / 960)
    return inv * u - values * (inv * inv * inv * mean), d_gain


def attention_back(w, gains, x32, n1, r1, qt, kt, vt, p, ot, mid, e, dn, dm, dmb, dot_, dqkv, cos3, sin3, dg, store_rows, dxt,
                   after_first, after_groups, after_rows, before):
    d, dg2 = norm_back(dn[...], mid[...], r1[:, 1:2], gains[1:2, :])
    d = d + e[...].astype(F32)
    dm[...] = d
    db = d.astype(BF)
    dmb[...] = db
    dg[1:2, :] = dg2
    d_o = nt(w[0, 2].reshape(640, 1024)[320:640], db).astype(BF)
    before()
    for h in range(5):
        dot_[h] = d_o[64 * h : 64 * h + 64]
    d_o = nt(w[0, 3].reshape(640, 1024), db).astype(BF)
    for h in range(10):
        dot_[5 + h] = d_o[64 * h : 64 * h + 64]
    o = ot[...].reshape(960, 256)
    store_rows(3, 0, nn(o[320:960], db))
    after_first()

    def group(k, carry):
        d3 = three(dot_, k)
        q3 = three(qt, k)
        pb = p[k]
        dp = nn(vt[k].T, d3)
        pf = pb.astype(F32)
        ds = pf * (dp - jnp.sum(pf * dp, axis=0, keepdims=True))
        ds = (ds * SCALE).astype(BF)
        dqkv[20 + k] = nt(d3, pb).astype(BF)
        dq = turn(nn(kt[k], ds), wide(cos3), wide(sin3), -1.0).astype(BF)
        for i in range(3):
            dqkv[3 * k + i] = dq[:, 256 * i : 256 * i + 256]
        dqkv[15 + k] = turn(nt(q3, ds), cos3[...], sin3[...], -1.0).astype(BF)
        return carry

    lax.fori_loop(0, 5, group, 0)
    after_groups()
    a = dqkv[0:10].reshape(640, 256)
    total = tn(a, w[0, 0].reshape(640, 1024))
    store_rows(0, 0, nn(a, n1[...]))
    a = dqkv[10:20].reshape(640, 256)
    total = total + tn(a, w[0, 1].reshape(640, 1024))
    store_rows(1, 0, nn(a, n1[...]))
    a = dqkv[20:25].reshape(320, 256)
    total = total + tn(a, w[0, 2].reshape(640, 1024)[0:320])
    store_rows(2, 0, nn(a, n1[...]))
    store_rows(2, 320, nn(o[0:320], dmb[...]))
    d, dg1 = norm_back(total, x32[...].astype(F32), r1[:, 0:1], gains[0:1, :])
    dg[0:1, :] = dg1
    after_rows()
    dxt[...] = (dm[...] + d)[:, 0:960].T


def gain_places():
    p = lax.broadcasted_iota(jnp.int32, (64, 1024), 1)
    owner = lax.broadcasted_iota(jnp.int32, (64, 1024), 0)
    mine = (p >= 15 * owner) & (p < 15 * owner + 15)
    pos = lax.broadcasted_iota(jnp.int32, (128, 1024), 1)
    lane = lax.broadcasted_iota(jnp.int32, (128, 1024), 0)
    base = ((pos.astype(F32) + 0.5) * (1.0 / 15)).astype(jnp.int32) * 15
    pick = jnp.where(pos - base + 64 == lane, 1.0, 0.0).astype(BF)
    return mine, pick


def collect_gains(w, table, gains):
    def step(i, carry):
        x, rest = i // 16, i % 16
        r = lax.broadcasted_iota(jnp.int32, (16, 128), 0)
        for c in range(2):
            block = w[x, rest // 4, rest % 4, c, 0:16, 896:1024].astype(F32)
            table[pl.ds(i * 2 + c, 1), :] = jnp.sum(jnp.where(r == 0, block, 0.0), axis=0, keepdims=True)
        return carry

    lax.fori_loop(0, 64, step, 0)
    mine, pick = gain_places()
    for half in range(2):
        rows = nn(table[64 * half : 64 * half + 64, :].astype(BF), pick)
        gains[half : half + 1, :] = jnp.sum(jnp.where(mine, rows, 0.0), axis=0, keepdims=True)


def spread_gains(dg, tails):
    mine, pick = gain_places()
    for half in range(2):
        rows = jnp.where(mine, dg[half : half + 1, :], 0.0).astype(BF)
        tails[64 * half : 64 * half + 64, :] = nt(rows, pick)


def mega_kernel(wt, own_gains, xt, et, ids, freq, yt, dxt, out, gain_out,
                w, acc, xp1, xm1, yp1, ym1, xpb, xmb, ypb, ymb, xps, xms, yps, yms, xpc, xmc, ypc, ymc, xpd, xmd, ypd, ymd, room, tiles, n1, n2, e, x32, mid, down, dn, qt, kt, vt, p, ot, dqkv,
                r1, cos3, sin3, mask3, dg, tails, gains,
                send_sem, recv_sem, sib_send, sib_recv, ring_send, ring_recv, core_send, core_recv, load_sem):
    xyz, core = place()
    barrier = pltpu.get_barrier_semaphore()
    near = [device_of(moved(xyz, axis, step), core) for axis in range(3) for step in (1, -1)]
    near.append(device_of(moved(xyz, 0, 2), core))
    for other in near + [device_of(xyz, 1 - core)]:
        pl.semaphore_signal(barrier, inc=1, device_id=other, device_id_type=MESH)
    loads = [pltpu.make_async_copy(xt, dqkv.at[pl.ds(0, 15)], load_sem.at[0]), pltpu.make_async_copy(et, ot, load_sem.at[1])]
    for copy in loads:
        copy.start()
    mine = xyz + (core,)
    w[mine + (slice(None), slice(0, 960))] = wt[...]
    w[mine + (slice(None), slice(960, 1024))] = jnp.zeros((80, 64), BF)
    block = w[mine + (slice(0, 16), slice(896, 1024))].astype(F32)
    row = jnp.concatenate([jnp.zeros((1, 64), F32), own_gains[...].astype(F32), jnp.zeros((1, 49), F32)], axis=1)
    r = lax.broadcasted_iota(jnp.int32, (16, 128), 0)
    w[mine + (slice(0, 16), slice(896, 1024))] = jnp.where(r == 0, block + row, block).astype(BF)
    pl.semaphore_wait(barrier, 8)

    def begin():
        for copy in loads:
            copy.wait()
        prepare(dqkv, ot, ids, freq, e, x32, cos3, sin3, mask3)

    gather_into(xyz, core, w, send_sem, recv_sem, sib_send, sib_recv, begin)
    collect_gains(w, tails, gains)
    attention(w, gains, x32, n1, r1, qt, kt, vt, p, ot, mid, n2, cos3, sin3, mask3)
    down[...] = jnp.zeros_like(down)
    dn[...] = jnp.zeros_like(dn)

    x, y, z = xyz

    order = [(y + step) % 4 for step in (2, 1, 3, 0)]

    def to_sibling(j):
        if j < 4:
            src, dst = w.at[pl.ds(1, 3), order[j], :, 1 - core], acc.at[pl.ds(1, 3), order[j]]
        else:
            src, dst = w.at[0, :, :, 1 - core], acc.at[0]
        return pltpu.make_async_remote_copy(src_ref=src, dst_ref=dst, send_sem=core_send.at[j], recv_sem=core_recv.at[j],
                                            device_id=device_of(xyz, 1 - core), device_id_type=MESH)

    def merge(j):
        to_sibling(j).wait_recv()

        def step(i, carry):
            at = (1 + i // 4, order[j], i % 4) if j < 4 else (0, i // 4, i % 4)
            acc[at] = (acc[at].astype(F32) + w[at + (core,)].astype(F32)).astype(BF)
            return carry

        lax.fori_loop(0, 12 if j < 4 else 16, step, 0)

    class Ring:
        def __init__(self, number, axis, lane, count, where, ref, bufs, item, half=256):
            self.half = half
            self.number, self.axis, self.lane, self.count = number, axis, lane, count
            self.where, self.ref, self.bufs, self.item = where, ref, bufs, item

        def copy(self, kind):
            h = self.half
            group, step, lo, size = ((2, 1, 0, h), (2, -1, h, h), (1, 1, 0, 2 * h), (-1, -1, 0, 2 * h))[kind]
            at = moved(xyz, self.axis, group)[self.axis]
            return pltpu.make_async_remote_copy(
                src_ref=self.ref(at, pl.ds(self.lane + lo, size)), dst_ref=self.bufs[kind],
                send_sem=ring_send.at[self.number, kind], recv_sem=ring_recv.at[self.number, kind],
                device_id=device_of(moved(xyz, self.axis, step), core), device_id_type=MESH)

        def fold(self, group, lo, size, kinds):
            for kind in kinds:
                self.copy(kind).wait_recv()
            at = moved(xyz, self.axis, group)[self.axis]

            def step(i, carry):
                spot = self.where(at, i) + (slice(None), pl.ds(self.lane + lo, size))
                total = acc[spot].astype(F32)
                for kind in kinds:
                    total = total + self.item(self.bufs[kind], i).astype(F32)
                acc[spot] = total.astype(BF)
                return carry

            if self.count == 1:
                step(0, 0)
            else:
                lax.fori_loop(0, self.count, step, 0)

        def begin(self):
            self.copy(0).start()
            self.copy(1).start()

        def plus(self):
            self.fold(1, 0, self.half, (0,))
            self.copy(2).start()

        def minus(self):
            self.fold(-1, self.half, self.half, (1,))
            self.copy(3).start()

        def middle(self):
            self.plus()
            self.minus()

        def end(self):
            self.fold(0, 0, 2 * self.half, (2, 3))

    mlp = pl.ds(1, 3)
    flat = lambda buf, i: buf[i]
    whole = lambda buf, i: buf[...]
    a1 = Ring(0, 1, 0, 12, lambda at, i: (1 + i // 4, at, i % 4), lambda at, l: acc.at[mlp, at, :, :, l],
              (xp1, xm1, yp1, ym1), lambda buf, i: buf[i // 4, i % 4])
    b1 = []
    for j in range(4):
        b1.append(Ring(1 + j, 2, 512, 3, lambda at, i, yj=order[j]: (1 + i, yj, at), lambda at, l, yj=order[j]: acc.at[mlp, yj, at, :, l],
                       (xpb.at[j], xmb.at[j], ypb.at[j], ymb.at[j]), flat))
    second = lambda n: (xps.at[n], xms.at[n], yps.at[n], yms.at[n])
    a2 = Ring(5, 2, 0, 3, lambda at, i: (1 + i, y, at), lambda at, l: acc.at[mlp, y, at, :, l], second(0), flat)
    b2 = Ring(6, 1, 512, 3, lambda at, i: (1 + i, at, z), lambda at, l: acc.at[mlp, at, z, :, l], second(1), flat)
    third = lambda n: (xpc.at[n], xmc.at[n], ypc.at[n], ymc.at[n])
    c1 = Ring(7, 1, 0, 4, lambda at, i: (0, at, i), lambda at, l: acc.at[0, at, :, :, l], third(0), flat)
    d1 = Ring(8, 2, 512, 4, lambda at, i: (0, i, at), lambda at, l: acc.at[0, :, at, :, l], third(1), flat)
    fourth = lambda n: (xpd.at[n], xmd.at[n], ypd.at[n], ymd.at[n])
    c2 = Ring(9, 2, 0, 1, lambda at, i: (0, y, at), lambda at, l: acc.at[0, y, at, :, l], fourth(0), whole)
    d2 = Ring(10, 1, 512, 1, lambda at, i: (0, at, z), lambda at, l: acc.at[0, at, z, :, l], fourth(1), whole)

    def chunk(j, carry):
        yj = (y + jnp.where(j == 0, 2, jnp.where(j == 1, 1, jnp.where(j == 2, 3, 0)))) % 4

        def store(cls, _, value):
            w[cls, yj] = value.astype(BF).reshape(4, 2, 80, 1024)

        def hook(n):
            @pl.when(j == 1)
            def _():
                merge(0)
                a1.begin()
                b1[0].begin()

            @pl.when(j == 2)
            def _():
                merge(1)
                b1[1].begin()
                b1[0].middle()

            @pl.when(j == 3)
            def _():
                merge(2)
                a1.plus()
                a1.minus()
                b1[2].begin()
                b1[1].middle()

        feed(w, yj, n2, e, down, dn, store, hook)
        for k in range(4):
            pl.when(j == k)(to_sibling(k).start)
        return carry

    lax.fori_loop(0, 4, chunk, 0)

    def after_first():
        merge(3)
        b1[3].begin()
        b1[2].middle()
        b1[0].end()

    def after_groups():
        b1[3].middle()
        b1[1].end()

    def after_rows():
        spread_late()
        to_sibling(4).start()

    dqkv[0:15] = (mid[...] + down[...])[:, 0:960].T.astype(BF).reshape(15, 64, 256)
    away = pltpu.make_async_copy(dqkv.at[pl.ds(0, 15)], yt, load_sem.at[2])
    away.start()

    def store_rows(yy, at, value):
        rows = value.shape[0]
        value = value.astype(BF).reshape(rows // 160, 2, 80, 1024)
        lo = at // 160
        w[0, yy, lo : lo + rows // 160] = value

    def place_tail(i, carry):
        yy, zz = i // 4, i % 4
        r = lax.broadcasted_iota(jnp.int32, (16, 128), 0)
        l = lax.broadcasted_iota(jnp.int32, (16, 128), 1)
        for c in range(2):
            new = w[0, yy, zz, c, 0:16, 896:1024].astype(F32)
            for xx in range(4):
                row = tails[pl.ds(xx * 32 + i * 2 + c, 1), :]
                new = jnp.where((r == xx) & (l >= 64), row, new)
            w[0, yy, zz, c, 0:16, 896:1024] = new.astype(BF)
        return carry

    def spread_late():
        spread_gains(dg, tails)
        lax.fori_loop(0, 16, place_tail, 0)

    attention_back(w, gains, x32, n1, r1, qt, kt, vt, p, ot, mid, e, dn, down, n2, dqkv, dqkv, cos3, sin3, dg, store_rows, dxt,
                   after_first, after_groups, after_rows, away.wait)
    merge(4)
    c1.begin()
    d1.begin()
    b1[2].end()
    b1[3].end()
    b2.begin()
    a1.end()
    a2.begin()
    d1.middle()
    c1.middle()
    b2.middle()
    a2.middle()
    d1.end()
    d2.begin()
    c1.end()
    c2.begin()
    a2.end()
    b2.end()
    d2.middle()
    c2.middle()
    d2.end()
    c2.end()
    e1 = Ring(11, 0, 0, 1, lambda at, i: (at, y, z), lambda at, l: acc.at[at, y, z, :, l],
              (room.at[0, :, pl.ds(0, 512)], room.at[0, :, pl.ds(512, 512)], room.at[1], room.at[2]), whole, 512)

    def tile(k):
        return pltpu.make_async_remote_copy(
            src_ref=acc.at[0, y, z, pl.ds(0, 16), pl.ds(896, 128)], dst_ref=tiles.at[k],
            send_sem=ring_send.at[12, k], recv_sem=ring_recv.at[12, k],
            device_id=device_of(moved(xyz, 0, (1, -1, 2)[k]), core), device_id_type=MESH)

    e1.begin()
    for k in range(3):
        tile(k).start()
    total = acc[0, y, z, 0:16, 896:1024].astype(F32)
    for k in range(3):
        tile(k).wait_recv()
        total = total + tiles[k].astype(F32)
    r = lax.broadcasted_iota(jnp.int32, (16, 128), 0)
    gain_out[...] = jnp.sum(jnp.where(r == x, total, 0.0), axis=0, keepdims=True)[:, 64:79]
    for k in range(3):
        tile(k).wait_send()
    e1.middle()
    e1.copy(2).wait_recv()
    e1.copy(3).wait_recv()
    out[...] = (acc[xyz].astype(F32) + room[1].astype(F32) + room[2].astype(F32))[:, 0:960]
    for j in range(5):
        to_sibling(j).wait_send()
    for ring in [a1, a2, b2, c1, d1, c2, d2, e1] + b1:
        for kind in range(4):
            ring.copy(kind).wait_send()


def mega(shard, own_gains, tokens_t, grad_t, ids, freq):
    vm = pl.BlockSpec(memory_space=pltpu.VMEM)
    far = pl.BlockSpec(memory_space=pl.ANY)
    slot = lambda *lead: pltpu.VMEM(lead + (80, 256), BF)
    slot2 = lambda *lead: pltpu.VMEM(lead + (80, 512), BF)
    return pl.pallas_call(
        mega_kernel,
        out_shape=(
            jax.ShapeDtypeStruct((15, 64, 256), BF),
            jax.ShapeDtypeStruct((960, 256), F32),
            jax.ShapeDtypeStruct((80, 960), F32),
            jax.ShapeDtypeStruct((1, 15), F32),
        ),
        in_specs=[vm, vm, far, far, vm, vm],
        out_specs=(far, vm, vm, vm),
        scratch_shapes=[
            pltpu.VMEM((4, 4, 4, 2, 80, 1024), BF),
            pltpu.VMEM((4, 4, 4, 80, 1024), BF),
            slot(3, 4), slot(3, 4), slot2(3, 4), slot2(3, 4),
            slot(4, 3), slot(4, 3), slot2(4, 3), slot2(4, 3),
            slot(2, 3), slot(2, 3), slot2(2, 3), slot2(2, 3),
            slot(2, 4), slot(2, 4), slot2(2, 4), slot2(2, 4),
            slot(2), slot(2), slot2(2), slot2(2),
            pltpu.VMEM((3, 80, 1024), BF),
            pltpu.VMEM((3, 16, 128), BF),
            pltpu.VMEM((256, 1024), BF),
            pltpu.VMEM((256, 1024), BF),
            pltpu.VMEM((256, 1024), BF),
            pltpu.VMEM((256, 1024), BF),
            pltpu.VMEM((256, 1024), F32),
            pltpu.VMEM((256, 1024), F32),
            pltpu.VMEM((256, 1024), F32),
            pltpu.VMEM((15, 64, 256), BF),
            pltpu.VMEM((5, 64, 256), BF),
            pltpu.VMEM((5, 64, 256), BF),
            pltpu.VMEM((5, 256, 768), BF),
            pltpu.VMEM((15, 64, 256), BF),
            pltpu.VMEM((25, 64, 256), BF),
            pltpu.VMEM((256, 2), F32),
            pltpu.VMEM((32, 256), F32),
            pltpu.VMEM((32, 256), F32),
            pltpu.VMEM((256, 256), BF),
            pltpu.VMEM((2, 1024), F32),
            pltpu.VMEM((128, 128), F32),
            pltpu.VMEM((2, 1024), F32),
            pltpu.SemaphoreType.DMA((4, 23)),
            pltpu.SemaphoreType.DMA((4, 23)),
            pltpu.SemaphoreType.DMA((4, 16)),
            pltpu.SemaphoreType.DMA((4, 16)),
            pltpu.SemaphoreType.DMA((13, 4)),
            pltpu.SemaphoreType.DMA((13, 4)),
            pltpu.SemaphoreType.DMA((5,)),
            pltpu.SemaphoreType.DMA((5,)),
            pltpu.SemaphoreType.DMA((3,)),
        ],
        compiler_params=pltpu.CompilerParams(collective_id=0, has_side_effects=True, vmem_limit_bytes=66900000),
    )(shard, own_gains, tokens_t.reshape(15, 64, 256), grad_t.reshape(15, 64, 256), ids, freq)


def body(tokens, layer_weights, norm_gains, seq_ids, out_grad):
    freq = np.power(rope_base, -np.arange(0, 64, 2) / 64).astype(np.float32)
    out_t, grad_t, weight_grad, last = mega(
        layer_weights[0].T, norm_gains, tokens.T, out_grad.T, seq_ids.reshape(1, 256), jnp.asarray(np.repeat(freq[:, None], 128, 1))
    )
    return (out_t.reshape(960, 256).T, grad_t.T, weight_grad.T[None], last)


def solution(mesh):
    return jax.shard_map(
        body,
        mesh=mesh,
        in_specs=(
            P(("fsdp", "dp"), None),
            P(None, None, ("fsdp", "dp")),
            P(None, ("fsdp", "dp")),
            P(("fsdp", "dp")),
            P(("fsdp", "dp"), None),
        ),
        out_specs=(
            P(("fsdp", "dp"), None),
            P(("fsdp", "dp"), None),
            P(None, None, ("fsdp", "dp")),
            P(None, ("fsdp", "dp")),
        ),
        check_vma=False,
    )
```
